32 devices in a mesh: sample: 2 (over x), space: 16 (over z, y, core).
Axes of the slice: x: 2, y: 2, z: 4, core: 2. Of those that a mesh axis runs over, the one named last changes fastest.
Arguments:
- features: bfloat16 [2, 4, 128, 128, 128], P('sample', None, 'space'), parts along dimension 0, may hold values from -6 to 6
- log_perm: float32 [2, 128, 128, 128], P('sample', 'space'), parts along dimension 0, may hold values from -1.5 to 1.5
- well_cells: int32 [2, 32], P('sample'), parts along dimension 0, may hold values from 0 to 2097151
- well_rates: float32 [2, 32], P('sample'), parts along dimension 0, may hold values from 10 to 70
- lift_in: bfloat16 [5, 128], replicated, may hold values from -2.5 to 2.5
- lift_out: bfloat16 [128, 32], replicated, may hold values from -0.5 to 0.5
- spec_weight: bfloat16 [2, 1024, 32, 2048], P(None, 'space'), may hold values from -2 to 2
- point_weight: bfloat16 [2, 32, 32], replicated, may hold values from -1 to 1
- dec_in: bfloat16 [32, 64], replicated, may hold values from -1 to 1
- dec_out: bfloat16 [64, 2], replicated, may hold values from -0.75 to 0.75
Outputs:
- states: float32 [2, 2, 128, 128, 128], P('sample', None, 'space'), parts along dimension 0
- residual: float32 [2, 128, 128, 128], P('sample', 'space'), parts along dimension 0
The draws below stay inside these ranges and needn't reach their ends.
There are 2 independent parts, one for each index of `sample`. The reference program is written for one: setup_inputs(seed, part) draws one part's arguments, and reference() takes and returns one part's arrays. A program takes and returns all parts, laid end to end along the dimension named above; an argument that names none is the same for every part. Nothing has to cross between parts.
Inputs may be any that keep to these rules, and one draw needn't show every extreme that they name: `well_cells`: cells of the sample's grid; several wells may share a cell.
All inputs are finite; a program needn't handle non-finite values.
Results may differ from the reference program's by a relative error of at most 0.03.
Values may be sent and summed in bfloat16 or wider, within the bound.
A program may use at most 192 MiB of HBM per device.

```python
import math
import jax
import jax.numpy as jnp
from jax import lax

BATCH = 1
NX = 128
NY = 128
NZ = 128
MX = 32
MY = 32
MZ = 32
C = 32
FIN = 4
LIFT = 128
DEC = 64
LAYERS = 2
WELLS = 32


def touch_ends(drawn, key, least, top_value):
    longest = drawn.shape.index(max(drawn.shape))
    spots = []
    for shift in (0, 1):
        where = [jax.random.randint(jax.random.fold_in(key, axis), (), 0, length) for axis, length in enumerate(drawn.shape)]
        where[longest] = (where[longest] + shift) % drawn.shape[longest]
        spots.append(tuple(where))
    return drawn.at[spots[0]].set(least).at[spots[1]].set(top_value)


def level_of(stream_key, extent, split, least, largest):
    def one(dim, parts):
        draws = jax.random.uniform(jax.random.fold_in(jax.random.fold_in(stream_key, 6), dim), (parts,), jnp.float32, least / len(split), largest / len(split))
        return jnp.repeat(jnp.exp(draws), extent[dim] // parts).reshape((-1,) + (1,) * (len(extent) - dim - 1))

    gain = one(*split[0])
    for cut in split[1:]:
        gain = gain * one(*cut)
    return gain


def bell_draw(rng, dims, scale, bound, pieces=(), held_as=jnp.bfloat16):
    level = level_of(rng, dims, pieces, -0.22, 0.18) if pieces else 1.0
    result = jax.random.normal(rng, dims, jnp.float32) * scale * level
    return jnp.minimum(jnp.maximum(result, -bound), bound).astype(held_as)


def setup_inputs(seed: int = 0, part: int = 0) -> dict:
    splits = jax.random.split(jax.random.key(seed), 11)
    own_keys = jax.random.split(jax.random.fold_in(splits[10], part), 11)
    return {
        "features": bell_draw(own_keys[0], (BATCH, FIN, NX, NY, NZ), 1.0, 6.0, ((2, 16),)),
        "log_perm": jnp.clip(jax.random.uniform(own_keys[1], (BATCH, NX, NY, NZ), jnp.float32, -1.5, 1.5) * level_of(own_keys[1], (BATCH, NX, NY, NZ), ((1, 16),), -0.4, 0.0), -1.5, 1.5),
        "well_cells": touch_ends(jax.random.randint(own_keys[2], (BATCH, WELLS), 0, NX * NY * NZ), jax.random.fold_in(own_keys[2], 1), 0, (NX * NY * NZ) - 1).astype(jnp.int32),
        "well_rates": jnp.clip(jax.random.uniform(own_keys[3], (BATCH, WELLS), jnp.float32, 10.0, 70.0), 10.0, 70.0),
        "lift_in": bell_draw(splits[4], (FIN + 1, LIFT), (FIN + 1) ** -0.5, 2.5),
        "lift_out": bell_draw(splits[5], (LIFT, C), LIFT ** -0.5, 0.5),
        "spec_weight": bell_draw(splits[6], (LAYERS, MY * MZ, C, MX * 2 * C), (C // 4) ** -0.5, 2.0, ((1, 16),)),
        "point_weight": bell_draw(splits[7], (LAYERS, C, C), C ** -0.5, 1.0),
        "dec_in": bell_draw(splits[8], (C, DEC), C ** -0.5, 1.0),
        "dec_out": bell_draw(splits[9], (DEC, 2), DEC ** -0.5, 0.75),
    }


def freq_table(length, kept, one_sided):
    indices = jnp.arange(kept, dtype=jnp.int32)
    if one_sided:
        return indices
    return jnp.where(indices < kept // 2, indices, length - kept + indices).astype(jnp.int32)

def wave_parts(length, kept, one_sided):
    freqs = freq_table(length, kept, one_sided)
    places = jnp.arange(length, dtype=jnp.int32)
    phase_turns = freqs[:, None] * places[None, :] % length
    angles = phase_turns.astype(jnp.float32) * (2.0 * math.pi / length)
    norm_scale = 1.0 / math.sqrt(length)
    return (jnp.cos(angles) * norm_scale, jnp.sin(angles) * norm_scale)

def forward_table(length, kept):
    cosine_vals, sine_vals = wave_parts(length, kept, False)
    return jnp.stack([jnp.stack([cosine_vals.T, -sine_vals.T], 1), jnp.stack([sine_vals.T, cosine_vals.T], 1)], 1).astype(jnp.bfloat16)

def inverse_table(length, kept):
    cosine_vals, sine_vals = wave_parts(length, kept, False)
    return jnp.stack([jnp.stack([cosine_vals, sine_vals], 1), jnp.stack([-sine_vals, cosine_vals], 1)], 1).astype(jnp.bfloat16)

def z_tables():
    cosine_vals, sine_vals = wave_parts(NZ, MZ, True)
    weights_k = jnp.where(jnp.arange(MZ) == 0, 1.0, 2.0).astype(jnp.float32)[:, None]
    z_forward = jnp.concatenate([cosine_vals.T, -sine_vals.T], 1).astype(jnp.bfloat16)
    z_inverse = jnp.concatenate([weights_k * cosine_vals, -weights_k * sine_vals], 0).astype(jnp.bfloat16)
    return (z_forward, z_inverse)

def gelu_tanh(values):
    return jax.nn.gelu(values, approximate=True)

def face_term(cond_a, cond_b, press_a, press_b):
    return 2.0 * cond_a * cond_b / (cond_a + cond_b) * (press_a - press_b)

def fourier_layer(hidden_state, weight_slice, point_slice, tables):
    z_forward, z_inverse, y_forward, y_inverse, x_forward, x_inverse = tables
    zspec = jnp.dot(hidden_state.reshape(-1, NZ), z_forward, preferred_element_type=jnp.float32)
    zspec = zspec.astype(jnp.bfloat16).reshape(NX, C, NY, 2, MZ)
    yz_spec = jnp.einsum('xcypk,ypqj->xcqjk', zspec.astype(jnp.float32), y_forward.astype(jnp.float32))
    yz_spec = yz_spec.astype(jnp.bfloat16).reshape(NX, C, 2, MY * MZ)
    spectrum = jnp.einsum('xcpm,xpqi->cqim', yz_spec.astype(jnp.float32), x_forward.astype(jnp.float32)).astype(jnp.bfloat16)
    mode_weights = weight_slice.reshape(MY * MZ, C, MX, 2, C).astype(jnp.float32)
    products = jnp.einsum('cqim,mcipo->imqpo', spectrum.astype(jnp.float32), mode_weights)
    real_part = products[:, :, 0, 0] - products[:, :, 1, 1]
    imag_part = products[:, :, 0, 1] + products[:, :, 1, 0]
    mixed_modes = jnp.stack([real_part, imag_part], 2).astype(jnp.bfloat16)
    back_field = jnp.einsum('imqo,iqpx->xopm', mixed_modes.astype(jnp.float32), x_inverse.astype(jnp.float32))
    back_field = back_field.astype(jnp.bfloat16).reshape(NX, C, 2, MY, MZ)
    y_back = jnp.einsum('xcqjk,jqpy->xcypk', back_field.astype(jnp.float32), y_inverse.astype(jnp.float32)).astype(jnp.bfloat16)
    spectral = jnp.dot(y_back.reshape(-1, 2 * MZ), z_inverse, preferred_element_type=jnp.float32).reshape(NX, C, NY * NZ)
    local_term = jnp.einsum('xcn,co->xon', hidden_state.astype(jnp.float32), point_slice.astype(jnp.float32))
    return gelu_tanh(spectral + local_term).astype(jnp.bfloat16)

def reference(features, log_perm, well_cells, well_rates, lift_in, lift_out, spec_weight, point_weight, dec_in, dec_out):
    z_forward, z_inverse = z_tables()
    tables = (z_forward, z_inverse, forward_table(NY, MY), inverse_table(NY, MY), forward_table(NX, MX), inverse_table(NX, MX))
    plane_size = NY * NZ
    all_states = []
    all_resid = []

    def lift_plane(plane_in):
        lift_hidden = jnp.dot(lift_in.T, plane_in, preferred_element_type=jnp.float32)
        lifted = gelu_tanh(lift_hidden).astype(jnp.bfloat16)
        return jnp.dot(lift_out.T, lifted, preferred_element_type=jnp.float32).astype(jnp.bfloat16)

    def decode_plane(plane_state):
        decoded = gelu_tanh(jnp.dot(dec_in.T, plane_state, preferred_element_type=jnp.float32)).astype(jnp.bfloat16)
        decoded_out = jnp.dot(dec_out.T, decoded, preferred_element_type=jnp.float32)
        return jnp.stack([decoded_out[0], jax.nn.sigmoid(decoded_out[1])], 0)
    for sample_idx in range(BATCH):
        perm_b = log_perm[sample_idx].astype(jnp.bfloat16)
        feature_planes = features[sample_idx].transpose(1, 0, 2, 3).reshape(NX, FIN, plane_size)
        lift_input = jnp.concatenate([feature_planes, perm_b.reshape(NX, 1, plane_size)], 1)
        hidden_state = lax.map(lift_plane, lift_input)
        for layer_idx in range(LAYERS):
            hidden_state = fourier_layer(hidden_state, spec_weight[layer_idx], point_weight[layer_idx], tables)
        plane_states = lax.map(decode_plane, hidden_state)
        states = plane_states.transpose(1, 0, 2).reshape(2, NX, NY, NZ)
        pressure = states[0]
        saturation = states[1]
        conduct = jnp.exp(log_perm[sample_idx]) * (saturation * saturation + 0.5 * (1.0 - saturation) * (1.0 - saturation))
        pad_cond = jnp.pad(conduct, 1)
        pad_press = jnp.pad(pressure, 1)
        flux_sum = face_term(conduct, pad_cond[2:, 1:-1, 1:-1], pressure, pad_press[2:, 1:-1, 1:-1])
        flux_sum = flux_sum + face_term(conduct, pad_cond[:-2, 1:-1, 1:-1], pressure, pad_press[:-2, 1:-1, 1:-1])
        flux_sum = flux_sum + face_term(conduct, pad_cond[1:-1, 2:, 1:-1], pressure, pad_press[1:-1, 2:, 1:-1])
        flux_sum = flux_sum + face_term(conduct, pad_cond[1:-1, :-2, 1:-1], pressure, pad_press[1:-1, :-2, 1:-1])
        flux_sum = flux_sum + face_term(conduct, pad_cond[1:-1, 1:-1, 2:], pressure, pad_press[1:-1, 1:-1, 2:])
        flux_sum = flux_sum + face_term(conduct, pad_cond[1:-1, 1:-1, :-2], pressure, pad_press[1:-1, 1:-1, :-2])
        source = jnp.zeros((NX * NY * NZ,), jnp.float32).at[well_cells[sample_idx]].add(well_rates[sample_idx])
        all_states.append(states)
        all_resid.append(flux_sum - source.reshape(NX, NY, NZ))
    return (jnp.stack(all_states, 0), jnp.stack(all_resid, 0))
```

```python
import math

import jax
import jax.numpy as jnp
import numpy as np
from jax import lax
from jax.experimental import pallas as pl
from jax.experimental.pallas import tpu as pltpu
from jax.sharding import PartitionSpec as P

NX = 128
NY = 128
NZ = 128
MX = 32
MY = 32
MZ = 32
C = 32
FIN = 4
LAYERS = 2
WELLS = 32


def padded_2(block, sides, width):
    for axis, dim in sides:
        count = lax.axis_size(axis)
        forward = [(i, i + 1) for i in range(count - 1)]
        backward = [(target, source) for source, target in forward]
        low = lax.ppermute(
            lax.slice_in_dim(block, block.shape[dim] - width, None, axis=dim), axis, forward
        )
        high = lax.ppermute(lax.slice_in_dim(block, 0, width, axis=dim), axis, backward)
        block = jnp.concatenate([low, block, high], axis=dim)
    return block


def freq_table(length, kept, one_sided):
    indices = jnp.arange(kept, dtype=jnp.int32)
    if one_sided:
        return indices
    return jnp.where(indices < kept // 2, indices, length - kept + indices)


def wave_parts(length, kept, one_sided):
    freqs = freq_table(length, kept, one_sided)
    places = jnp.arange(length, dtype=jnp.int32)
    phase_turns = freqs[:, None] * places[None, :] % length
    angles = phase_turns.astype(jnp.float32) * (2.0 * math.pi / length)
    norm_scale = 1.0 / math.sqrt(length)
    return (jnp.cos(angles) * norm_scale, jnp.sin(angles) * norm_scale)


def forward_table(length, kept):
    cosine_vals, sine_vals = wave_parts(length, kept, False)
    return jnp.stack(
        [jnp.stack([cosine_vals.T, -sine_vals.T], 1), jnp.stack([sine_vals.T, cosine_vals.T], 1)], 1
    ).astype(jnp.bfloat16)


def inverse_table(length, kept):
    cosine_vals, sine_vals = wave_parts(length, kept, False)
    return jnp.stack(
        [jnp.stack([cosine_vals, sine_vals], 1), jnp.stack([-sine_vals, cosine_vals], 1)], 1
    ).astype(jnp.bfloat16)


def z_tables():
    cosine_vals, sine_vals = wave_parts(NZ, MZ, True)
    weights_k = jnp.where(jnp.arange(MZ) == 0, 1.0, 2.0).astype(jnp.float32)[:, None]
    z_forward = jnp.concatenate([cosine_vals.T, -sine_vals.T], 1).astype(jnp.bfloat16)
    z_inverse = jnp.concatenate([weights_k * cosine_vals, -weights_k * sine_vals], 0).astype(
        jnp.bfloat16
    )
    return (z_forward, z_inverse)


def gelu_tanh(values):
    return jax.nn.gelu(values, approximate=True)


def face_term(cond_a, cond_b, press_a, press_b):
    return 2.0 * cond_a * cond_b / (cond_a + cond_b) * (press_a - press_b)


def mobility_of(saturation, log_values):
    return jnp.exp(log_values) * (
        saturation * saturation + 0.5 * (1.0 - saturation) * (1.0 - saturation)
    )


def darcy(pressure, conduct, well_cells, well_rates):
    batches, planes = pressure.shape[0], pressure.shape[1]
    space_index = lax.axis_index("space")
    pad_cond = jnp.pad(conduct, ((0, 0), (0, 0), (1, 1), (1, 1)))
    pad_press = jnp.pad(pressure, ((0, 0), (0, 0), (1, 1), (1, 1)))
    flux_sum = face_term(conduct, pad_cond[:, :, 2:, 1:-1], pressure, pad_press[:, :, 2:, 1:-1])
    flux_sum = flux_sum + face_term(
        conduct, pad_cond[:, :, :-2, 1:-1], pressure, pad_press[:, :, :-2, 1:-1]
    )
    flux_sum = flux_sum + face_term(
        conduct, pad_cond[:, :, 1:-1, 2:], pressure, pad_press[:, :, 1:-1, 2:]
    )
    flux_sum = flux_sum + face_term(
        conduct, pad_cond[:, :, 1:-1, :-2], pressure, pad_press[:, :, 1:-1, :-2]
    )
    fields = jnp.stack([pressure, conduct], 1)
    padded = padded_2(fields.astype(jnp.bfloat16), (("space", 2),), 1).astype(fields.dtype)
    press_low = padded[:, 0, 0]
    press_high = padded[:, 0, -1]
    cond_low = padded[:, 1, 0]
    cond_high = padded[:, 1, -1]
    press_below = jnp.concatenate([press_low[:, None], pressure[:, :-1]], 1)
    cond_below = jnp.concatenate([cond_low[:, None], conduct[:, :-1]], 1)
    press_above = jnp.concatenate([pressure[:, 1:], press_high[:, None]], 1)
    cond_above = jnp.concatenate([conduct[:, 1:], cond_high[:, None]], 1)
    lower_terms = face_term(conduct, cond_below, pressure, press_below)
    upper_terms = face_term(conduct, cond_above, pressure, press_above)
    flux_sum = flux_sum + lower_terms + upper_terms
    well_x = well_cells // (NY * NZ) - space_index * planes
    well_y = well_cells // NZ % NY
    well_z = well_cells % NZ
    onehot_x = (well_x[:, :, None] == jnp.arange(planes, dtype=jnp.int32)[None, None, :]).astype(
        jnp.float32
    ) * well_rates[:, :, None]
    onehot_y = (well_y[:, :, None] == jnp.arange(NY, dtype=jnp.int32)[None, None, :]).astype(
        jnp.float32
    )
    onehot_z = (well_z[:, :, None] == jnp.arange(NZ, dtype=jnp.int32)[None, None, :]).astype(
        jnp.float32
    )
    plane_rows = (onehot_x[:, :, :, None] * onehot_y[:, :, None, :]).reshape(
        batches, WELLS, planes * NY
    )
    source = jnp.einsum(
        "bwa,bwz->baz", plane_rows, onehot_z, precision=lax.Precision.HIGHEST
    ).reshape(batches, planes, NY, NZ)
    return flux_sum - source


def local_general(
    features,
    log_perm,
    well_cells,
    well_rates,
    lift_in,
    lift_out,
    spec_weight,
    point_weight,
    dec_in,
    dec_out,
):
    batches = features.shape[0]
    planes = features.shape[2]
    space_index = lax.axis_index("space")
    block = spec_weight.shape[1]
    cell_count = planes * NY * NZ
    z_forward, z_inverse = z_tables()
    y_forward = forward_table(NY, MY)
    y_inverse = inverse_table(NY, MY)
    x_forward = forward_table(NX, MX)
    x_inverse = inverse_table(NX, MX)
    perm_b = log_perm.astype(jnp.bfloat16).reshape(batches, 1, cell_count)
    lift_input = jnp.concatenate([features.reshape(batches, FIN, cell_count), perm_b], 1)
    lift_hidden = jnp.einsum("bfn,fh->bhn", lift_input, lift_in, preferred_element_type=jnp.float32)
    lifted = gelu_tanh(lift_hidden).astype(jnp.bfloat16)
    hidden_state = jnp.einsum(
        "bhn,hc->bcn", lifted, lift_out, preferred_element_type=jnp.float32
    ).astype(jnp.bfloat16)
    for layer_idx in range(LAYERS):
        zspec = jnp.dot(hidden_state.reshape(-1, NZ), z_forward, preferred_element_type=jnp.float32)
        zspec = zspec.astype(jnp.bfloat16).reshape(batches * C * planes, NY, 2, MZ)
        yz_spec = jnp.einsum(
            "aypk,ypqj->aqjk", zspec, y_forward, preferred_element_type=jnp.float32
        )
        yz_spec = yz_spec.astype(jnp.bfloat16).reshape(batches, C, planes, 2, MY * MZ)
        mode_weights = spec_weight[layer_idx].reshape(block, C, MX, 2, C)
        spectrum = jnp.einsum(
            "bcxpm,xpqi->bcqim",
            lax.all_to_all(yz_spec, "space", split_axis=4, concat_axis=2, tiled=True),
            x_forward,
            preferred_element_type=jnp.float32,
        ).astype(jnp.bfloat16)
        products = jnp.einsum(
            "bcqim,mcipo->bimqpo", spectrum, mode_weights, preferred_element_type=jnp.float32
        )
        real_part = products[:, :, :, 0, 0] - products[:, :, :, 1, 1]
        imag_part = products[:, :, :, 0, 1] + products[:, :, :, 1, 0]
        mixed_modes = jnp.stack([real_part, imag_part], 3).astype(jnp.bfloat16)
        back_field = jnp.einsum(
            "bimqo,iqpx->boxpm", mixed_modes, x_inverse, preferred_element_type=jnp.float32
        ).astype(jnp.bfloat16)
        returned = lax.all_to_all(back_field, "space", split_axis=2, concat_axis=4, tiled=True)
        returned = returned.reshape(batches * C * planes, 2, MY, MZ)
        y_back = jnp.einsum(
            "aqjk,jqpy->aypk", returned, y_inverse, preferred_element_type=jnp.float32
        ).astype(jnp.bfloat16)
        spectral = jnp.dot(
            y_back.reshape(-1, 2 * MZ), z_inverse, preferred_element_type=jnp.float32
        ).reshape(batches, C, cell_count)
        local_term = jnp.einsum(
            "bcn,co->bon", hidden_state, point_weight[layer_idx], preferred_element_type=jnp.float32
        )
        hidden_state = gelu_tanh(spectral + local_term).astype(jnp.bfloat16)
    decoded = gelu_tanh(
        jnp.einsum("bcn,cd->bdn", hidden_state, dec_in, preferred_element_type=jnp.float32)
    ).astype(jnp.bfloat16)
    decoded_out = jnp.einsum("bdn,de->ben", decoded, dec_out, preferred_element_type=jnp.float32)
    pressure = decoded_out[:, 0].reshape(batches, planes, NY, NZ)
    saturation = jax.nn.sigmoid(decoded_out[:, 1]).reshape(batches, planes, NY, NZ)
    states = jnp.stack([pressure, saturation], 1)
    conduct = mobility_of(saturation, log_perm)
    return (states, darcy(pressure, conduct, well_cells, well_rates))


BF = jnp.bfloat16
F32 = jnp.float32
PAIRS = NY // 2
SKEW = 4
PITCH = PAIRS + SKEW
MODE_STEP = 8
ROWS = 8
UNROLL = 4
LIFT_UNROLL = 4
LANES = 128


def np_waves(length, kept, one_sided):
    index = np.arange(kept)
    freqs = index if one_sided else np.where(index < kept // 2, index, length - kept + index)
    angles = (freqs[:, None] * np.arange(length)[None, :] % length) * (2.0 * math.pi / length)
    norm = 1.0 / math.sqrt(length)
    return np.cos(angles) * norm, np.sin(angles) * norm


def np_forward(length, kept):
    cosine, sine = np_waves(length, kept, False)
    return np.stack([np.stack([cosine.T, -sine.T], 1), np.stack([sine.T, cosine.T], 1)], 1)


def np_inverse(length, kept):
    cosine, sine = np_waves(length, kept, False)
    return np.stack([np.stack([cosine, sine], 1), np.stack([-sine, cosine], 1)], 1)


def by_plane(table, axis, count):
    planes = NX // count
    order = np.arange(NX).reshape(count, planes).T.reshape(-1)
    return np.take(table, order, axis)


def tables_for(count):
    own = MY // count
    cosine, sine = np_waves(NZ, MZ, True)
    twice = np.where(np.arange(MZ) == 0, 1.0, 2.0)[:, None]
    z_forward = np.concatenate([cosine.T, -sine.T], 1)
    z_inverse = np.concatenate([twice * cosine, -twice * sine], 0)
    y_forward = np_forward(NY, MY).reshape(PAIRS, 2, 2, 2, count, own)
    y_inverse = np_inverse(NY, MY).reshape(count, own, 2, 2, PAIRS, 2)
    pair = np.eye(2)
    tables = {
        "zf": np.kron(pair, z_forward),
        "zi": 0.5 * np.kron(pair, z_inverse),
        "yf": y_forward.transpose(3, 5, 4, 1, 2, 0).reshape(2 * MY, 2 * NY),
        "yi": y_inverse.transpose(5, 3, 4, 2, 1, 0).reshape(2 * NY, 2 * MY),
        "xf": by_plane(np_forward(NX, MX).transpose(2, 3, 1, 0), 3, count).reshape(2 * MX, 2 * NX),
        "xi": by_plane(np_inverse(NX, MX).transpose(2, 3, 0, 1), 1, count).reshape(2 * NX, 2 * MX),
    }
    return {name: jnp.asarray(table.astype(np.float32)).astype(BF) for name, table in tables.items()}


def dot32(a, b):
    return jnp.dot(a, b, preferred_element_type=F32)


def gelu_of_half(values):
    u = values.astype(BF)
    scale = math.sqrt(2.0 / math.pi)
    inner = u * (BF(2.0 * scale) + BF(8.0 * scale * 0.044715) * (u * u))
    return u + u * jnp.tanh(inner)


def swap_blocks(four):
    shape = four[0].shape
    lane = lax.broadcasted_iota(jnp.int32, shape, 1)
    low = lane < 64
    even = lane % 64 < 32
    a0, a1, a2, a3 = four

    def cross(a, b, keep, shift):
        return (
            jnp.where(keep, a, pltpu.roll(b, shift, 1)),
            jnp.where(keep, pltpu.roll(a, LANES - shift, 1), b),
        )

    b0, b2 = cross(a0, a2, low, 64)
    b1, b3 = cross(a1, a3, low, 64)
    c0, c1 = cross(b0, b1, even, 32)
    c2, c3 = cross(b2, b3, even, 32)
    return c0, c1, c2, c3


def send_plane(me, count, plane, send, recv, send_sem, recv_sem):
    for shift in range(1, count):
        target = lax.rem(me + shift, count)
        pltpu.make_async_remote_copy(
            src_ref=send.at[plane, target],
            dst_ref=recv.at[plane, me],
            send_sem=send_sem.at[plane],
            recv_sem=recv_sem.at[plane],
            device_id={"space": target},
            device_id_type=pl.DeviceIdType.MESH,
        ).start()
    recv[plane, me] = send[plane, me]


def wait_plane(count, plane, buffer, sem):
    part = buffer.at[plane, pl.ds(0, count - 1)]
    pltpu.make_async_copy(part, part, sem.at[plane]).wait()


def to_modes(plane, count, yf_ref, zs, flat, send):
    pieces = []
    for group in range(C // 4):
        four = [zs[(group * 4 + r) * PITCH : (group * 4 + r) * PITCH + PAIRS, :] for r in range(4)]
        pieces.append(jnp.concatenate([p.astype(BF) for p in swap_blocks(four)], 0))
    modes = dot32(yf_ref[...], jnp.concatenate(pieces, 1))
    tiles = C * MZ // LANES
    slots = 2 * MY // count * tiles
    for s in range(2 * MY // count):
        for t in range(tiles):
            flat[pl.ds(s * tiles + t, count, stride=slots + SKEW), :] = modes[
                s * count : (s + 1) * count, t * LANES : (t + 1) * LANES
            ]
    for dst in range(count):
        send[plane, dst] = flat[pl.ds(dst * (slots + SKEW), slots), :].astype(BF)


def lay_out(zs, start, values):
    for r in range(ROWS):
        zs[pl.ds(start + r, C, stride=PITCH), :] = values[r * C : (r + 1) * C, :]


def hid_rows(index):
    return pl.ds(pl.multiple_of(index * ROWS * C, ROWS * C), ROWS * C)


def lift_plane(plane, feat_ref, perm_ref, in_ref, lo_ref, zf_ref, hid, plain, xs, zs):
    for f in range(FIN + 1):
        plain[...] = perm_ref[0, plane] if f == FIN else feat_ref[0, f, plane].astype(F32)
        for y2 in range(2):
            xs[y2, pl.ds(f, PAIRS, stride=8), :] = plain[pl.ds(y2, PAIRS, stride=2), :]
    width = lo_ref.shape[1]
    parts = in_ref.shape[0] // width

    def group(step, carry):
        base = step * LIFT_UNROLL

        def first(n):
            u, r = n // parts, n % parts
            start = pl.multiple_of((base + u) * ROWS * 8, ROWS * 8)
            x = jnp.concatenate([xs[y2, pl.ds(start, ROWS * 8), :] for y2 in range(2)], 1)
            return dot32(in_ref[r * width : (r + 1) * width, :], x.astype(BF))

        now = first(0)
        done = []
        for n in range(LIFT_UNROLL * parts):
            later = first(n + 1) if n + 1 < LIFT_UNROLL * parts else None
            done.append(dot32(lo_ref[...], gelu_of_half(now)).astype(BF))
            now = later
            if len(done) == parts:
                index = base + n // parts
                hidden = jnp.concatenate(done, 0)
                done = []
                hid[plane, hid_rows(index), :] = hidden
                lay_out(zs, index * ROWS, dot32(hidden, zf_ref[...]))
        return carry

    lax.fori_loop(0, PAIRS // ROWS // LIFT_UNROLL, group, 0)


def from_modes(plane, count, recv, yi_ref, flat, zs):
    tiles = C * MZ // LANES
    slots = 2 * MY // count * tiles
    for src in range(count):
        flat[pl.ds(src * (slots + SKEW), slots), :] = recv[plane, src].astype(F32)
    rows = []
    for s in range(2 * MY // count):
        rows.append(
            jnp.concatenate(
                [flat[pl.ds(s * tiles + t, count, stride=slots + SKEW), :] for t in range(tiles)], 1
            ).astype(BF)
        )
    back = dot32(yi_ref[...], jnp.concatenate(rows, 0))
    for group in range(C // 4):
        lanes = slice(group * LANES, (group + 1) * LANES)
        four = [back[g * PAIRS : (g + 1) * PAIRS, lanes] for g in range(4)]
        for r, piece in enumerate(swap_blocks(four)):
            zs[(group * 4 + r) * PITCH : (group * 4 + r) * PITCH + PAIRS, :] = piece


def layer_rows(plane, index, zs, hid, zi_ref, kp):
    start = index * ROWS
    parts = [zs[pl.ds(start + r, C, stride=PITCH), :].astype(BF) for r in range(ROWS)]
    spectral = dot32(jnp.concatenate(parts, 0), zi_ref[...])
    return gelu_of_half(spectral + dot32(kp, hid[plane, hid_rows(index), :]))


def middle_plane(plane, kp, zi_ref, zf_ref, hid, zs, zs2):
    def block(index, carry):
        hidden = layer_rows(plane, index, zs, hid, zi_ref, kp)
        hid[plane, hid_rows(index), :] = hidden
        lay_out(zs2, index * ROWS, dot32(hidden, zf_ref[...]))
        return carry

    lax.fori_loop(0, PAIRS // ROWS, block, 0, unroll=UNROLL)


def final_plane(plane, kp, zi_ref, di_ref, do_ref, perm_ref, hid, zs, st_ref, cond_ref):
    def block(index, carry):
        hidden = layer_rows(plane, index, zs, hid, zi_ref, kp)
        both = dot32(do_ref[...], gelu_of_half(dot32(di_ref[...], hidden)))
        for y2 in range(2):
            lanes = slice(y2 * NZ, (y2 + 1) * NZ)
            where = pl.ds(index * ROWS * 2 + y2, ROWS, stride=2)
            st_ref[0, 0, plane, where, :] = both[:ROWS, lanes]
            st_ref[0, 1, plane, where, :] = both[ROWS:, lanes]
        return carry

    lax.fori_loop(0, PAIRS // ROWS, block, 0, unroll=UNROLL)
    sat = jax.nn.sigmoid(st_ref[0, 1, plane])
    st_ref[0, 1, plane] = sat
    cond_ref[0, plane] = mobility_of(sat, perm_ref[0, plane])


def mix_modes(planes, count, recv, send, wbuf, xf_ref, xi_ref, flat, spec, rows, mixed, turned):
    own = MY // count
    tiles = C * MZ // LANES
    slots = 2 * own * tiles
    pitch = slots + SKEW
    every = count * planes
    lane = lax.broadcasted_iota(jnp.int32, (1, LANES), 1)
    low = lane < 64
    even = lane % 64 < 32

    def unpack(plane, carry):
        for src in range(count):
            start = (plane * count + src) * pitch
            flat[pl.ds(start, slots), :] = recv[plane, src].astype(F32)
        return carry

    lax.fori_loop(0, planes, unpack, 0)

    def column(p, t):
        return flat[pl.ds(p * own * tiles + t, every, stride=pitch), :].astype(BF)

    for pair in range(own * tiles // 2):
        right = jnp.concatenate(
            [
                jnp.concatenate([column(p, pair * 2 + half) for half in range(2)], 1)
                for p in range(2)
            ],
            0,
        )
        total = dot32(xf_ref[...], right)
        for half in range(2):
            part = total[:, half * LANES : (half + 1) * LANES].T
            for r in range(4):
                first = (pair * 2 + half) * 4 + r
                spec[pl.ds(first * (MZ + SKEW), MZ), : 2 * MX] = part[r * MZ : (r + 1) * MZ, :]
    groups = own * MZ // MODE_STEP
    for group in range(groups):
        jj, k = group * MODE_STEP // MZ, group * MODE_STEP % MZ
        base = jj * C * (MZ + SKEW) + k
        picked = [
            spec[pl.ds(base + r, C, stride=MZ + SKEW), : 2 * MX] for r in range(MODE_STEP)
        ]
        rows[group] = jnp.concatenate(picked, 0).T
    wide = MODE_STEP * C
    own_mode = lax.broadcasted_iota(jnp.int32, (MODE_STEP, wide), 0) == (
        lax.broadcasted_iota(jnp.int32, (MODE_STEP, wide), 1) // C
    )
    per = wide // (2 * C)

    def step(group, carry):
        first = pl.multiple_of(group * MODE_STEP, MODE_STEP)
        for piece in range(MX // per):
            left = []
            for i in range(per):
                for q in range(2):
                    row = rows[group, pl.ds(q * MX + piece * per + i, MODE_STEP, stride=0), :]
                    left.append(jnp.where(own_mode, row, 0.0))
            lo = piece * wide
            weights = wbuf[pl.ds(first, MODE_STEP), :, lo : lo + wide].reshape(wide, wide)
            both = dot32(jnp.concatenate(left, 0).astype(BF), weights)

            def part(i, q, t):
                at = (i * 2 + q) * MODE_STEP
                return both[at : at + MODE_STEP, t * LANES : (t + 1) * LANES]

            for t in range(2):
                real, imag = (
                    jnp.where(low, part(2 * t, q, t), part(2 * t + 1, q, t)) for q in range(2)
                )
                turn = jnp.where(even, -pltpu.roll(imag, LANES - C, 1), pltpu.roll(imag, C, 1))
                mixed[pl.ds(first, MODE_STEP), lo + t * LANES : lo + (t + 1) * LANES] = real + turn
        return carry

    lax.fori_loop(0, groups, step, 0)
    for block in range(MX * 2 * C // LANES):
        part = mixed[:, block * LANES : (block + 1) * LANES].T
        for r in range(4):
            first = (block * 4 + r) * (C + SKEW)
            turned[pl.ds(first, C), : own * MZ] = part[r * C : (r + 1) * C, :]
    for pair in range(tiles // 2):
        right = [[], []]
        for half in range(2):
            o = (pair * 2 + half) * 4
            a = [turned[pl.ds(o + r, 2 * MX, stride=C + SKEW), :] for r in range(4)]
            b = jnp.where(low, a[0], pltpu.roll(a[2], 64, 1))
            c = jnp.where(low, a[1], pltpu.roll(a[3], 64, 1))
            right[0].append(jnp.where(even, b, pltpu.roll(c, 32, 1)))
            right[1].append(jnp.where(even, pltpu.roll(b, LANES - 32, 1), c))
        for jj in range(own):
            back = dot32(xi_ref[...], jnp.concatenate(right[jj], 1).astype(BF))
            for p in range(2):
                for half in range(2):
                    slot = (p * own + jj) * tiles + pair * 2 + half
                    flat[pl.ds(slot, every, stride=pitch), :] = back[
                        p * every : (p + 1) * every, half * LANES : (half + 1) * LANES
                    ]

    def pack(plane, carry):
        for dst in range(count):
            start = (plane * count + dst) * pitch
            send[plane, dst] = flat[pl.ds(start, slots), :].astype(BF)
        return carry

    lax.fori_loop(0, planes, pack, 0)


def whole_kernel(
    planes, count, feat_ref, perm_ref, lift_in, lift_out, point, dec_in, dec_out, zf_ref, zi_ref,
    yf_ref, yi_ref, xf_ref, xi_ref, w_hbm, st_ref, cond_ref,
    hid, wbuf, send_f, recv_f, send_b, recv_b, flat, spec, rows, mixed, turned, zs, zs2, xs, plain,
    in_ref, lo_ref, kp_ref, di_ref, do_ref, w_sem, sf_sem, rf_sem, sb_sem, rb_sem,
):
    me = lax.axis_index("space")
    barrier = pltpu.get_barrier_semaphore()
    for shift in range(1, count):
        pl.semaphore_signal(
            barrier,
            inc=1,
            device_id={"space": lax.rem(me + shift, count)},
            device_id_type=pl.DeviceIdType.MESH,
        )
    fetch = pltpu.make_async_copy(w_hbm.at[0], wbuf, w_sem.at[0])
    fetch.start()
    xs[...] = jnp.zeros_like(xs)
    in_ref[...] = diag_of(lift_in[...], ROWS, 8, 0.5)
    lo_ref[...] = diag_of(lift_out[...], 2, lift_out.shape[1], 1.0, True)
    for layer in range(LAYERS):
        kp_ref[layer] = diag_of(point[layer], ROWS, C, 0.5)
    di_ref[...] = diag_of(dec_in[...], ROWS, C, 0.5)
    dec = dec_out.shape[1]
    do_ref[...] = spread(
        dec_out[...],
        2 * ROWS,
        ROWS * dec,
        lambda i: i // ROWS,
        lambda j: j % dec,
        lambda i, j: i % ROWS == j // dec,
        1.0,
        True,
    )
    pl.semaphore_wait(barrier, count - 1)

    def over(body):
        def run(plane, carry):
            body(plane)
            return carry

        lax.fori_loop(0, planes, run, 0)

    def lift(plane):
        lift_plane(plane, feat_ref, perm_ref, in_ref, lo_ref, zf_ref, hid, plain, xs, zs)
        to_modes(plane, count, yf_ref, zs, flat, send_f)
        send_plane(me, count, plane, send_f, recv_f, sf_sem, rf_sem)

    over(lift)
    for layer in range(LAYERS):
        fetch.wait()
        over(lambda plane: wait_plane(count, plane, recv_f, rf_sem))
        over(lambda plane: wait_plane(count, plane, send_f, sf_sem))
        mix_modes(
            planes, count, recv_f, send_b, wbuf, xf_ref, xi_ref, flat, spec, rows, mixed, turned
        )
        if layer + 1 < LAYERS:
            fetch = pltpu.make_async_copy(w_hbm.at[layer + 1], wbuf, w_sem.at[layer + 1])
            fetch.start()
        over(lambda plane: send_plane(me, count, plane, send_b, recv_b, sb_sem, rb_sem))

        def rest(plane):
            wait_plane(count, plane, recv_b, rb_sem)
            from_modes(plane, count, recv_b, yi_ref, flat, zs)
            if layer + 1 < LAYERS:
                middle_plane(plane, kp_ref[layer], zi_ref, zf_ref, hid, zs, zs2)
                to_modes(plane, count, yf_ref, zs2, flat, send_f)
                send_plane(me, count, plane, send_f, recv_f, sf_sem, rf_sem)
            else:
                final_plane(
                    plane, kp_ref[layer], zi_ref, di_ref, do_ref, perm_ref, hid, zs, st_ref, cond_ref
                )

        over(rest)
        over(lambda plane: wait_plane(count, plane, send_b, sb_sem))


def ones_where(shape, test, value=1.0):
    row = lax.broadcasted_iota(jnp.int32, shape, 0)
    col = lax.broadcasted_iota(jnp.int32, shape, 1)
    return jnp.where(test(row, col), value, 0.0)


def spread(matrix, rows, cols, row_of, col_of, keep, value, turned):
    depth, height = matrix.shape[::-1] if turned else matrix.shape
    take = ones_where((rows, height), lambda i, j: row_of(i) == j).astype(BF)
    put = ones_where((depth, cols), lambda i, j: col_of(j) == i).astype(BF)
    dims = (((1,), (0 if turned else 1,)), ((), ()))
    part = lax.dot_general(take, matrix, dims, preferred_element_type=F32)
    return (dot32(part.astype(BF), put) * ones_where((rows, cols), keep, value)).astype(BF)


def diag_of(matrix, copies, width, value, turned=False):
    height = matrix.shape[0 if turned else 1]
    return spread(
        matrix,
        copies * height,
        copies * width,
        lambda i: i % height,
        lambda j: j % width,
        lambda i, j: i // height == j // width,
        value,
        turned,
    )


def local_fast(
    features,
    log_perm,
    well_cells,
    well_rates,
    lift_in,
    lift_out,
    spec_weight,
    point_weight,
    dec_in,
    dec_out,
):
    planes = features.shape[2]
    count = lax.axis_size("space")
    own = MY // count
    modes = own * MZ
    slots = 2 * modes * C // LANES
    tables = tables_for(count)
    lift, dec = lift_in.shape[1], dec_in.shape[1]
    operands = (
        features,
        log_perm,
        lift_in,
        lift_out.T,
        point_weight,
        dec_in,
        dec_out.T,
    ) + tuple(tables[name] for name in ("zf", "zi", "yf", "yi", "xf", "xi"))
    vmem = pl.BlockSpec(memory_space=pltpu.VMEM)
    exchange = pltpu.VMEM((planes, count, slots, LANES), BF)
    states, conduct = pl.pallas_call(
        lambda *refs: whole_kernel(planes, count, *refs),
        in_specs=[vmem] * len(operands) + [pl.BlockSpec(memory_space=pl.ANY)],
        out_specs=[vmem, vmem],
        out_shape=[
            jax.ShapeDtypeStruct((1, 2, planes, NY, NZ), F32),
            jax.ShapeDtypeStruct((1, planes, NY, NZ), F32),
        ],
        scratch_shapes=[
            pltpu.VMEM((planes, PAIRS * C, 2 * NZ), BF),
            pltpu.VMEM(spec_weight.shape[1:], BF),
            exchange,
            exchange,
            exchange,
            exchange,
            pltpu.VMEM((planes * count * (slots + SKEW), LANES), F32),
            pltpu.VMEM((own * C * (MZ + SKEW), LANES), F32),
            pltpu.VMEM((modes // MODE_STEP, 2 * MX, MODE_STEP * C), F32),
            pltpu.VMEM((modes, MX * 2 * C), F32),
            pltpu.VMEM((2 * MX * (C + SKEW), LANES), F32),
            pltpu.VMEM((C * PITCH, LANES), F32),
            pltpu.VMEM((C * PITCH, LANES), F32),
            pltpu.VMEM((2, PAIRS * 8, NZ), F32),
            pltpu.VMEM((NY, NZ), F32),
            pltpu.VMEM((ROWS * lift, ROWS * 8), BF),
            pltpu.VMEM((2 * C, 2 * lift), BF),
            pltpu.VMEM((LAYERS, ROWS * C, ROWS * C), BF),
            pltpu.VMEM((ROWS * dec, ROWS * C), BF),
            pltpu.VMEM((2 * ROWS, ROWS * dec), BF),
            pltpu.SemaphoreType.DMA((LAYERS,)),
        ]
        + [pltpu.SemaphoreType.DMA((planes,))] * 4,
        compiler_params=pltpu.CompilerParams(
            collective_id=0, has_side_effects=True, vmem_limit_bytes=60 * 1024 * 1024
        ),
        name="whole",
    )(*operands, spec_weight)
    return (states, darcy(states[:, 0], conduct, well_cells, well_rates))


def local(features, log_perm, well_cells, well_rates, lift_in, lift_out, spec_weight, *rest):
    batches, planes = features.shape[0], features.shape[2]
    count = lax.axis_size("space")
    fits = batches == 1 and planes == 8 and count % 8 == 0 and MY == 2 * count
    run = local_fast if fits else local_general
    return run(
        features, log_perm, well_cells, well_rates, lift_in, lift_out, spec_weight, *rest
    )


def solution(mesh):
    return jax.shard_map(
        local,
        mesh=mesh,
        in_specs=(
            P("sample", None, "space", None, None),
            P("sample", "space", None, None),
            P("sample", None),
            P("sample", None),
            P(),
            P(),
            P(None, "space", None, None),
            P(),
            P(),
            P(),
        ),
        out_specs=(P("sample", None, "space", None, None), P("sample", "space", None, None)),
        check_vma=False,
    )
```

```python
import math

import jax
import jax.numpy as jnp
import numpy as np
from jax import lax
from jax.experimental import pallas as pl
from jax.experimental.pallas import tpu as pltpu
from jax.sharding import PartitionSpec as P

NX = 128
NY = 128
NZ = 128
MX = 32
MY = 32
MZ = 32
C = 32
FIN = 4
LAYERS = 2
WELLS = 32


def padded_2(block, sides, width):
    for axis, dim in sides:
        count = lax.axis_size(axis)
        forward = [(i, i + 1) for i in range(count - 1)]
        backward = [(target, source) for source, target in forward]
        low = lax.ppermute(
            lax.slice_in_dim(block, block.shape[dim] - width, None, axis=dim), axis, forward
        )
        high = lax.ppermute(lax.slice_in_dim(block, 0, width, axis=dim), axis, backward)
        block = jnp.concatenate([low, block, high], axis=dim)
    return block


def freq_table(length, kept, one_sided):
    indices = jnp.arange(kept, dtype=jnp.int32)
    if one_sided:
        return indices
    return jnp.where(indices < kept // 2, indices, length - kept + indices)


def wave_parts(length, kept, one_sided):
    freqs = freq_table(length, kept, one_sided)
    places = jnp.arange(length, dtype=jnp.int32)
    phase_turns = freqs[:, None] * places[None, :] % length
    angles = phase_turns.astype(jnp.float32) * (2.0 * math.pi / length)
    norm_scale = 1.0 / math.sqrt(length)
    return (jnp.cos(angles) * norm_scale, jnp.sin(angles) * norm_scale)


def forward_table(length, kept):
    cosine_vals, sine_vals = wave_parts(length, kept, False)
    return jnp.stack(
        [jnp.stack([cosine_vals.T, -sine_vals.T], 1), jnp.stack([sine_vals.T, cosine_vals.T], 1)], 1
    ).astype(jnp.bfloat16)


def inverse_table(length, kept):
    cosine_vals, sine_vals = wave_parts(length, kept, False)
    return jnp.stack(
        [jnp.stack([cosine_vals, sine_vals], 1), jnp.stack([-sine_vals, cosine_vals], 1)], 1
    ).astype(jnp.bfloat16)


def z_tables():
    cosine_vals, sine_vals = wave_parts(NZ, MZ, True)
    weights_k = jnp.where(jnp.arange(MZ) == 0, 1.0, 2.0).astype(jnp.float32)[:, None]
    z_forward = jnp.concatenate([cosine_vals.T, -sine_vals.T], 1).astype(jnp.bfloat16)
    z_inverse = jnp.concatenate([weights_k * cosine_vals, -weights_k * sine_vals], 0).astype(
        jnp.bfloat16
    )
    return (z_forward, z_inverse)


def gelu_tanh(values):
    return jax.nn.gelu(values, approximate=True)


def face_term(cond_a, cond_b, press_a, press_b):
    return 2.0 * cond_a * cond_b / (cond_a + cond_b) * (press_a - press_b)


def mobility_of(saturation, log_values):
    return jnp.exp(log_values) * (
        saturation * saturation + 0.5 * (1.0 - saturation) * (1.0 - saturation)
    )


def darcy(pressure, conduct, well_cells, well_rates):
    batches, planes = pressure.shape[0], pressure.shape[1]
    space_index = lax.axis_index("space")
    pad_cond = jnp.pad(conduct, ((0, 0), (0, 0), (1, 1), (1, 1)))
    pad_press = jnp.pad(pressure, ((0, 0), (0, 0), (1, 1), (1, 1)))
    flux_sum = face_term(conduct, pad_cond[:, :, 2:, 1:-1], pressure, pad_press[:, :, 2:, 1:-1])
    flux_sum = flux_sum + face_term(
        conduct, pad_cond[:, :, :-2, 1:-1], pressure, pad_press[:, :, :-2, 1:-1]
    )
    flux_sum = flux_sum + face_term(
        conduct, pad_cond[:, :, 1:-1, 2:], pressure, pad_press[:, :, 1:-1, 2:]
    )
    flux_sum = flux_sum + face_term(
        conduct, pad_cond[:, :, 1:-1, :-2], pressure, pad_press[:, :, 1:-1, :-2]
    )
    fields = jnp.stack([pressure, conduct], 1)
    padded = padded_2(fields.astype(jnp.bfloat16), (("space", 2),), 1).astype(fields.dtype)
    press_low = padded[:, 0, 0]
    press_high = padded[:, 0, -1]
    cond_low = padded[:, 1, 0]
    cond_high = padded[:, 1, -1]
    press_below = jnp.concatenate([press_low[:, None], pressure[:, :-1]], 1)
    cond_below = jnp.concatenate([cond_low[:, None], conduct[:, :-1]], 1)
    press_above = jnp.concatenate([pressure[:, 1:], press_high[:, None]], 1)
    cond_above = jnp.concatenate([conduct[:, 1:], cond_high[:, None]], 1)
    lower_terms = face_term(conduct, cond_below, pressure, press_below)
    upper_terms = face_term(conduct, cond_above, pressure, press_above)
    flux_sum = flux_sum + lower_terms + upper_terms
    well_x = well_cells // (NY * NZ) - space_index * planes
    well_y = well_cells // NZ % NY
    well_z = well_cells % NZ
    onehot_x = (well_x[:, :, None] == jnp.arange(planes, dtype=jnp.int32)[None, None, :]).astype(
        jnp.float32
    ) * well_rates[:, :, None]
    onehot_y = (well_y[:, :, None] == jnp.arange(NY, dtype=jnp.int32)[None, None, :]).astype(
        jnp.float32
    )
    onehot_z = (well_z[:, :, None] == jnp.arange(NZ, dtype=jnp.int32)[None, None, :]).astype(
        jnp.float32
    )
    plane_rows = (onehot_x[:, :, :, None] * onehot_y[:, :, None, :]).reshape(
        batches, WELLS, planes * NY
    )
    source = jnp.einsum(
        "bwa,bwz->baz", plane_rows, onehot_z, precision=lax.Precision.HIGHEST
    ).reshape(batches, planes, NY, NZ)
    return flux_sum - source


def local_general(
    features,
    log_perm,
    well_cells,
    well_rates,
    lift_in,
    lift_out,
    spec_weight,
    point_weight,
    dec_in,
    dec_out,
):
    batches = features.shape[0]
    planes = features.shape[2]
    space_index = lax.axis_index("space")
    block = spec_weight.shape[1]
    cell_count = planes * NY * NZ
    z_forward, z_inverse = z_tables()
    y_forward = forward_table(NY, MY)
    y_inverse = inverse_table(NY, MY)
    x_forward = forward_table(NX, MX)
    x_inverse = inverse_table(NX, MX)
    perm_b = log_perm.astype(jnp.bfloat16).reshape(batches, 1, cell_count)
    lift_input = jnp.concatenate([features.reshape(batches, FIN, cell_count), perm_b], 1)
    lift_hidden = jnp.einsum("bfn,fh->bhn", lift_input, lift_in, preferred_element_type=jnp.float32)
    lifted = gelu_tanh(lift_hidden).astype(jnp.bfloat16)
    hidden_state = jnp.einsum(
        "bhn,hc->bcn", lifted, lift_out, preferred_element_type=jnp.float32
    ).astype(jnp.bfloat16)
    for layer_idx in range(LAYERS):
        zspec = jnp.dot(hidden_state.reshape(-1, NZ), z_forward, preferred_element_type=jnp.float32)
        zspec = zspec.astype(jnp.bfloat16).reshape(batches * C * planes, NY, 2, MZ)
        yz_spec = jnp.einsum(
            "aypk,ypqj->aqjk", zspec, y_forward, preferred_element_type=jnp.float32
        )
        yz_spec = yz_spec.astype(jnp.bfloat16).reshape(batches, C, planes, 2, MY * MZ)
        mode_weights = spec_weight[layer_idx].reshape(block, C, MX, 2, C)
        spectrum = jnp.einsum(
            "bcxpm,xpqi->bcqim",
            lax.all_to_all(yz_spec, "space", split_axis=4, concat_axis=2, tiled=True),
            x_forward,
            preferred_element_type=jnp.float32,
        ).astype(jnp.bfloat16)
        products = jnp.einsum(
            "bcqim,mcipo->bimqpo", spectrum, mode_weights, preferred_element_type=jnp.float32
        )
        real_part = products[:, :, :, 0, 0] - products[:, :, :, 1, 1]
        imag_part = products[:, :, :, 0, 1] + products[:, :, :, 1, 0]
        mixed_modes = jnp.stack([real_part, imag_part], 3).astype(jnp.bfloat16)
        back_field = jnp.einsum(
            "bimqo,iqpx->boxpm", mixed_modes, x_inverse, preferred_element_type=jnp.float32
        ).astype(jnp.bfloat16)
        returned = lax.all_to_all(back_field, "space", split_axis=2, concat_axis=4, tiled=True)
        returned = returned.reshape(batches * C * planes, 2, MY, MZ)
        y_back = jnp.einsum(
            "aqjk,jqpy->aypk", returned, y_inverse, preferred_element_type=jnp.float32
        ).astype(jnp.bfloat16)
        spectral = jnp.dot(
            y_back.reshape(-1, 2 * MZ), z_inverse, preferred_element_type=jnp.float32
        ).reshape(batches, C, cell_count)
        local_term = jnp.einsum(
            "bcn,co->bon", hidden_state, point_weight[layer_idx], preferred_element_type=jnp.float32
        )
        hidden_state = gelu_tanh(spectral + local_term).astype(jnp.bfloat16)
    decoded = gelu_tanh(
        jnp.einsum("bcn,cd->bdn", hidden_state, dec_in, preferred_element_type=jnp.float32)
    ).astype(jnp.bfloat16)
    decoded_out = jnp.einsum("bdn,de->ben", decoded, dec_out, preferred_element_type=jnp.float32)
    pressure = decoded_out[:, 0].reshape(batches, planes, NY, NZ)
    saturation = jax.nn.sigmoid(decoded_out[:, 1]).reshape(batches, planes, NY, NZ)
    states = jnp.stack([pressure, saturation], 1)
    conduct = mobility_of(saturation, log_perm)
    return (states, darcy(pressure, conduct, well_cells, well_rates))


BF = jnp.bfloat16
F32 = jnp.float32
PAIRS = NY // 2
SKEW = 4
PITCH = PAIRS + SKEW
MODE_STEP = 8
ROWS = 8
LOOK = 4
LAG = 1
MID = 2
LANES = 128


def np_waves(length, kept, one_sided):
    index = np.arange(kept)
    freqs = index if one_sided else np.where(index < kept // 2, index, length - kept + index)
    angles = (freqs[:, None] * np.arange(length)[None, :] % length) * (2.0 * math.pi / length)
    norm = 1.0 / math.sqrt(length)
    return np.cos(angles) * norm, np.sin(angles) * norm


def np_forward(length, kept):
    cosine, sine = np_waves(length, kept, False)
    return np.stack([np.stack([cosine.T, -sine.T], 1), np.stack([sine.T, cosine.T], 1)], 1)


def np_inverse(length, kept):
    cosine, sine = np_waves(length, kept, False)
    return np.stack([np.stack([cosine, sine], 1), np.stack([-sine, cosine], 1)], 1)


def by_plane(table, axis, count):
    planes = NX // count
    order = np.arange(NX).reshape(count, planes).T.reshape(-1)
    return np.take(table, order, axis)


def tables_for(count):
    own = MY // count
    cosine, sine = np_waves(NZ, MZ, True)
    twice = np.where(np.arange(MZ) == 0, 1.0, 2.0)[:, None]
    z_forward = np.concatenate([cosine.T, -sine.T], 1)
    z_inverse = np.concatenate([twice * cosine, -twice * sine], 0)
    y_forward = np_forward(NY, MY).reshape(PAIRS, 2, 2, 2, count, own)
    y_inverse = np_inverse(NY, MY).reshape(count, own, 2, 2, PAIRS, 2)
    four = np.eye(4)
    z_forward = np.einsum("zpk,cd->czpdk", z_forward.reshape(NZ, 2, MZ), four)
    z_inverse = np.einsum("pkz,cd->pckdz", z_inverse.reshape(2, MZ, NZ), four)
    tables = {
        "zf": z_forward.reshape(4 * NZ, 8 * MZ),
        "zi": 0.5 * z_inverse.reshape(8 * MZ, 4 * NZ),
        "yf": y_forward.transpose(3, 5, 4, 1, 2, 0).reshape(2 * MY, 2 * NY),
        "yi": y_inverse.transpose(5, 3, 4, 2, 1, 0).reshape(2 * NY, 2 * MY),
        "xf": by_plane(np_forward(NX, MX).transpose(2, 3, 1, 0), 3, count).reshape(2 * MX, 2 * NX),
        "xi": by_plane(np_inverse(NX, MX).transpose(2, 3, 0, 1), 1, count).reshape(2 * NX, 2 * MX),
    }
    return {name: jnp.asarray(table.astype(np.float32)).astype(BF) for name, table in tables.items()}


def dot32(a, b):
    return jnp.dot(a, b, preferred_element_type=F32)


def gelu_of_half(values):
    u = values.astype(BF)
    scale = math.sqrt(2.0 / math.pi)
    inner = u * (BF(2.0 * scale) + BF(8.0 * scale * 0.044715) * (u * u))
    return u + u * jnp.tanh(inner)


def send_plane(me, count, plane, send, recv, send_sem, recv_sem):
    for shift in range(1, count):
        target = lax.rem(me + shift, count)
        pltpu.make_async_remote_copy(
            src_ref=send.at[plane, target],
            dst_ref=recv.at[plane, me],
            send_sem=send_sem.at[plane],
            recv_sem=recv_sem.at[plane],
            device_id={"space": target},
            device_id_type=pl.DeviceIdType.MESH,
        ).start()
    recv[plane, me] = send[plane, me]


def wait_plane(count, plane, buffer, sem):
    part = buffer.at[plane, pl.ds(0, count - 1)]
    pltpu.make_async_copy(part, part, sem.at[plane]).wait()


def to_modes(plane, count, zf_ref, yf_ref, zs, flat, send):
    tiles = C * MZ // LANES
    slots = 2 * MY // count * tiles
    for pair in range(tiles // 2):
        columns = []
        for group in (pair * 2, pair * 2 + 1):
            halves = []
            for y2 in range(2):
                left = [zs[y2, pl.ds((group * 4 + r) * PITCH, PAIRS), :] for r in range(4)]
                halves.append(dot32(jnp.concatenate(left, 1).astype(BF), zf_ref[...]).astype(BF))
            parts = [half[:, p * LANES : (p + 1) * LANES] for half in halves for p in range(2)]
            columns.append(jnp.concatenate(parts, 0))
        modes = dot32(yf_ref[...], jnp.concatenate(columns, 1))
        for s in range(2 * MY // count):
            for half in range(2):
                flat[pl.ds(s * tiles + pair * 2 + half, count, stride=slots + SKEW), :] = modes[
                    s * count : (s + 1) * count, half * LANES : (half + 1) * LANES
                ]
    for dst in range(count):
        send[plane, dst] = flat[pl.ds(dst * (slots + SKEW), slots), :].astype(BF)


def lay_out(zs, start, values):
    for y2 in range(2):
        for r in range(ROWS):
            zs[y2, pl.ds(start + r, C, stride=PITCH), :] = values[
                r * C : (r + 1) * C, y2 * NZ : (y2 + 1) * NZ
            ]


def hid_rows(index):
    return pl.ds(index * ROWS * C, ROWS * C)


def lift_plane(plane, feat_ref, perm_ref, in_ref, lo_ref, hid, plain, xs, zs):
    for f in range(FIN + 1):
        plain[...] = perm_ref[0, plane] if f == FIN else feat_ref[0, f, plane].astype(F32)
        for y2 in range(2):
            xs[y2, pl.ds(f, PAIRS, stride=8), :] = plain[pl.ds(y2, PAIRS, stride=2), :]
    width = lo_ref.shape[1]
    parts = in_ref.shape[0] // width
    total = PAIRS // ROWS * parts

    def first(n):
        u, r = n // parts, n % parts
        x = jnp.concatenate([xs[y2, pl.ds(u * ROWS * 8, ROWS * 8), :] for y2 in range(2)], 1)
        return dot32(in_ref[r * width : (r + 1) * width, :], x.astype(BF))

    ahead = {n: first(n) for n in range(LOOK)}
    raw = {}

    def finish(n):
        if n % parts == parts - 1:
            u = n // parts
            hidden = jnp.concatenate([raw.pop(u * parts + r) for r in range(parts)], 0)
            hid[plane, hid_rows(u), :] = hidden.astype(BF)
            lay_out(zs, u * ROWS, hidden)

    for n in range(total):
        if n + LOOK < total:
            ahead[n + LOOK] = first(n + LOOK)
        raw[n] = dot32(lo_ref[...], gelu_of_half(ahead.pop(n)))
        if n >= LAG:
            finish(n - LAG)
    for n in range(total - LAG, total):
        finish(n)


def from_modes(plane, count, recv, yi_ref, zi_ref, flat, sp):
    tiles = C * MZ // LANES
    slots = 2 * MY // count * tiles
    for src in range(count):
        flat[pl.ds(src * (slots + SKEW), slots), :] = recv[plane, src].astype(F32)
    for pair in range(tiles // 2):
        rows = []
        for s in range(2 * MY // count):
            part = [
                flat[pl.ds(s * tiles + pair * 2 + half, count, stride=slots + SKEW), :]
                for half in range(2)
            ]
            rows.append(jnp.concatenate(part, 1))
        back = dot32(yi_ref[...], jnp.concatenate(rows, 0).astype(BF)).astype(BF)
        for half in range(2):
            lanes = slice(half * LANES, (half + 1) * LANES)
            for y2 in range(2):
                left = [back[(y2 * 2 + p) * PAIRS : (y2 * 2 + p + 1) * PAIRS, lanes] for p in range(2)]
                field = dot32(jnp.concatenate(left, 1), zi_ref[...])
                for r in range(4):
                    o = (pair * 2 + half) * 4 + r
                    sp[y2, pl.ds(o, PAIRS, stride=C + SKEW), :] = field[:, r * NZ : (r + 1) * NZ]


def field_rows(index, sp):
    halves = []
    for y2 in range(2):
        rows = [sp[y2, pl.ds((index * ROWS + r) * (C + SKEW), C), :] for r in range(ROWS)]
        halves.append(jnp.concatenate(rows, 0))
    return jnp.concatenate(halves, 1)


def middle_plane(plane, kp, hid, sp, zs):
    total = PAIRS // ROWS

    def local_term(index):
        return dot32(kp[...], hid[plane, hid_rows(index), :])

    ahead = {n: local_term(n) for n in range(MID)}
    for n in range(total):
        if n + MID < total:
            ahead[n + MID] = local_term(n + MID)
        hidden = gelu_of_half(ahead.pop(n) + field_rows(n, sp))
        hid[plane, hid_rows(n), :] = hidden
        lay_out(zs, n * ROWS, hidden.astype(F32))


def final_plane(plane, kp, di_ref, do_ref, perm_ref, hid, sp, st_ref, cond_ref):
    total = PAIRS // ROWS
    width = di_ref.shape[1]
    parts = di_ref.shape[0] // width

    def local_term(index):
        return dot32(kp[...], hid[plane, hid_rows(index), :])

    def decode(n):
        hidden = gelu_of_half(ahead.pop(n) + field_rows(n, sp))
        return [dot32(di_ref[r * width : (r + 1) * width, :], hidden) for r in range(parts)]

    ahead = {n: local_term(n) for n in range(MID)}
    raw = {0: decode(0)}
    for n in range(total):
        if n + MID < total:
            ahead[n + MID] = local_term(n + MID)
        if n + 1 < total:
            raw[n + 1] = decode(n + 1)
        both = 0.0
        for r, part in enumerate(raw.pop(n)):
            both = both + dot32(do_ref[:, r * width : (r + 1) * width], gelu_of_half(part))
        for y2 in range(2):
            lanes = slice(y2 * NZ, (y2 + 1) * NZ)
            where = pl.ds(n * ROWS * 2 + y2, ROWS, stride=2)
            st_ref[0, 0, plane, where, :] = both[:ROWS, lanes]
            st_ref[0, 1, plane, where, :] = both[ROWS:, lanes]
    sat = jax.nn.sigmoid(st_ref[0, 1, plane])
    st_ref[0, 1, plane] = sat
    cond_ref[0, plane] = mobility_of(sat, perm_ref[0, plane])


def mix_modes(planes, count, recv, send, wbuf, xf_ref, xi_ref, flat, spec, rows, mixed, turned):
    own = MY // count
    tiles = C * MZ // LANES
    slots = 2 * own * tiles
    pitch = slots + SKEW
    every = count * planes
    lane = lax.broadcasted_iota(jnp.int32, (1, LANES), 1)
    low = lane < 64
    even = lane % 64 < 32

    def unpack(plane, carry):
        for src in range(count):
            start = (plane * count + src) * pitch
            flat[pl.ds(start, slots), :] = recv[plane, src].astype(F32)
        return carry

    lax.fori_loop(0, planes, unpack, 0)

    def column(p, t):
        return flat[pl.ds(p * own * tiles + t, every, stride=pitch), :].astype(BF)

    for pair in range(own * tiles // 2):
        right = jnp.concatenate(
            [
                jnp.concatenate([column(p, pair * 2 + half) for half in range(2)], 1)
                for p in range(2)
            ],
            0,
        )
        total = dot32(xf_ref[...], right)
        for half in range(2):
            part = total[:, half * LANES : (half + 1) * LANES].T
            for r in range(4):
                first = (pair * 2 + half) * 4 + r
                spec[pl.ds(first * (MZ + SKEW), MZ), : 2 * MX] = part[r * MZ : (r + 1) * MZ, :]
    groups = own * MZ // MODE_STEP
    for group in range(groups):
        jj, k = group * MODE_STEP // MZ, group * MODE_STEP % MZ
        base = jj * C * (MZ + SKEW) + k
        picked = [
            spec[pl.ds(base + r, C, stride=MZ + SKEW), : 2 * MX] for r in range(MODE_STEP)
        ]
        rows[group] = jnp.concatenate(picked, 0).T
    wide = MODE_STEP * C
    own_mode = lax.broadcasted_iota(jnp.int32, (MODE_STEP, wide), 0) == (
        lax.broadcasted_iota(jnp.int32, (MODE_STEP, wide), 1) // C
    )
    per = wide // (2 * C)

    def step(group, carry):
        first = pl.multiple_of(group * MODE_STEP, MODE_STEP)
        for piece in range(MX // per):
            left = []
            for i in range(per):
                for q in range(2):
                    row = rows[group, pl.ds(q * MX + piece * per + i, MODE_STEP, stride=0), :]
                    left.append(jnp.where(own_mode, row, 0.0))
            lo = piece * wide
            weights = wbuf[pl.ds(first, MODE_STEP), :, lo : lo + wide].reshape(wide, wide)
            both = dot32(jnp.concatenate(left, 0).astype(BF), weights)

            def part(i, q, t):
                at = (i * 2 + q) * MODE_STEP
                return both[at : at + MODE_STEP, t * LANES : (t + 1) * LANES]

            for t in range(2):
                real, imag = (
                    jnp.where(low, part(2 * t, q, t), part(2 * t + 1, q, t)) for q in range(2)
                )
                turn = jnp.where(even, -pltpu.roll(imag, LANES - C, 1), pltpu.roll(imag, C, 1))
                mixed[pl.ds(first, MODE_STEP), lo + t * LANES : lo + (t + 1) * LANES] = real + turn
        return carry

    lax.fori_loop(0, groups, step, 0)
    for block in range(MX * 2 * C // LANES):
        part = mixed[:, block * LANES : (block + 1) * LANES].T
        for r in range(4):
            first = (block * 4 + r) * (C + SKEW)
            turned[pl.ds(first, C), : own * MZ] = part[r * C : (r + 1) * C, :]
    for pair in range(tiles // 2):
        right = [[], []]
        for half in range(2):
            o = (pair * 2 + half) * 4
            a = [turned[pl.ds(o + r, 2 * MX, stride=C + SKEW), :] for r in range(4)]
            b = jnp.where(low, a[0], pltpu.roll(a[2], 64, 1))
            c = jnp.where(low, a[1], pltpu.roll(a[3], 64, 1))
            right[0].append(jnp.where(even, b, pltpu.roll(c, 32, 1)))
            right[1].append(jnp.where(even, pltpu.roll(b, LANES - 32, 1), c))
        for jj in range(own):
            back = dot32(xi_ref[...], jnp.concatenate(right[jj], 1).astype(BF))
            for p in range(2):
                for half in range(2):
                    slot = (p * own + jj) * tiles + pair * 2 + half
                    flat[pl.ds(slot, every, stride=pitch), :] = back[
                        p * every : (p + 1) * every, half * LANES : (half + 1) * LANES
                    ]

    def pack(plane, carry):
        for dst in range(count):
            start = (plane * count + dst) * pitch
            send[plane, dst] = flat[pl.ds(start, slots), :].astype(BF)
        return carry

    lax.fori_loop(0, planes, pack, 0)


def whole_kernel(
    planes, count, feat_ref, perm_ref, lift_in, lift_out, point, dec_in, dec_out, zf_ref, zi_ref,
    yf_ref, yi_ref, xf_ref, xi_ref, w_hbm, st_ref, cond_ref,
    hid, wbuf, send_f, recv_f, send_b, recv_b, flat, spec, rows, mixed, turned, zs, sp, xs, plain,
    in_ref, lo_ref, kp_ref, di_ref, do_ref, w_sem, sf_sem, rf_sem, sb_sem, rb_sem,
):
    me = lax.axis_index("space")
    barrier = pltpu.get_barrier_semaphore()
    for shift in range(1, count):
        pl.semaphore_signal(
            barrier,
            inc=1,
            device_id={"space": lax.rem(me + shift, count)},
            device_id_type=pl.DeviceIdType.MESH,
        )
    fetch = pltpu.make_async_copy(w_hbm.at[0], wbuf, w_sem.at[0])
    fetch.start()
    xs[...] = jnp.zeros_like(xs)
    in_ref[...] = diag_of(lift_in[...], ROWS, 8, 0.5)
    lo_ref[...] = diag_of(lift_out[...], 2, lift_out.shape[1], 1.0, True)
    for layer in range(LAYERS):
        kp_ref[layer] = diag_of(point[layer], ROWS, C, 0.5)
    di_ref[...] = diag_of(dec_in[...], ROWS, C, 0.5)
    dec = dec_out.shape[1]
    do_ref[...] = spread(
        dec_out[...],
        2 * ROWS,
        ROWS * dec,
        lambda i: i // ROWS,
        lambda j: j % dec,
        lambda i, j: i % ROWS == j // dec,
        1.0,
        True,
    )
    pl.semaphore_wait(barrier, count - 1)

    def over(body):
        def run(plane, carry):
            body(plane)
            return carry

        lax.fori_loop(0, planes, run, 0)

    def lift(plane):
        lift_plane(plane, feat_ref, perm_ref, in_ref, lo_ref, hid, plain, xs, zs)
        to_modes(plane, count, zf_ref, yf_ref, zs, flat, send_f)
        send_plane(me, count, plane, send_f, recv_f, sf_sem, rf_sem)

    over(lift)
    for layer in range(LAYERS):
        fetch.wait()
        over(lambda plane: wait_plane(count, plane, recv_f, rf_sem))
        over(lambda plane: wait_plane(count, plane, send_f, sf_sem))
        mix_modes(
            planes, count, recv_f, send_b, wbuf, xf_ref, xi_ref, flat, spec, rows, mixed, turned
        )
        if layer + 1 < LAYERS:
            fetch = pltpu.make_async_copy(w_hbm.at[layer + 1], wbuf, w_sem.at[layer + 1])
            fetch.start()
        over(lambda plane: send_plane(me, count, plane, send_b, recv_b, sb_sem, rb_sem))
        kp = kp_ref.at[layer]

        def rest(plane):
            wait_plane(count, plane, recv_b, rb_sem)
            from_modes(plane, count, recv_b, yi_ref, zi_ref, flat, sp)
            if layer + 1 < LAYERS:
                middle_plane(plane, kp, hid, sp, zs)
                to_modes(plane, count, zf_ref, yf_ref, zs, flat, send_f)
                send_plane(me, count, plane, send_f, recv_f, sf_sem, rf_sem)
            else:
                final_plane(plane, kp, di_ref, do_ref, perm_ref, hid, sp, st_ref, cond_ref)

        over(rest)
        over(lambda plane: wait_plane(count, plane, send_b, sb_sem))


def ones_where(shape, test, value=1.0):
    row = lax.broadcasted_iota(jnp.int32, shape, 0)
    col = lax.broadcasted_iota(jnp.int32, shape, 1)
    return jnp.where(test(row, col), value, 0.0)


def spread(matrix, rows, cols, row_of, col_of, keep, value, turned):
    depth, height = matrix.shape[::-1] if turned else matrix.shape
    take = ones_where((rows, height), lambda i, j: row_of(i) == j).astype(BF)
    put = ones_where((depth, cols), lambda i, j: col_of(j) == i).astype(BF)
    dims = (((1,), (0 if turned else 1,)), ((), ()))
    part = lax.dot_general(take, matrix, dims, preferred_element_type=F32)
    return (dot32(part.astype(BF), put) * ones_where((rows, cols), keep, value)).astype(BF)


def diag_of(matrix, copies, width, value, turned=False):
    height = matrix.shape[0 if turned else 1]
    return spread(
        matrix,
        copies * height,
        copies * width,
        lambda i: i % height,
        lambda j: j % width,
        lambda i, j: i // height == j // width,
        value,
        turned,
    )


def local_fast(
    features,
    log_perm,
    well_cells,
    well_rates,
    lift_in,
    lift_out,
    spec_weight,
    point_weight,
    dec_in,
    dec_out,
):
    planes = features.shape[2]
    count = lax.axis_size("space")
    own = MY // count
    modes = own * MZ
    slots = 2 * modes * C // LANES
    tables = tables_for(count)
    lift, dec = lift_in.shape[1], dec_in.shape[1]
    operands = (
        features,
        log_perm,
        lift_in,
        lift_out.T,
        point_weight,
        dec_in,
        dec_out.T,
    ) + tuple(tables[name] for name in ("zf", "zi", "yf", "yi", "xf", "xi"))
    vmem = pl.BlockSpec(memory_space=pltpu.VMEM)
    exchange = pltpu.VMEM((planes, count, slots, LANES), BF)
    states, conduct = pl.pallas_call(
        lambda *refs: whole_kernel(planes, count, *refs),
        in_specs=[vmem] * len(operands) + [pl.BlockSpec(memory_space=pl.ANY)],
        out_specs=[vmem, vmem],
        out_shape=[
            jax.ShapeDtypeStruct((1, 2, planes, NY, NZ), F32),
            jax.ShapeDtypeStruct((1, planes, NY, NZ), F32),
        ],
        scratch_shapes=[
            pltpu.VMEM((planes, PAIRS * C, 2 * NZ), BF),
            pltpu.VMEM(spec_weight.shape[1:], BF),
            exchange,
            exchange,
            exchange,
            exchange,
            pltpu.VMEM((planes * count * (slots + SKEW), LANES), F32),
            pltpu.VMEM((own * C * (MZ + SKEW), LANES), F32),
            pltpu.VMEM((modes // MODE_STEP, 2 * MX, MODE_STEP * C), F32),
            pltpu.VMEM((modes, MX * 2 * C), F32),
            pltpu.VMEM((2 * MX * (C + SKEW), LANES), F32),
            pltpu.VMEM((2, C * PITCH, LANES), F32),
            pltpu.VMEM((2, PAIRS * (C + SKEW), LANES), F32),
            pltpu.VMEM((2, PAIRS * 8, NZ), F32),
            pltpu.VMEM((NY, NZ), F32),
            pltpu.VMEM((ROWS * lift, ROWS * 8), BF),
            pltpu.VMEM((2 * C, 2 * lift), BF),
            pltpu.VMEM((LAYERS, ROWS * C, ROWS * C), BF),
            pltpu.VMEM((ROWS * dec, ROWS * C), BF),
            pltpu.VMEM((2 * ROWS, ROWS * dec), BF),
            pltpu.SemaphoreType.DMA((LAYERS,)),
        ]
        + [pltpu.SemaphoreType.DMA((planes,))] * 4,
        compiler_params=pltpu.CompilerParams(
            collective_id=0, has_side_effects=True, vmem_limit_bytes=60 * 1024 * 1024
        ),
        name="whole",
    )(*operands, spec_weight)
    return (states, darcy(states[:, 0], conduct, well_cells, well_rates))


def local(features, log_perm, well_cells, well_rates, lift_in, lift_out, spec_weight, *rest):
    batches, planes = features.shape[0], features.shape[2]
    count = lax.axis_size("space")
    fits = batches == 1 and planes == 8 and count % 8 == 0 and MY == 2 * count
    run = local_fast if fits else local_general
    return run(
        features, log_perm, well_cells, well_rates, lift_in, lift_out, spec_weight, *rest
    )


def solution(mesh):
    return jax.shard_map(
        local,
        mesh=mesh,
        in_specs=(
            P("sample", None, "space", None, None),
            P("sample", "space", None, None),
            P("sample", None),
            P("sample", None),
            P(),
            P(),
            P(None, "space", None, None),
            P(),
            P(),
            P(),
        ),
        out_specs=(P("sample", None, "space", None, None), P("sample", "space", None, None)),
        check_vma=False,
    )
```

```python
import math

import jax
import jax.numpy as jnp
import numpy as np
from jax import lax
from jax.experimental import pallas as pl
from jax.experimental.pallas import tpu as pltpu
from jax.sharding import PartitionSpec as P

NX = 128
NY = 128
NZ = 128
MX = 32
MY = 32
MZ = 32
C = 32
FIN = 4
LAYERS = 2
WELLS = 32


def padded_2(block, sides, width):
    for axis, dim in sides:
        count = lax.axis_size(axis)
        forward = [(i, i + 1) for i in range(count - 1)]
        backward = [(target, source) for source, target in forward]
        low = lax.ppermute(
            lax.slice_in_dim(block, block.shape[dim] - width, None, axis=dim), axis, forward
        )
        high = lax.ppermute(lax.slice_in_dim(block, 0, width, axis=dim), axis, backward)
        block = jnp.concatenate([low, block, high], axis=dim)
    return block


def freq_table(length, kept, one_sided):
    indices = jnp.arange(kept, dtype=jnp.int32)
    if one_sided:
        return indices
    return jnp.where(indices < kept // 2, indices, length - kept + indices)


def wave_parts(length, kept, one_sided):
    freqs = freq_table(length, kept, one_sided)
    places = jnp.arange(length, dtype=jnp.int32)
    phase_turns = freqs[:, None] * places[None, :] % length
    angles = phase_turns.astype(jnp.float32) * (2.0 * math.pi / length)
    norm_scale = 1.0 / math.sqrt(length)
    return (jnp.cos(angles) * norm_scale, jnp.sin(angles) * norm_scale)


def forward_table(length, kept):
    cosine_vals, sine_vals = wave_parts(length, kept, False)
    return jnp.stack(
        [jnp.stack([cosine_vals.T, -sine_vals.T], 1), jnp.stack([sine_vals.T, cosine_vals.T], 1)], 1
    ).astype(jnp.bfloat16)


def inverse_table(length, kept):
    cosine_vals, sine_vals = wave_parts(length, kept, False)
    return jnp.stack(
        [jnp.stack([cosine_vals, sine_vals], 1), jnp.stack([-sine_vals, cosine_vals], 1)], 1
    ).astype(jnp.bfloat16)


def z_tables():
    cosine_vals, sine_vals = wave_parts(NZ, MZ, True)
    weights_k = jnp.where(jnp.arange(MZ) == 0, 1.0, 2.0).astype(jnp.float32)[:, None]
    z_forward = jnp.concatenate([cosine_vals.T, -sine_vals.T], 1).astype(jnp.bfloat16)
    z_inverse = jnp.concatenate([weights_k * cosine_vals, -weights_k * sine_vals], 0).astype(
        jnp.bfloat16
    )
    return (z_forward, z_inverse)


def gelu_tanh(values):
    return jax.nn.gelu(values, approximate=True)


def face_term(cond_a, cond_b, press_a, press_b):
    return 2.0 * cond_a * cond_b / (cond_a + cond_b) * (press_a - press_b)


def mobility_of(saturation, log_values):
    return jnp.exp(log_values) * (
        saturation * saturation + 0.5 * (1.0 - saturation) * (1.0 - saturation)
    )


def darcy(pressure, conduct, well_cells, well_rates):
    batches, planes = pressure.shape[0], pressure.shape[1]
    space_index = lax.axis_index("space")
    pad_cond = jnp.pad(conduct, ((0, 0), (0, 0), (1, 1), (1, 1)))
    pad_press = jnp.pad(pressure, ((0, 0), (0, 0), (1, 1), (1, 1)))
    flux_sum = face_term(conduct, pad_cond[:, :, 2:, 1:-1], pressure, pad_press[:, :, 2:, 1:-1])
    flux_sum = flux_sum + face_term(
        conduct, pad_cond[:, :, :-2, 1:-1], pressure, pad_press[:, :, :-2, 1:-1]
    )
    flux_sum = flux_sum + face_term(
        conduct, pad_cond[:, :, 1:-1, 2:], pressure, pad_press[:, :, 1:-1, 2:]
    )
    flux_sum = flux_sum + face_term(
        conduct, pad_cond[:, :, 1:-1, :-2], pressure, pad_press[:, :, 1:-1, :-2]
    )
    fields = jnp.stack([pressure, conduct], 1)
    padded = padded_2(fields.astype(jnp.bfloat16), (("space", 2),), 1).astype(fields.dtype)
    press_low = padded[:, 0, 0]
    press_high = padded[:, 0, -1]
    cond_low = padded[:, 1, 0]
    cond_high = padded[:, 1, -1]
    press_below = jnp.concatenate([press_low[:, None], pressure[:, :-1]], 1)
    cond_below = jnp.concatenate([cond_low[:, None], conduct[:, :-1]], 1)
    press_above = jnp.concatenate([pressure[:, 1:], press_high[:, None]], 1)
    cond_above = jnp.concatenate([conduct[:, 1:], cond_high[:, None]], 1)
    lower_terms = face_term(conduct, cond_below, pressure, press_below)
    upper_terms = face_term(conduct, cond_above, pressure, press_above)
    flux_sum = flux_sum + lower_terms + upper_terms
    well_x = well_cells // (NY * NZ) - space_index * planes
    well_y = well_cells // NZ % NY
    well_z = well_cells % NZ
    onehot_x = (well_x[:, :, None] == jnp.arange(planes, dtype=jnp.int32)[None, None, :]).astype(
        jnp.float32
    ) * well_rates[:, :, None]
    onehot_y = (well_y[:, :, None] == jnp.arange(NY, dtype=jnp.int32)[None, None, :]).astype(
        jnp.float32
    )
    onehot_z = (well_z[:, :, None] == jnp.arange(NZ, dtype=jnp.int32)[None, None, :]).astype(
        jnp.float32
    )
    plane_rows = (onehot_x[:, :, :, None] * onehot_y[:, :, None, :]).reshape(
        batches, WELLS, planes * NY
    )
    source = jnp.einsum(
        "bwa,bwz->baz", plane_rows, onehot_z, precision=lax.Precision.HIGHEST
    ).reshape(batches, planes, NY, NZ)
    return flux_sum - source


def local_general(
    features,
    log_perm,
    well_cells,
    well_rates,
    lift_in,
    lift_out,
    spec_weight,
    point_weight,
    dec_in,
    dec_out,
):
    batches = features.shape[0]
    planes = features.shape[2]
    space_index = lax.axis_index("space")
    block = spec_weight.shape[1]
    cell_count = planes * NY * NZ
    z_forward, z_inverse = z_tables()
    y_forward = forward_table(NY, MY)
    y_inverse = inverse_table(NY, MY)
    x_forward = forward_table(NX, MX)
    x_inverse = inverse_table(NX, MX)
    perm_b = log_perm.astype(jnp.bfloat16).reshape(batches, 1, cell_count)
    lift_input = jnp.concatenate([features.reshape(batches, FIN, cell_count), perm_b], 1)
    lift_hidden = jnp.einsum("bfn,fh->bhn", lift_input, lift_in, preferred_element_type=jnp.float32)
    lifted = gelu_tanh(lift_hidden).astype(jnp.bfloat16)
    hidden_state = jnp.einsum(
        "bhn,hc->bcn", lifted, lift_out, preferred_element_type=jnp.float32
    ).astype(jnp.bfloat16)
    for layer_idx in range(LAYERS):
        zspec = jnp.dot(hidden_state.reshape(-1, NZ), z_forward, preferred_element_type=jnp.float32)
        zspec = zspec.astype(jnp.bfloat16).reshape(batches * C * planes, NY, 2, MZ)
        yz_spec = jnp.einsum(
            "aypk,ypqj->aqjk", zspec, y_forward, preferred_element_type=jnp.float32
        )
        yz_spec = yz_spec.astype(jnp.bfloat16).reshape(batches, C, planes, 2, MY * MZ)
        mode_weights = spec_weight[layer_idx].reshape(block, C, MX, 2, C)
        spectrum = jnp.einsum(
            "bcxpm,xpqi->bcqim",
            lax.all_to_all(yz_spec, "space", split_axis=4, concat_axis=2, tiled=True),
            x_forward,
            preferred_element_type=jnp.float32,
        ).astype(jnp.bfloat16)
        products = jnp.einsum(
            "bcqim,mcipo->bimqpo", spectrum, mode_weights, preferred_element_type=jnp.float32
        )
        real_part = products[:, :, :, 0, 0] - products[:, :, :, 1, 1]
        imag_part = products[:, :, :, 0, 1] + products[:, :, :, 1, 0]
        mixed_modes = jnp.stack([real_part, imag_part], 3).astype(jnp.bfloat16)
        back_field = jnp.einsum(
            "bimqo,iqpx->boxpm", mixed_modes, x_inverse, preferred_element_type=jnp.float32
        ).astype(jnp.bfloat16)
        returned = lax.all_to_all(back_field, "space", split_axis=2, concat_axis=4, tiled=True)
        returned = returned.reshape(batches * C * planes, 2, MY, MZ)
        y_back = jnp.einsum(
            "aqjk,jqpy->aypk", returned, y_inverse, preferred_element_type=jnp.float32
        ).astype(jnp.bfloat16)
        spectral = jnp.dot(
            y_back.reshape(-1, 2 * MZ), z_inverse, preferred_element_type=jnp.float32
        ).reshape(batches, C, cell_count)
        local_term = jnp.einsum(
            "bcn,co->bon", hidden_state, point_weight[layer_idx], preferred_element_type=jnp.float32
        )
        hidden_state = gelu_tanh(spectral + local_term).astype(jnp.bfloat16)
    decoded = gelu_tanh(
        jnp.einsum("bcn,cd->bdn", hidden_state, dec_in, preferred_element_type=jnp.float32)
    ).astype(jnp.bfloat16)
    decoded_out = jnp.einsum("bdn,de->ben", decoded, dec_out, preferred_element_type=jnp.float32)
    pressure = decoded_out[:, 0].reshape(batches, planes, NY, NZ)
    saturation = jax.nn.sigmoid(decoded_out[:, 1]).reshape(batches, planes, NY, NZ)
    states = jnp.stack([pressure, saturation], 1)
    conduct = mobility_of(saturation, log_perm)
    return (states, darcy(pressure, conduct, well_cells, well_rates))


BF = jnp.bfloat16
F32 = jnp.float32
PAIRS = NY // 2
SKEW = 4
PITCH = PAIRS + SKEW
MODE_STEP = 8
ROWS = 8
LOOK = 4
LAG = 1
MID = 3
TB = 2
FB = 4
LANES = 128


def np_waves(length, kept, one_sided):
    index = np.arange(kept)
    freqs = index if one_sided else np.where(index < kept // 2, index, length - kept + index)
    angles = (freqs[:, None] * np.arange(length)[None, :] % length) * (2.0 * math.pi / length)
    norm = 1.0 / math.sqrt(length)
    return np.cos(angles) * norm, np.sin(angles) * norm


def np_forward(length, kept):
    cosine, sine = np_waves(length, kept, False)
    return np.stack([np.stack([cosine.T, -sine.T], 1), np.stack([sine.T, cosine.T], 1)], 1)


def np_inverse(length, kept):
    cosine, sine = np_waves(length, kept, False)
    return np.stack([np.stack([cosine, sine], 1), np.stack([-sine, cosine], 1)], 1)


def by_plane(table, axis, count):
    planes = NX // count
    order = np.arange(NX).reshape(count, planes).T.reshape(-1)
    return np.take(table, order, axis)


def tables_for(count):
    own = MY // count
    cosine, sine = np_waves(NZ, MZ, True)
    twice = np.where(np.arange(MZ) == 0, 1.0, 2.0)[:, None]
    z_forward = np.concatenate([cosine.T, -sine.T], 1)
    z_inverse = np.concatenate([twice * cosine, -twice * sine], 0)
    y_forward = np_forward(NY, MY).reshape(PAIRS, 2, 2, 2, count, own)
    y_inverse = np_inverse(NY, MY).reshape(count, own, 2, 2, PAIRS, 2)
    four = np.eye(4)
    z_forward = np.einsum("zpk,cd->czpdk", z_forward.reshape(NZ, 2, MZ), four)
    z_inverse = np.einsum("pkz,cd->pckdz", z_inverse.reshape(2, MZ, NZ), four)
    tables = {
        "zf": z_forward.reshape(4 * NZ, 8 * MZ),
        "zi": 0.5 * z_inverse.reshape(8 * MZ, 4 * NZ),
        "yf": y_forward.transpose(3, 5, 4, 1, 2, 0).reshape(2 * MY, 2 * NY),
        "yi": y_inverse.transpose(5, 3, 4, 2, 1, 0).reshape(2 * NY, 2 * MY),
        "xf": by_plane(np_forward(NX, MX).transpose(2, 3, 1, 0), 3, count).reshape(2 * MX, 2 * NX),
        "xi": by_plane(np_inverse(NX, MX).transpose(2, 3, 0, 1), 1, count).reshape(2 * NX, 2 * MX),
    }
    return {name: jnp.asarray(table.astype(np.float32)).astype(BF) for name, table in tables.items()}


def dot32(a, b):
    return jnp.dot(a, b, preferred_element_type=F32)


def gelu_of_half(values):
    u = values.astype(BF)
    scale = math.sqrt(2.0 / math.pi)
    inner = u * (BF(2.0 * scale) + BF(8.0 * scale * 0.044715) * (u * u))
    return u + u * jnp.tanh(inner)


def send_plane(me, count, plane, send, recv, send_sem, recv_sem):
    for shift in range(1, count):
        target = lax.rem(me + shift, count)
        pltpu.make_async_remote_copy(
            src_ref=send.at[plane, target],
            dst_ref=recv.at[plane, me],
            send_sem=send_sem.at[plane],
            recv_sem=recv_sem.at[plane],
            device_id={"space": target},
            device_id_type=pl.DeviceIdType.MESH,
        ).start()
    recv[plane, me] = send[plane, me]


def wait_plane(count, plane, buffer, sem):
    part = buffer.at[plane, pl.ds(0, count - 1)]
    pltpu.make_async_copy(part, part, sem.at[plane]).wait()


def to_modes(plane, count, zf_ref, yf_ref, zs, flat, send):
    tiles = C * MZ // LANES
    slots = 2 * MY // count * tiles
    halves = {}
    for first in range(0, tiles, 2 * TB):
        some = [(group, y2) for group in range(first, first + 2 * TB) for y2 in range(2)]
        left = [
            jnp.concatenate(
                [zs[y2, pl.ds((group * 4 + r) * PITCH, PAIRS), :] for r in range(4)], 1
            ).astype(BF)
            for group, y2 in some
        ]
        waves = dot32(jnp.concatenate(left, 0), zf_ref[...]).astype(BF)
        for n, key in enumerate(some):
            halves[key] = waves[n * PAIRS : (n + 1) * PAIRS, :]
    for pair in range(tiles // 2):
        columns = []
        for group in (pair * 2, pair * 2 + 1):
            parts = [
                halves[group, y2][:, p * LANES : (p + 1) * LANES] for y2 in range(2) for p in range(2)
            ]
            columns.append(jnp.concatenate(parts, 0))
        modes = dot32(yf_ref[...], jnp.concatenate(columns, 1))
        for s in range(2 * MY // count):
            for half in range(2):
                flat[pl.ds(s * tiles + pair * 2 + half, count, stride=slots + SKEW), :] = modes[
                    s * count : (s + 1) * count, half * LANES : (half + 1) * LANES
                ]
    for dst in range(count):
        send[plane, dst] = flat[pl.ds(dst * (slots + SKEW), slots), :].astype(BF)


def lay_out(zs, start, values):
    for y2 in range(2):
        for r in range(ROWS):
            zs[y2, pl.ds(start + r, C, stride=PITCH), :] = values[
                r * C : (r + 1) * C, y2 * NZ : (y2 + 1) * NZ
            ]


def hid_rows(index):
    return pl.ds(index * ROWS * C, ROWS * C)


def lift_plane(plane, feat_ref, perm_ref, in_ref, lo_ref, hid, plain, xs, zs):
    for f in range(FIN + 1):
        plain[...] = perm_ref[0, plane] if f == FIN else feat_ref[0, f, plane].astype(F32)
        for y2 in range(2):
            xs[y2, pl.ds(f, PAIRS, stride=8), :] = plain[pl.ds(y2, PAIRS, stride=2), :]
    width = lo_ref.shape[1]
    parts = in_ref.shape[0] // width
    total = PAIRS // ROWS * parts

    def first(n):
        u, r = n // parts, n % parts
        x = jnp.concatenate([xs[y2, pl.ds(u * ROWS * 8, ROWS * 8), :] for y2 in range(2)], 1)
        return dot32(in_ref[r * width : (r + 1) * width, :], x.astype(BF))

    ahead = {n: first(n) for n in range(LOOK)}
    raw = {}

    def finish(n):
        if n % parts == parts - 1:
            u = n // parts
            hidden = jnp.concatenate([raw.pop(u * parts + r) for r in range(parts)], 0)
            hid[plane, hid_rows(u), :] = hidden.astype(BF)
            lay_out(zs, u * ROWS, hidden)

    for n in range(total):
        if n + LOOK < total:
            ahead[n + LOOK] = first(n + LOOK)
        raw[n] = dot32(lo_ref[...], gelu_of_half(ahead.pop(n)))
        if n >= LAG:
            finish(n - LAG)
    for n in range(total - LAG, total):
        finish(n)


def from_modes(plane, count, recv, yi_ref, zi_ref, flat, sp):
    tiles = C * MZ // LANES
    slots = 2 * MY // count * tiles
    for src in range(count):
        flat[pl.ds(src * (slots + SKEW), slots), :] = recv[plane, src].astype(F32)

    def back_of(pair):
        rows = []
        for s in range(2 * MY // count):
            part = [
                flat[pl.ds(s * tiles + pair * 2 + half, count, stride=slots + SKEW), :]
                for half in range(2)
            ]
            rows.append(jnp.concatenate(part, 1))
        return dot32(yi_ref[...], jnp.concatenate(rows, 0).astype(BF)).astype(BF)

    for first in range(0, tiles // 2, FB):
        left, some = [], []
        for pair in range(first, first + FB):
            back = back_of(pair)
            for half in range(2):
                lanes = slice(half * LANES, (half + 1) * LANES)
                for y2 in range(2):
                    parts = [
                        back[(y2 * 2 + p) * PAIRS : (y2 * 2 + p + 1) * PAIRS, lanes] for p in range(2)
                    ]
                    left.append(jnp.concatenate(parts, 1))
                    some.append(((pair * 2 + half) * 4, y2))
        field = dot32(jnp.concatenate(left, 0), zi_ref[...])
        for n, (o, y2) in enumerate(some):
            for r in range(4):
                sp[y2, pl.ds(o + r, PAIRS, stride=C + SKEW), :] = field[
                    n * PAIRS : (n + 1) * PAIRS, r * NZ : (r + 1) * NZ
                ]


def field_rows(index, sp):
    halves = []
    for y2 in range(2):
        rows = [sp[y2, pl.ds((index * ROWS + r) * (C + SKEW), C), :] for r in range(ROWS)]
        halves.append(jnp.concatenate(rows, 0))
    return jnp.concatenate(halves, 1)


def middle_plane(plane, kp, hid, sp, zs):
    total = PAIRS // ROWS

    def local_term(index):
        return dot32(kp[...], hid[plane, hid_rows(index), :])

    ahead = {n: local_term(n) for n in range(MID)}
    for n in range(total):
        if n + MID < total:
            ahead[n + MID] = local_term(n + MID)
        hidden = gelu_of_half(ahead.pop(n) + field_rows(n, sp))
        hid[plane, hid_rows(n), :] = hidden
        lay_out(zs, n * ROWS, hidden.astype(F32))


def final_plane(plane, kp, di_ref, do_ref, perm_ref, hid, sp, st_ref, cond_ref):
    total = PAIRS // ROWS
    width = di_ref.shape[1]
    parts = di_ref.shape[0] // width

    def local_term(index):
        return dot32(kp[...], hid[plane, hid_rows(index), :])

    def mixed(n):
        return gelu_of_half(ahead.pop(n) + field_rows(n, sp))

    def decode(hidden, r):
        return dot32(di_ref[r * width : (r + 1) * width, :], hidden)

    def shrink(n, r):
        return dot32(do_ref[:, r * width : (r + 1) * width], gelu_of_half(raw.pop((n, r))))

    ahead = {n: local_term(n) for n in range(MID)}
    raw = {}
    hiddens = {0: mixed(0)}
    for r in range(parts):
        raw[0, r] = decode(hiddens[0], r)
    hiddens[1] = mixed(1)
    for n in range(total):
        if n + MID < total:
            ahead[n + MID] = local_term(n + MID)
        both = 0.0
        for r in range(parts):
            if n + 1 < total:
                raw[n + 1, r] = decode(hiddens[n + 1], r)
            both = both + shrink(n, r)
            if r == 0 and n + 2 < total:
                hiddens[n + 2] = mixed(n + 2)
        for y2 in range(2):
            lanes = slice(y2 * NZ, (y2 + 1) * NZ)
            where = pl.ds(n * ROWS * 2 + y2, ROWS, stride=2)
            st_ref[0, 0, plane, where, :] = both[:ROWS, lanes]
            st_ref[0, 1, plane, where, :] = both[ROWS:, lanes]
    sat = jax.nn.sigmoid(st_ref[0, 1, plane])
    st_ref[0, 1, plane] = sat
    cond_ref[0, plane] = mobility_of(sat, perm_ref[0, plane])


def mix_modes(planes, count, recv, send, wbuf, xf_ref, xi_ref, flat, spec, rows, mixed, turned):
    own = MY // count
    tiles = C * MZ // LANES
    slots = 2 * own * tiles
    pitch = slots + SKEW
    every = count * planes
    lane = lax.broadcasted_iota(jnp.int32, (1, LANES), 1)
    low = lane < 64
    even = lane % 64 < 32

    def unpack(plane, carry):
        for src in range(count):
            start = (plane * count + src) * pitch
            flat[pl.ds(start, slots), :] = recv[plane, src].astype(F32)
        return carry

    lax.fori_loop(0, planes, unpack, 0)

    def column(p, t):
        return flat[pl.ds(p * own * tiles + t, every, stride=pitch), :].astype(BF)

    for pair in range(own * tiles // 2):
        right = jnp.concatenate(
            [
                jnp.concatenate([column(p, pair * 2 + half) for half in range(2)], 1)
                for p in range(2)
            ],
            0,
        )
        total = dot32(xf_ref[...], right)
        for half in range(2):
            part = total[:, half * LANES : (half + 1) * LANES].T
            for r in range(4):
                first = (pair * 2 + half) * 4 + r
                spec[pl.ds(first * (MZ + SKEW), MZ), : 2 * MX] = part[r * MZ : (r + 1) * MZ, :]
    groups = own * MZ // MODE_STEP
    for group in range(groups):
        jj, k = group * MODE_STEP // MZ, group * MODE_STEP % MZ
        base = jj * C * (MZ + SKEW) + k
        picked = [
            spec[pl.ds(base + r, C, stride=MZ + SKEW), : 2 * MX] for r in range(MODE_STEP)
        ]
        rows[group] = jnp.concatenate(picked, 0).T
    wide = MODE_STEP * C
    own_mode = lax.broadcasted_iota(jnp.int32, (MODE_STEP, wide), 0) == (
        lax.broadcasted_iota(jnp.int32, (MODE_STEP, wide), 1) // C
    )
    per = wide // (2 * C)

    def step(group, carry):
        first = pl.multiple_of(group * MODE_STEP, MODE_STEP)
        for piece in range(MX // per):
            left = []
            for i in range(per):
                for q in range(2):
                    row = rows[group, pl.ds(q * MX + piece * per + i, MODE_STEP, stride=0), :]
                    left.append(jnp.where(own_mode, row, 0.0))
            lo = piece * wide
            weights = wbuf[pl.ds(first, MODE_STEP), :, lo : lo + wide].reshape(wide, wide)
            both = dot32(jnp.concatenate(left, 0).astype(BF), weights)

            def part(i, q, t):
                at = (i * 2 + q) * MODE_STEP
                return both[at : at + MODE_STEP, t * LANES : (t + 1) * LANES]

            for t in range(2):
                real, imag = (
                    jnp.where(low, part(2 * t, q, t), part(2 * t + 1, q, t)) for q in range(2)
                )
                turn = jnp.where(even, -pltpu.roll(imag, LANES - C, 1), pltpu.roll(imag, C, 1))
                mixed[pl.ds(first, MODE_STEP), lo + t * LANES : lo + (t + 1) * LANES] = real + turn
        return carry

    lax.fori_loop(0, groups, step, 0)
    for block in range(MX * 2 * C // LANES):
        part = mixed[:, block * LANES : (block + 1) * LANES].T
        for r in range(4):
            first = (block * 4 + r) * (C + SKEW)
            turned[pl.ds(first, C), : own * MZ] = part[r * C : (r + 1) * C, :]
    for pair in range(tiles // 2):
        right = [[], []]
        for half in range(2):
            o = (pair * 2 + half) * 4
            a = [turned[pl.ds(o + r, 2 * MX, stride=C + SKEW), :] for r in range(4)]
            b = jnp.where(low, a[0], pltpu.roll(a[2], 64, 1))
            c = jnp.where(low, a[1], pltpu.roll(a[3], 64, 1))
            right[0].append(jnp.where(even, b, pltpu.roll(c, 32, 1)))
            right[1].append(jnp.where(even, pltpu.roll(b, LANES - 32, 1), c))
        for jj in range(own):
            back = dot32(xi_ref[...], jnp.concatenate(right[jj], 1).astype(BF))
            for p in range(2):
                for half in range(2):
                    slot = (p * own + jj) * tiles + pair * 2 + half
                    flat[pl.ds(slot, every, stride=pitch), :] = back[
                        p * every : (p + 1) * every, half * LANES : (half + 1) * LANES
                    ]

    def pack(plane, carry):
        for dst in range(count):
            start = (plane * count + dst) * pitch
            send[plane, dst] = flat[pl.ds(start, slots), :].astype(BF)
        return carry

    lax.fori_loop(0, planes, pack, 0)


def whole_kernel(
    planes, count, feat_ref, perm_ref, lift_in, lift_out, point, dec_in, dec_out, zf_ref, zi_ref,
    yf_ref, yi_ref, xf_ref, xi_ref, w_hbm, st_ref, cond_ref,
    hid, wbuf, send_f, recv_f, send_b, recv_b, flat, spec, rows, mixed, turned, zs, sp, xs, plain,
    in_ref, lo_ref, kp_ref, di_ref, do_ref, w_sem, sf_sem, rf_sem, sb_sem, rb_sem,
):
    me = lax.axis_index("space")
    barrier = pltpu.get_barrier_semaphore()
    for shift in range(1, count):
        pl.semaphore_signal(
            barrier,
            inc=1,
            device_id={"space": lax.rem(me + shift, count)},
            device_id_type=pl.DeviceIdType.MESH,
        )
    fetch = pltpu.make_async_copy(w_hbm.at[0], wbuf, w_sem.at[0])
    fetch.start()
    xs[...] = jnp.zeros_like(xs)
    in_ref[...] = diag_of(lift_in[...], ROWS, 8, 0.5)
    lo_ref[...] = diag_of(lift_out[...], 2, lift_out.shape[1], 1.0, True)
    for layer in range(LAYERS):
        kp_ref[layer] = diag_of(point[layer], ROWS, C, 0.5)
    di_ref[...] = diag_of(dec_in[...], ROWS, C, 0.5)
    dec = dec_out.shape[1]
    do_ref[...] = spread(
        dec_out[...],
        2 * ROWS,
        ROWS * dec,
        lambda i: i // ROWS,
        lambda j: j % dec,
        lambda i, j: i % ROWS == j // dec,
        1.0,
        True,
    )
    pl.semaphore_wait(barrier, count - 1)

    def over(body):
        def run(plane, carry):
            body(plane)
            return carry

        lax.fori_loop(0, planes, run, 0)

    def lift(plane):
        lift_plane(plane, feat_ref, perm_ref, in_ref, lo_ref, hid, plain, xs, zs)
        to_modes(plane, count, zf_ref, yf_ref, zs, flat, send_f)
        send_plane(me, count, plane, send_f, recv_f, sf_sem, rf_sem)

    over(lift)
    for layer in range(LAYERS):
        fetch.wait()
        over(lambda plane: wait_plane(count, plane, recv_f, rf_sem))
        over(lambda plane: wait_plane(count, plane, send_f, sf_sem))
        mix_modes(
            planes, count, recv_f, send_b, wbuf, xf_ref, xi_ref, flat, spec, rows, mixed, turned
        )
        if layer + 1 < LAYERS:
            fetch = pltpu.make_async_copy(w_hbm.at[layer + 1], wbuf, w_sem.at[layer + 1])
            fetch.start()
        over(lambda plane: send_plane(me, count, plane, send_b, recv_b, sb_sem, rb_sem))
        kp = kp_ref.at[layer]

        def rest(plane):
            wait_plane(count, plane, recv_b, rb_sem)
            from_modes(plane, count, recv_b, yi_ref, zi_ref, flat, sp)
            if layer + 1 < LAYERS:
                middle_plane(plane, kp, hid, sp, zs)
                to_modes(plane, count, zf_ref, yf_ref, zs, flat, send_f)
                send_plane(me, count, plane, send_f, recv_f, sf_sem, rf_sem)
            else:
                final_plane(plane, kp, di_ref, do_ref, perm_ref, hid, sp, st_ref, cond_ref)

        over(rest)
        over(lambda plane: wait_plane(count, plane, send_b, sb_sem))


def ones_where(shape, test, value=1.0):
    row = lax.broadcasted_iota(jnp.int32, shape, 0)
    col = lax.broadcasted_iota(jnp.int32, shape, 1)
    return jnp.where(test(row, col), value, 0.0)


def spread(matrix, rows, cols, row_of, col_of, keep, value, turned):
    depth, height = matrix.shape[::-1] if turned else matrix.shape
    take = ones_where((rows, height), lambda i, j: row_of(i) == j).astype(BF)
    put = ones_where((depth, cols), lambda i, j: col_of(j) == i).astype(BF)
    dims = (((1,), (0 if turned else 1,)), ((), ()))
    part = lax.dot_general(take, matrix, dims, preferred_element_type=F32)
    return (dot32(part.astype(BF), put) * ones_where((rows, cols), keep, value)).astype(BF)


def diag_of(matrix, copies, width, value, turned=False):
    height = matrix.shape[0 if turned else 1]
    return spread(
        matrix,
        copies * height,
        copies * width,
        lambda i: i % height,
        lambda j: j % width,
        lambda i, j: i // height == j // width,
        value,
        turned,
    )


def local_fast(
    features,
    log_perm,
    well_cells,
    well_rates,
    lift_in,
    lift_out,
    spec_weight,
    point_weight,
    dec_in,
    dec_out,
):
    planes = features.shape[2]
    count = lax.axis_size("space")
    own = MY // count
    modes = own * MZ
    slots = 2 * modes * C // LANES
    tables = tables_for(count)
    lift, dec = lift_in.shape[1], dec_in.shape[1]
    operands = (
        features,
        log_perm,
        lift_in,
        lift_out.T,
        point_weight,
        dec_in,
        dec_out.T,
    ) + tuple(tables[name] for name in ("zf", "zi", "yf", "yi", "xf", "xi"))
    vmem = pl.BlockSpec(memory_space=pltpu.VMEM)
    exchange = pltpu.VMEM((planes, count, slots, LANES), BF)
    states, conduct = pl.pallas_call(
        lambda *refs: whole_kernel(planes, count, *refs),
        in_specs=[vmem] * len(operands) + [pl.BlockSpec(memory_space=pl.ANY)],
        out_specs=[vmem, vmem],
        out_shape=[
            jax.ShapeDtypeStruct((1, 2, planes, NY, NZ), F32),
            jax.ShapeDtypeStruct((1, planes, NY, NZ), F32),
        ],
        scratch_shapes=[
            pltpu.VMEM((planes, PAIRS * C, 2 * NZ), BF),
            pltpu.VMEM(spec_weight.shape[1:], BF),
            exchange,
            exchange,
            exchange,
            exchange,
            pltpu.VMEM((planes * count * (slots + SKEW), LANES), F32),
            pltpu.VMEM((own * C * (MZ + SKEW), LANES), F32),
            pltpu.VMEM((modes // MODE_STEP, 2 * MX, MODE_STEP * C), F32),
            pltpu.VMEM((modes, MX * 2 * C), F32),
            pltpu.VMEM((2 * MX * (C + SKEW), LANES), F32),
            pltpu.VMEM((2, C * PITCH, LANES), F32),
            pltpu.VMEM((2, PAIRS * (C + SKEW), LANES), F32),
            pltpu.VMEM((2, PAIRS * 8, NZ), F32),
            pltpu.VMEM((NY, NZ), F32),
            pltpu.VMEM((ROWS * lift, ROWS * 8), BF),
            pltpu.VMEM((2 * C, 2 * lift), BF),
            pltpu.VMEM((LAYERS, ROWS * C, ROWS * C), BF),
            pltpu.VMEM((ROWS * dec, ROWS * C), BF),
            pltpu.VMEM((2 * ROWS, ROWS * dec), BF),
            pltpu.SemaphoreType.DMA((LAYERS,)),
        ]
        + [pltpu.SemaphoreType.DMA((planes,))] * 4,
        compiler_params=pltpu.CompilerParams(
            collective_id=0, has_side_effects=True, vmem_limit_bytes=60 * 1024 * 1024
        ),
        name="whole",
    )(*operands, spec_weight)
    return (states, darcy(states[:, 0], conduct, well_cells, well_rates))


def local(features, log_perm, well_cells, well_rates, lift_in, lift_out, spec_weight, *rest):
    batches, planes = features.shape[0], features.shape[2]
    count = lax.axis_size("space")
    fits = batches == 1 and planes == 8 and count % 8 == 0 and MY == 2 * count
    run = local_fast if fits else local_general
    return run(
        features, log_perm, well_cells, well_rates, lift_in, lift_out, spec_weight, *rest
    )


def solution(mesh):
    return jax.shard_map(
        local,
        mesh=mesh,
        in_specs=(
            P("sample", None, "space", None, None),
            P("sample", "space", None, None),
            P("sample", None),
            P("sample", None),
            P(),
            P(),
            P(None, "space", None, None),
            P(),
            P(),
            P(),
        ),
        out_specs=(P("sample", None, "space", None, None), P("sample", "space", None, None)),
        check_vma=False,
    )
```

```python
import math

import jax
import jax.numpy as jnp
import numpy as np
from jax import lax
from jax.experimental import pallas as pl
from jax.experimental.pallas import tpu as pltpu
from jax.sharding import PartitionSpec as P

NX = 128
NY = 128
NZ = 128
MX = 32
MY = 32
MZ = 32
C = 32
FIN = 4
LAYERS = 2
WELLS = 32


def padded_2(block, sides, width):
    for axis, dim in sides:
        count = lax.axis_size(axis)
        forward = [(i, i + 1) for i in range(count - 1)]
        backward = [(target, source) for source, target in forward]
        low = lax.ppermute(
            lax.slice_in_dim(block, block.shape[dim] - width, None, axis=dim), axis, forward
        )
        high = lax.ppermute(lax.slice_in_dim(block, 0, width, axis=dim), axis, backward)
        block = jnp.concatenate([low, block, high], axis=dim)
    return block


def freq_table(length, kept, one_sided):
    indices = jnp.arange(kept, dtype=jnp.int32)
    if one_sided:
        return indices
    return jnp.where(indices < kept // 2, indices, length - kept + indices)


def wave_parts(length, kept, one_sided):
    freqs = freq_table(length, kept, one_sided)
    places = jnp.arange(length, dtype=jnp.int32)
    phase_turns = freqs[:, None] * places[None, :] % length
    angles = phase_turns.astype(jnp.float32) * (2.0 * math.pi / length)
    norm_scale = 1.0 / math.sqrt(length)
    return (jnp.cos(angles) * norm_scale, jnp.sin(angles) * norm_scale)


def forward_table(length, kept):
    cosine_vals, sine_vals = wave_parts(length, kept, False)
    return jnp.stack(
        [jnp.stack([cosine_vals.T, -sine_vals.T], 1), jnp.stack([sine_vals.T, cosine_vals.T], 1)], 1
    ).astype(jnp.bfloat16)


def inverse_table(length, kept):
    cosine_vals, sine_vals = wave_parts(length, kept, False)
    return jnp.stack(
        [jnp.stack([cosine_vals, sine_vals], 1), jnp.stack([-sine_vals, cosine_vals], 1)], 1
    ).astype(jnp.bfloat16)


def z_tables():
    cosine_vals, sine_vals = wave_parts(NZ, MZ, True)
    weights_k = jnp.where(jnp.arange(MZ) == 0, 1.0, 2.0).astype(jnp.float32)[:, None]
    z_forward = jnp.concatenate([cosine_vals.T, -sine_vals.T], 1).astype(jnp.bfloat16)
    z_inverse = jnp.concatenate([weights_k * cosine_vals, -weights_k * sine_vals], 0).astype(
        jnp.bfloat16
    )
    return (z_forward, z_inverse)


def gelu_tanh(values):
    return jax.nn.gelu(values, approximate=True)


def face_term(cond_a, cond_b, press_a, press_b):
    return 2.0 * cond_a * cond_b / (cond_a + cond_b) * (press_a - press_b)


def mobility_of(saturation, log_values):
    return jnp.exp(log_values) * (
        saturation * saturation + 0.5 * (1.0 - saturation) * (1.0 - saturation)
    )


def darcy(pressure, conduct, well_cells, well_rates):
    batches, planes = pressure.shape[0], pressure.shape[1]
    space_index = lax.axis_index("space")
    pad_cond = jnp.pad(conduct, ((0, 0), (0, 0), (1, 1), (1, 1)))
    pad_press = jnp.pad(pressure, ((0, 0), (0, 0), (1, 1), (1, 1)))
    flux_sum = face_term(conduct, pad_cond[:, :, 2:, 1:-1], pressure, pad_press[:, :, 2:, 1:-1])
    flux_sum = flux_sum + face_term(
        conduct, pad_cond[:, :, :-2, 1:-1], pressure, pad_press[:, :, :-2, 1:-1]
    )
    flux_sum = flux_sum + face_term(
        conduct, pad_cond[:, :, 1:-1, 2:], pressure, pad_press[:, :, 1:-1, 2:]
    )
    flux_sum = flux_sum + face_term(
        conduct, pad_cond[:, :, 1:-1, :-2], pressure, pad_press[:, :, 1:-1, :-2]
    )
    fields = jnp.stack([pressure, conduct], 1)
    padded = padded_2(fields.astype(jnp.bfloat16), (("space", 2),), 1).astype(fields.dtype)
    press_low = padded[:, 0, 0]
    press_high = padded[:, 0, -1]
    cond_low = padded[:, 1, 0]
    cond_high = padded[:, 1, -1]
    press_below = jnp.concatenate([press_low[:, None], pressure[:, :-1]], 1)
    cond_below = jnp.concatenate([cond_low[:, None], conduct[:, :-1]], 1)
    press_above = jnp.concatenate([pressure[:, 1:], press_high[:, None]], 1)
    cond_above = jnp.concatenate([conduct[:, 1:], cond_high[:, None]], 1)
    lower_terms = face_term(conduct, cond_below, pressure, press_below)
    upper_terms = face_term(conduct, cond_above, pressure, press_above)
    flux_sum = flux_sum + lower_terms + upper_terms
    well_x = well_cells // (NY * NZ) - space_index * planes
    well_y = well_cells // NZ % NY
    well_z = well_cells % NZ
    onehot_x = (well_x[:, :, None] == jnp.arange(planes, dtype=jnp.int32)[None, None, :]).astype(
        jnp.float32
    ) * well_rates[:, :, None]
    onehot_y = (well_y[:, :, None] == jnp.arange(NY, dtype=jnp.int32)[None, None, :]).astype(
        jnp.float32
    )
    onehot_z = (well_z[:, :, None] == jnp.arange(NZ, dtype=jnp.int32)[None, None, :]).astype(
        jnp.float32
    )
    plane_rows = (onehot_x[:, :, :, None] * onehot_y[:, :, None, :]).reshape(
        batches, WELLS, planes * NY
    )
    source = jnp.einsum(
        "bwa,bwz->baz", plane_rows, onehot_z, precision=lax.Precision.HIGHEST
    ).reshape(batches, planes, NY, NZ)
    return flux_sum - source


def local_general(
    features,
    log_perm,
    well_cells,
    well_rates,
    lift_in,
    lift_out,
    spec_weight,
    point_weight,
    dec_in,
    dec_out,
):
    batches = features.shape[0]
    planes = features.shape[2]
    space_index = lax.axis_index("space")
    block = spec_weight.shape[1]
    cell_count = planes * NY * NZ
    z_forward, z_inverse = z_tables()
    y_forward = forward_table(NY, MY)
    y_inverse = inverse_table(NY, MY)
    x_forward = forward_table(NX, MX)
    x_inverse = inverse_table(NX, MX)
    perm_b = log_perm.astype(jnp.bfloat16).reshape(batches, 1, cell_count)
    lift_input = jnp.concatenate([features.reshape(batches, FIN, cell_count), perm_b], 1)
    lift_hidden = jnp.einsum("bfn,fh->bhn", lift_input, lift_in, preferred_element_type=jnp.float32)
    lifted = gelu_tanh(lift_hidden).astype(jnp.bfloat16)
    hidden_state = jnp.einsum(
        "bhn,hc->bcn", lifted, lift_out, preferred_element_type=jnp.float32
    ).astype(jnp.bfloat16)
    for layer_idx in range(LAYERS):
        zspec = jnp.dot(hidden_state.reshape(-1, NZ), z_forward, preferred_element_type=jnp.float32)
        zspec = zspec.astype(jnp.bfloat16).reshape(batches * C * planes, NY, 2, MZ)
        yz_spec = jnp.einsum(
            "aypk,ypqj->aqjk", zspec, y_forward, preferred_element_type=jnp.float32
        )
        yz_spec = yz_spec.astype(jnp.bfloat16).reshape(batches, C, planes, 2, MY * MZ)
        mode_weights = spec_weight[layer_idx].reshape(block, C, MX, 2, C)
        spectrum = jnp.einsum(
            "bcxpm,xpqi->bcqim",
            lax.all_to_all(yz_spec, "space", split_axis=4, concat_axis=2, tiled=True),
            x_forward,
            preferred_element_type=jnp.float32,
        ).astype(jnp.bfloat16)
        products = jnp.einsum(
            "bcqim,mcipo->bimqpo", spectrum, mode_weights, preferred_element_type=jnp.float32
        )
        real_part = products[:, :, :, 0, 0] - products[:, :, :, 1, 1]
        imag_part = products[:, :, :, 0, 1] + products[:, :, :, 1, 0]
        mixed_modes = jnp.stack([real_part, imag_part], 3).astype(jnp.bfloat16)
        back_field = jnp.einsum(
            "bimqo,iqpx->boxpm", mixed_modes, x_inverse, preferred_element_type=jnp.float32
        ).astype(jnp.bfloat16)
        returned = lax.all_to_all(back_field, "space", split_axis=2, concat_axis=4, tiled=True)
        returned = returned.reshape(batches * C * planes, 2, MY, MZ)
        y_back = jnp.einsum(
            "aqjk,jqpy->aypk", returned, y_inverse, preferred_element_type=jnp.float32
        ).astype(jnp.bfloat16)
        spectral = jnp.dot(
            y_back.reshape(-1, 2 * MZ), z_inverse, preferred_element_type=jnp.float32
        ).reshape(batches, C, cell_count)
        local_term = jnp.einsum(
            "bcn,co->bon", hidden_state, point_weight[layer_idx], preferred_element_type=jnp.float32
        )
        hidden_state = gelu_tanh(spectral + local_term).astype(jnp.bfloat16)
    decoded = gelu_tanh(
        jnp.einsum("bcn,cd->bdn", hidden_state, dec_in, preferred_element_type=jnp.float32)
    ).astype(jnp.bfloat16)
    decoded_out = jnp.einsum("bdn,de->ben", decoded, dec_out, preferred_element_type=jnp.float32)
    pressure = decoded_out[:, 0].reshape(batches, planes, NY, NZ)
    saturation = jax.nn.sigmoid(decoded_out[:, 1]).reshape(batches, planes, NY, NZ)
    states = jnp.stack([pressure, saturation], 1)
    conduct = mobility_of(saturation, log_perm)
    return (states, darcy(pressure, conduct, well_cells, well_rates))


BF = jnp.bfloat16
F32 = jnp.float32
PAIRS = NY // 2
SKEW = 4
PITCH = PAIRS + SKEW
MODE_STEP = 8
ROWS = 8
LOOK = 4
LAG = 1
MID = 3
TB = 2
FB = 4
LANES = 128


def np_waves(length, kept, one_sided):
    index = np.arange(kept)
    freqs = index if one_sided else np.where(index < kept // 2, index, length - kept + index)
    angles = (freqs[:, None] * np.arange(length)[None, :] % length) * (2.0 * math.pi / length)
    norm = 1.0 / math.sqrt(length)
    return np.cos(angles) * norm, np.sin(angles) * norm


def np_forward(length, kept):
    cosine, sine = np_waves(length, kept, False)
    return np.stack([np.stack([cosine.T, -sine.T], 1), np.stack([sine.T, cosine.T], 1)], 1)


def np_inverse(length, kept):
    cosine, sine = np_waves(length, kept, False)
    return np.stack([np.stack([cosine, sine], 1), np.stack([-sine, cosine], 1)], 1)


def by_plane(table, axis, count):
    planes = NX // count
    order = np.arange(NX).reshape(count, planes).T.reshape(-1)
    return np.take(table, order, axis)


def tables_for(count):
    own = MY // count
    cosine, sine = np_waves(NZ, MZ, True)
    twice = np.where(np.arange(MZ) == 0, 1.0, 2.0)[:, None]
    z_forward = np.concatenate([cosine.T, -sine.T], 1)
    z_inverse = np.concatenate([twice * cosine, -twice * sine], 0)
    y_forward = np_forward(NY, MY).reshape(PAIRS, 2, 2, 2, count, own)
    y_inverse = np_inverse(NY, MY).reshape(count, own, 2, 2, PAIRS, 2)
    four = np.eye(4)
    z_forward = np.einsum("zpk,cd->czpdk", z_forward.reshape(NZ, 2, MZ), four)
    z_inverse = np.einsum("pkz,cd->pckdz", z_inverse.reshape(2, MZ, NZ), four)
    tables = {
        "zf": z_forward.reshape(4 * NZ, 8 * MZ),
        "zi": 0.5 * z_inverse.reshape(8 * MZ, 4 * NZ),
        "yf": y_forward.transpose(3, 5, 4, 1, 2, 0).reshape(2 * MY, 2 * NY),
        "yi": y_inverse.transpose(5, 3, 4, 2, 1, 0).reshape(2 * NY, 2 * MY),
        "xf": by_plane(np_forward(NX, MX).transpose(2, 3, 1, 0), 3, count).reshape(2 * MX, 2 * NX),
        "xi": by_plane(np_inverse(NX, MX).transpose(2, 3, 0, 1), 1, count).reshape(2 * NX, 2 * MX),
    }
    return {name: jnp.asarray(table.astype(np.float32)).astype(BF) for name, table in tables.items()}


def dot32(a, b):
    return jnp.dot(a, b, preferred_element_type=F32)


def gelu_of_half(values):
    u = values.astype(BF)
    scale = math.sqrt(2.0 / math.pi)
    inner = u * (BF(2.0 * scale) + BF(8.0 * scale * 0.044715) * (u * u))
    return u + u * jnp.tanh(inner)


def send_plane(me, count, plane, send, recv, send_sem, recv_sem):
    for shift in range(1, count):
        target = lax.rem(me + shift, count)
        pltpu.make_async_remote_copy(
            src_ref=send.at[plane, target],
            dst_ref=recv.at[plane, me],
            send_sem=send_sem.at[plane],
            recv_sem=recv_sem.at[plane],
            device_id={"space": target},
            device_id_type=pl.DeviceIdType.MESH,
        ).start()
    recv[plane, me] = send[plane, me]


def wait_plane(count, plane, buffer, sem):
    part = buffer.at[plane, pl.ds(0, count - 1)]
    pltpu.make_async_copy(part, part, sem.at[plane]).wait()


def to_modes(plane, count, zf_ref, yf_ref, zs, flat, send):
    tiles = C * MZ // LANES
    slots = 2 * MY // count * tiles
    halves = {}
    for first in range(0, tiles, 2 * TB):
        some = [(group, y2) for group in range(first, first + 2 * TB) for y2 in range(2)]
        left = [
            jnp.concatenate(
                [zs[y2, pl.ds((group * 4 + r) * PITCH, PAIRS), :] for r in range(4)], 1
            ).astype(BF)
            for group, y2 in some
        ]
        waves = dot32(jnp.concatenate(left, 0), zf_ref[...]).astype(BF)
        for n, key in enumerate(some):
            halves[key] = waves[n * PAIRS : (n + 1) * PAIRS, :]
    for pair in range(tiles // 2):
        columns = []
        for group in (pair * 2, pair * 2 + 1):
            parts = [
                halves[group, y2][:, p * LANES : (p + 1) * LANES] for y2 in range(2) for p in range(2)
            ]
            columns.append(jnp.concatenate(parts, 0))
        modes = dot32(yf_ref[...], jnp.concatenate(columns, 1))
        for s in range(2 * MY // count):
            for half in range(2):
                flat[pl.ds(s * tiles + pair * 2 + half, count, stride=slots + SKEW), :] = modes[
                    s * count : (s + 1) * count, half * LANES : (half + 1) * LANES
                ]
    for dst in range(count):
        send[plane, dst] = flat[pl.ds(dst * (slots + SKEW), slots), :].astype(BF)


def lay_out(zs, start, values):
    for y2 in range(2):
        for r in range(ROWS):
            zs[y2, pl.ds(start + r, C, stride=PITCH), :] = values[
                r * C : (r + 1) * C, y2 * NZ : (y2 + 1) * NZ
            ]


def hid_rows(index):
    return pl.ds(index * ROWS * C, ROWS * C)


def lift_plane(plane, feat_ref, perm_ref, in_ref, lo_ref, hid, plain, xs, zs):
    for f in range(FIN + 1):
        plain[...] = perm_ref[0, plane] if f == FIN else feat_ref[0, f, plane].astype(F32)
        for y2 in range(2):
            xs[y2, pl.ds(f, PAIRS, stride=8), :] = plain[pl.ds(y2, PAIRS, stride=2), :]
    width = lo_ref.shape[1]
    parts = in_ref.shape[0] // width
    total = PAIRS // ROWS * parts

    def first(n):
        u, r = n // parts, n % parts
        x = jnp.concatenate([xs[y2, pl.ds(u * ROWS * 8, ROWS * 8), :] for y2 in range(2)], 1)
        return dot32(in_ref[r * width : (r + 1) * width, :], x.astype(BF))

    ahead = {n: first(n) for n in range(LOOK)}
    raw = {}

    def finish(n):
        if n % parts == parts - 1:
            u = n // parts
            hidden = jnp.concatenate([raw.pop(u * parts + r) for r in range(parts)], 0)
            hid[plane, hid_rows(u), :] = hidden.astype(BF)
            lay_out(zs, u * ROWS, hidden)

    for n in range(total):
        if n + LOOK < total:
            ahead[n + LOOK] = first(n + LOOK)
        raw[n] = dot32(lo_ref[...], gelu_of_half(ahead.pop(n)))
        if n >= LAG:
            finish(n - LAG)
    for n in range(total - LAG, total):
        finish(n)


def from_modes(plane, count, recv, yi_ref, zi_ref, flat, sp):
    tiles = C * MZ // LANES
    slots = 2 * MY // count * tiles
    for src in range(count):
        flat[pl.ds(src * (slots + SKEW), slots), :] = recv[plane, src].astype(F32)

    def back_of(pair):
        rows = []
        for s in range(2 * MY // count):
            part = [
                flat[pl.ds(s * tiles + pair * 2 + half, count, stride=slots + SKEW), :]
                for half in range(2)
            ]
            rows.append(jnp.concatenate(part, 1))
        return dot32(yi_ref[...], jnp.concatenate(rows, 0).astype(BF)).astype(BF)

    for first in range(0, tiles // 2, FB):
        left, some = [], []
        for pair in range(first, first + FB):
            back = back_of(pair)
            for half in range(2):
                lanes = slice(half * LANES, (half + 1) * LANES)
                for y2 in range(2):
                    parts = [
                        back[(y2 * 2 + p) * PAIRS : (y2 * 2 + p + 1) * PAIRS, lanes] for p in range(2)
                    ]
                    left.append(jnp.concatenate(parts, 1))
                    some.append(((pair * 2 + half) * 4, y2))
        field = dot32(jnp.concatenate(left, 0), zi_ref[...])
        for n, (o, y2) in enumerate(some):
            for r in range(4):
                sp[y2, pl.ds(o + r, PAIRS, stride=C + SKEW), :] = field[
                    n * PAIRS : (n + 1) * PAIRS, r * NZ : (r + 1) * NZ
                ]


def field_rows(index, sp):
    halves = []
    for y2 in range(2):
        rows = [sp[y2, pl.ds((index * ROWS + r) * (C + SKEW), C), :] for r in range(ROWS)]
        halves.append(jnp.concatenate(rows, 0))
    return jnp.concatenate(halves, 1)


def middle_plane(plane, kp, hid, sp, zs):
    total = PAIRS // ROWS

    def local_term(index):
        return dot32(kp[...], hid[plane, hid_rows(index), :])

    ahead = {n: local_term(n) for n in range(MID)}
    for n in range(total):
        if n + MID < total:
            ahead[n + MID] = local_term(n + MID)
        hidden = gelu_of_half(ahead.pop(n) + field_rows(n, sp))
        hid[plane, hid_rows(n), :] = hidden
        lay_out(zs, n * ROWS, hidden.astype(F32))


def final_plane(plane, kp, di_ref, do_ref, perm_ref, hid, sp, st_ref):
    total = PAIRS // ROWS
    width = di_ref.shape[1]
    parts = di_ref.shape[0] // width

    def local_term(index):
        return dot32(kp[...], hid[plane, hid_rows(index), :])

    def mixed(n):
        return gelu_of_half(ahead.pop(n) + field_rows(n, sp))

    def decode(hidden, r):
        return dot32(di_ref[r * width : (r + 1) * width, :], hidden)

    def shrink(n, r):
        return dot32(do_ref[:, r * width : (r + 1) * width], gelu_of_half(raw.pop((n, r))))

    ahead = {n: local_term(n) for n in range(MID)}
    raw = {}
    hiddens = {0: mixed(0)}
    for r in range(parts):
        raw[0, r] = decode(hiddens[0], r)
    hiddens[1] = mixed(1)
    for n in range(total):
        if n + MID < total:
            ahead[n + MID] = local_term(n + MID)
        both = 0.0
        for r in range(parts):
            if n + 1 < total:
                raw[n + 1, r] = decode(hiddens[n + 1], r)
            both = both + shrink(n, r)
            if r == 0 and n + 2 < total:
                hiddens[n + 2] = mixed(n + 2)
        for y2 in range(2):
            lanes = slice(y2 * NZ, (y2 + 1) * NZ)
            where = pl.ds(n * ROWS * 2 + y2, ROWS, stride=2)
            st_ref[0, 0, plane, where, :] = both[:ROWS, lanes]
            st_ref[0, 1, plane, where, :] = both[ROWS:, lanes]

def residual_plane(plane, me, planes, perm_ref, cells, rates, ends, st_ref, res_ref, cond):
    sat = jax.nn.sigmoid(st_ref[0, 1, plane])
    st_ref[0, 1, plane] = sat
    conduct = mobility_of(sat, perm_ref[0, plane])
    cond[plane] = conduct
    pressure = st_ref[0, 0, plane]
    flux = 0.0
    for axis in range(2):
        length = pressure.shape[axis]
        inner = lax.broadcasted_iota(jnp.int32, pressure.shape, axis) < length - 1
        beyond = (pltpu.roll(field, length - 1, axis) for field in (conduct, pressure))
        cond_next, press_next = beyond
        face = jnp.where(inner, face_term(conduct, cond_next, pressure, press_next), 0.0)
        flux = flux + face - pltpu.roll(face, 1, axis)
    shape = (NY, cells.shape[1])
    here = cells[...] - (me * planes + plane) * (NY * NZ)
    starts = lax.broadcasted_iota(jnp.int32, shape, 0) * NZ
    offset = here - starts
    hit = (offset >= 0) & (offset < NZ)
    left = jnp.where(hit, rates[...], 0.0).astype(BF)
    dims = (((1,), (1,)), ((), ()))
    source = lax.dot_general(left, ends[...], dims, preferred_element_type=F32)
    res_ref[0, plane] = flux - source


def add_face(plane, st_ref, res_ref, cond):
    face = face_term(cond[plane], cond[plane + 1], st_ref[0, 0, plane], st_ref[0, 0, plane + 1])
    res_ref[0, plane] = res_ref[0, plane] + face
    res_ref[0, plane + 1] = res_ref[0, plane + 1] - face


def edge_copy(me, count, side, edge_send, edge_recv, es_sem, er_sem):
    return pltpu.make_async_remote_copy(
        src_ref=edge_send.at[side],
        dst_ref=edge_recv.at[1 - side],
        send_sem=es_sem.at[side],
        recv_sem=er_sem.at[1 - side],
        device_id={"space": lax.rem(me + (1 if side else count - 1), count)},
        device_id_type=pl.DeviceIdType.MESH,
    )


def wells_of(cells_ref, rates_ref, cells, rates, ends):
    rate = rates_ref[...]
    high = rate.astype(BF).astype(F32)
    middle = (rate - high).astype(BF).astype(F32)
    for n, part in enumerate((high, middle, rate - high - middle)):
        lanes = slice(n * WELLS, (n + 1) * WELLS)
        cells[:, lanes] = cells_ref[...]
        rates[:, lanes] = part
    column = lax.broadcasted_iota(jnp.int32, ends.shape, 0)
    ends[...] = jnp.where((cells[...] & (NZ - 1)) == column, 1.0, 0.0).astype(BF)


def mix_modes(planes, count, recv, send, wbuf, xf_ref, xi_ref, flat, spec, rows, mixed, turned):
    own = MY // count
    tiles = C * MZ // LANES
    slots = 2 * own * tiles
    pitch = slots + SKEW
    every = count * planes
    lane = lax.broadcasted_iota(jnp.int32, (1, LANES), 1)
    low = lane < 64
    even = lane % 64 < 32

    def unpack(plane, carry):
        for src in range(count):
            start = (plane * count + src) * pitch
            flat[pl.ds(start, slots), :] = recv[plane, src].astype(F32)
        return carry

    lax.fori_loop(0, planes, unpack, 0)

    def column(p, t):
        return flat[pl.ds(p * own * tiles + t, every, stride=pitch), :].astype(BF)

    for pair in range(own * tiles // 2):
        right = jnp.concatenate(
            [
                jnp.concatenate([column(p, pair * 2 + half) for half in range(2)], 1)
                for p in range(2)
            ],
            0,
        )
        total = dot32(xf_ref[...], right)
        for half in range(2):
            part = total[:, half * LANES : (half + 1) * LANES].T
            for r in range(4):
                first = (pair * 2 + half) * 4 + r
                spec[pl.ds(first * (MZ + SKEW), MZ), : 2 * MX] = part[r * MZ : (r + 1) * MZ, :]
    groups = own * MZ // MODE_STEP
    for group in range(groups):
        jj, k = group * MODE_STEP // MZ, group * MODE_STEP % MZ
        base = jj * C * (MZ + SKEW) + k
        picked = [
            spec[pl.ds(base + r, C, stride=MZ + SKEW), : 2 * MX] for r in range(MODE_STEP)
        ]
        rows[group] = jnp.concatenate(picked, 0).T
    wide = MODE_STEP * C
    own_mode = lax.broadcasted_iota(jnp.int32, (MODE_STEP, wide), 0) == (
        lax.broadcasted_iota(jnp.int32, (MODE_STEP, wide), 1) // C
    )
    per = wide // (2 * C)

    def step(group, carry):
        first = pl.multiple_of(group * MODE_STEP, MODE_STEP)
        for piece in range(MX // per):
            left = []
            for i in range(per):
                for q in range(2):
                    row = rows[group, pl.ds(q * MX + piece * per + i, MODE_STEP, stride=0), :]
                    left.append(jnp.where(own_mode, row, 0.0))
            lo = piece * wide
            weights = wbuf[pl.ds(first, MODE_STEP), :, lo : lo + wide].reshape(wide, wide)
            both = dot32(jnp.concatenate(left, 0).astype(BF), weights)

            def part(i, q, t):
                at = (i * 2 + q) * MODE_STEP
                return both[at : at + MODE_STEP, t * LANES : (t + 1) * LANES]

            for t in range(2):
                real, imag = (
                    jnp.where(low, part(2 * t, q, t), part(2 * t + 1, q, t)) for q in range(2)
                )
                turn = jnp.where(even, -pltpu.roll(imag, LANES - C, 1), pltpu.roll(imag, C, 1))
                mixed[pl.ds(first, MODE_STEP), lo + t * LANES : lo + (t + 1) * LANES] = real + turn
        return carry

    lax.fori_loop(0, groups, step, 0)
    for block in range(MX * 2 * C // LANES):
        part = mixed[:, block * LANES : (block + 1) * LANES].T
        for r in range(4):
            first = (block * 4 + r) * (C + SKEW)
            turned[pl.ds(first, C), : own * MZ] = part[r * C : (r + 1) * C, :]
    for pair in range(tiles // 2):
        right = [[], []]
        for half in range(2):
            o = (pair * 2 + half) * 4
            a = [turned[pl.ds(o + r, 2 * MX, stride=C + SKEW), :] for r in range(4)]
            b = jnp.where(low, a[0], pltpu.roll(a[2], 64, 1))
            c = jnp.where(low, a[1], pltpu.roll(a[3], 64, 1))
            right[0].append(jnp.where(even, b, pltpu.roll(c, 32, 1)))
            right[1].append(jnp.where(even, pltpu.roll(b, LANES - 32, 1), c))
        for jj in range(own):
            back = dot32(xi_ref[...], jnp.concatenate(right[jj], 1).astype(BF))
            for p in range(2):
                for half in range(2):
                    slot = (p * own + jj) * tiles + pair * 2 + half
                    flat[pl.ds(slot, every, stride=pitch), :] = back[
                        p * every : (p + 1) * every, half * LANES : (half + 1) * LANES
                    ]

    def pack(plane, carry):
        for dst in range(count):
            start = (plane * count + dst) * pitch
            send[plane, dst] = flat[pl.ds(start, slots), :].astype(BF)
        return carry

    lax.fori_loop(0, planes, pack, 0)


def whole_kernel(
    planes, count, feat_ref, perm_ref, lift_in, lift_out, point, dec_in, dec_out, zf_ref, zi_ref,
    yf_ref, yi_ref, xf_ref, xi_ref, cells_ref, rates_ref, w_hbm, st_ref, res_ref,
    hid, wbuf, send_f, recv_f, send_b, recv_b, flat, spec, rows, mixed, turned, zs, sp, xs, plain,
    in_ref, lo_ref, kp_ref, di_ref, do_ref, cond, cells, rates, ends, edge_send, edge_recv,
    w_sem, sf_sem, rf_sem, sb_sem, rb_sem, es_sem, er_sem,
):
    me = lax.axis_index("space")
    barrier = pltpu.get_barrier_semaphore()
    for shift in range(1, count):
        pl.semaphore_signal(
            barrier,
            inc=1,
            device_id={"space": lax.rem(me + shift, count)},
            device_id_type=pl.DeviceIdType.MESH,
        )
    fetch = pltpu.make_async_copy(w_hbm.at[0], wbuf, w_sem.at[0])
    fetch.start()
    xs[...] = jnp.zeros_like(xs)
    in_ref[...] = diag_of(lift_in[...], ROWS, 8, 0.5)
    lo_ref[...] = diag_of(lift_out[...], 2, lift_out.shape[1], 1.0, True)
    for layer in range(LAYERS):
        kp_ref[layer] = diag_of(point[layer], ROWS, C, 0.5)
    di_ref[...] = diag_of(dec_in[...], ROWS, C, 0.5)
    dec = dec_out.shape[1]
    do_ref[...] = spread(
        dec_out[...],
        2 * ROWS,
        ROWS * dec,
        lambda i: i // ROWS,
        lambda j: j % dec,
        lambda i, j: i % ROWS == j // dec,
        1.0,
        True,
    )
    wells_of(cells_ref, rates_ref, cells, rates, ends)
    pl.semaphore_wait(barrier, count - 1)

    def over(body):
        def run(plane, carry):
            body(plane)
            return carry

        lax.fori_loop(0, planes, run, 0)

    def lift(plane):
        lift_plane(plane, feat_ref, perm_ref, in_ref, lo_ref, hid, plain, xs, zs)
        to_modes(plane, count, zf_ref, yf_ref, zs, flat, send_f)
        send_plane(me, count, plane, send_f, recv_f, sf_sem, rf_sem)

    over(lift)
    for layer in range(LAYERS):
        fetch.wait()
        over(lambda plane: wait_plane(count, plane, recv_f, rf_sem))
        over(lambda plane: wait_plane(count, plane, send_f, sf_sem))
        mix_modes(
            planes, count, recv_f, send_b, wbuf, xf_ref, xi_ref, flat, spec, rows, mixed, turned
        )
        if layer + 1 < LAYERS:
            fetch = pltpu.make_async_copy(w_hbm.at[layer + 1], wbuf, w_sem.at[layer + 1])
            fetch.start()
        last = layer + 1 == LAYERS

        def turn(index):
            return lax.rem(planes - index, planes) if last else index

        over(lambda n: send_plane(me, count, turn(n), send_b, recv_b, sb_sem, rb_sem))
        kp = kp_ref.at[layer]

        def rest(index):
            plane = turn(index)
            wait_plane(count, plane, recv_b, rb_sem)
            from_modes(plane, count, recv_b, yi_ref, zi_ref, flat, sp)
            if not last:
                middle_plane(plane, kp, hid, sp, zs)
                to_modes(plane, count, zf_ref, yf_ref, zs, flat, send_f)
                send_plane(me, count, plane, send_f, recv_f, sf_sem, rf_sem)
            else:
                final_plane(plane, kp, di_ref, do_ref, perm_ref, hid, sp, st_ref)
                residual_plane(
                    plane, me, planes, perm_ref, cells, rates, ends, st_ref, res_ref, cond
                )

                @pl.when(index == 1)
                def _():
                    for side in range(2):
                        edge_send[side, 0] = st_ref[0, 0, side * (planes - 1)].astype(BF)
                        edge_send[side, 1] = cond[side * (planes - 1)].astype(BF)
                        edge_copy(me, count, side, edge_send, edge_recv, es_sem, er_sem).start()

                @pl.when(index >= 2)
                def _():
                    add_face(plane, st_ref, res_ref, cond)

        over(rest)
        over(lambda plane: wait_plane(count, plane, send_b, sb_sem))
    add_face(0, st_ref, res_ref, cond)
    for side in range(2):
        edge_copy(me, count, side, edge_send, edge_recv, es_sem, er_sem).wait()
    for side in range(2):
        plane = side * (planes - 1)
        press, conduct = (edge_recv[side, n].astype(F32) for n in range(2))
        face = face_term(cond[plane], conduct, st_ref[0, 0, plane], press)
        inside = me < count - 1 if side else me > 0
        res_ref[0, plane] = res_ref[0, plane] + jnp.where(inside, face, 0.0)


def ones_where(shape, test, value=1.0):
    row = lax.broadcasted_iota(jnp.int32, shape, 0)
    col = lax.broadcasted_iota(jnp.int32, shape, 1)
    return jnp.where(test(row, col), value, 0.0)


def spread(matrix, rows, cols, row_of, col_of, keep, value, turned):
    depth, height = matrix.shape[::-1] if turned else matrix.shape
    take = ones_where((rows, height), lambda i, j: row_of(i) == j).astype(BF)
    put = ones_where((depth, cols), lambda i, j: col_of(j) == i).astype(BF)
    dims = (((1,), (0 if turned else 1,)), ((), ()))
    part = lax.dot_general(take, matrix, dims, preferred_element_type=F32)
    return (dot32(part.astype(BF), put) * ones_where((rows, cols), keep, value)).astype(BF)


def diag_of(matrix, copies, width, value, turned=False):
    height = matrix.shape[0 if turned else 1]
    return spread(
        matrix,
        copies * height,
        copies * width,
        lambda i: i % height,
        lambda j: j % width,
        lambda i, j: i // height == j // width,
        value,
        turned,
    )


def local_fast(
    features,
    log_perm,
    well_cells,
    well_rates,
    lift_in,
    lift_out,
    spec_weight,
    point_weight,
    dec_in,
    dec_out,
):
    planes = features.shape[2]
    count = lax.axis_size("space")
    own = MY // count
    modes = own * MZ
    slots = 2 * modes * C // LANES
    tables = tables_for(count)
    lift, dec = lift_in.shape[1], dec_in.shape[1]
    operands = (
        features,
        log_perm,
        lift_in,
        lift_out.T,
        point_weight,
        dec_in,
        dec_out.T,
    ) + tuple(tables[name] for name in ("zf", "zi", "yf", "yi", "xf", "xi"))
    operands = operands + (well_cells, well_rates)
    vmem = pl.BlockSpec(memory_space=pltpu.VMEM)
    exchange = pltpu.VMEM((planes, count, slots, LANES), BF)
    return pl.pallas_call(
        lambda *refs: whole_kernel(planes, count, *refs),
        in_specs=[vmem] * len(operands) + [pl.BlockSpec(memory_space=pl.ANY)],
        out_specs=[vmem, vmem],
        out_shape=[
            jax.ShapeDtypeStruct((1, 2, planes, NY, NZ), F32),
            jax.ShapeDtypeStruct((1, planes, NY, NZ), F32),
        ],
        scratch_shapes=[
            pltpu.VMEM((planes, PAIRS * C, 2 * NZ), BF),
            pltpu.VMEM(spec_weight.shape[1:], BF),
            exchange,
            exchange,
            exchange,
            exchange,
            pltpu.VMEM((planes * count * (slots + SKEW), LANES), F32),
            pltpu.VMEM((own * C * (MZ + SKEW), LANES), F32),
            pltpu.VMEM((modes // MODE_STEP, 2 * MX, MODE_STEP * C), F32),
            pltpu.VMEM((modes, MX * 2 * C), F32),
            pltpu.VMEM((2 * MX * (C + SKEW), LANES), F32),
            pltpu.VMEM((2, C * PITCH, LANES), F32),
            pltpu.VMEM((2, PAIRS * (C + SKEW), LANES), F32),
            pltpu.VMEM((2, PAIRS * 8, NZ), F32),
            pltpu.VMEM((NY, NZ), F32),
            pltpu.VMEM((ROWS * lift, ROWS * 8), BF),
            pltpu.VMEM((2 * C, 2 * lift), BF),
            pltpu.VMEM((LAYERS, ROWS * C, ROWS * C), BF),
            pltpu.VMEM((ROWS * dec, ROWS * C), BF),
            pltpu.VMEM((2 * ROWS, ROWS * dec), BF),
            pltpu.VMEM((planes, NY, NZ), F32),
            pltpu.VMEM((1, 3 * WELLS), jnp.int32),
            pltpu.VMEM((1, 3 * WELLS), F32),
            pltpu.VMEM((NZ, 3 * WELLS), BF),
            pltpu.VMEM((2, 2, NY, NZ), BF),
            pltpu.VMEM((2, 2, NY, NZ), BF),
            pltpu.SemaphoreType.DMA((LAYERS,)),
        ]
        + [pltpu.SemaphoreType.DMA((planes,))] * 4
        + [pltpu.SemaphoreType.DMA((2,))] * 2,
        compiler_params=pltpu.CompilerParams(
            collective_id=0, has_side_effects=True, vmem_limit_bytes=60 * 1024 * 1024
        ),
        name="whole",
    )(*operands, spec_weight)


def local(features, log_perm, well_cells, well_rates, lift_in, lift_out, spec_weight, *rest):
    batches, planes = features.shape[0], features.shape[2]
    count = lax.axis_size("space")
    fits = batches == 1 and planes == 8 and count % 8 == 0 and MY == 2 * count
    run = local_fast if fits else local_general
    return run(
        features, log_perm, well_cells, well_rates, lift_in, lift_out, spec_weight, *rest
    )


def solution(mesh):
    return jax.shard_map(
        local,
        mesh=mesh,
        in_specs=(
            P("sample", None, "space", None, None),
            P("sample", "space", None, None),
            P("sample", None),
            P("sample", None),
            P(),
            P(),
            P(None, "space", None, None),
            P(),
            P(),
            P(),
        ),
        out_specs=(P("sample", None, "space", None, None), P("sample", "space", None, None)),
        check_vma=False,
    )
```

```python
import math

import jax
import jax.numpy as jnp
import numpy as np
from jax import lax
from jax.experimental import pallas as pl
from jax.experimental.pallas import tpu as pltpu
from jax.sharding import PartitionSpec as P

NX = 128
NY = 128
NZ = 128
MX = 32
MY = 32
MZ = 32
C = 32
FIN = 4
LAYERS = 2
WELLS = 32


def padded_2(block, sides, width):
    for axis, dim in sides:
        count = lax.axis_size(axis)
        forward = [(i, i + 1) for i in range(count - 1)]
        backward = [(target, source) for source, target in forward]
        low = lax.ppermute(
            lax.slice_in_dim(block, block.shape[dim] - width, None, axis=dim), axis, forward
        )
        high = lax.ppermute(lax.slice_in_dim(block, 0, width, axis=dim), axis, backward)
        block = jnp.concatenate([low, block, high], axis=dim)
    return block


def freq_table(length, kept, one_sided):
    indices = jnp.arange(kept, dtype=jnp.int32)
    if one_sided:
        return indices
    return jnp.where(indices < kept // 2, indices, length - kept + indices)


def wave_parts(length, kept, one_sided):
    freqs = freq_table(length, kept, one_sided)
    places = jnp.arange(length, dtype=jnp.int32)
    phase_turns = freqs[:, None] * places[None, :] % length
    angles = phase_turns.astype(jnp.float32) * (2.0 * math.pi / length)
    norm_scale = 1.0 / math.sqrt(length)
    return (jnp.cos(angles) * norm_scale, jnp.sin(angles) * norm_scale)


def forward_table(length, kept):
    cosine_vals, sine_vals = wave_parts(length, kept, False)
    return jnp.stack(
        [jnp.stack([cosine_vals.T, -sine_vals.T], 1), jnp.stack([sine_vals.T, cosine_vals.T], 1)], 1
    ).astype(jnp.bfloat16)


def inverse_table(length, kept):
    cosine_vals, sine_vals = wave_parts(length, kept, False)
    return jnp.stack(
        [jnp.stack([cosine_vals, sine_vals], 1), jnp.stack([-sine_vals, cosine_vals], 1)], 1
    ).astype(jnp.bfloat16)


def z_tables():
    cosine_vals, sine_vals = wave_parts(NZ, MZ, True)
    weights_k = jnp.where(jnp.arange(MZ) == 0, 1.0, 2.0).astype(jnp.float32)[:, None]
    z_forward = jnp.concatenate([cosine_vals.T, -sine_vals.T], 1).astype(jnp.bfloat16)
    z_inverse = jnp.concatenate([weights_k * cosine_vals, -weights_k * sine_vals], 0).astype(
        jnp.bfloat16
    )
    return (z_forward, z_inverse)


def gelu_tanh(values):
    return jax.nn.gelu(values, approximate=True)


def face_term(cond_a, cond_b, press_a, press_b):
    return 2.0 * cond_a * cond_b / (cond_a + cond_b) * (press_a - press_b)


def mobility_of(saturation, log_values):
    return jnp.exp(log_values) * (
        saturation * saturation + 0.5 * (1.0 - saturation) * (1.0 - saturation)
    )


def darcy(pressure, conduct, well_cells, well_rates):
    batches, planes = pressure.shape[0], pressure.shape[1]
    space_index = lax.axis_index("space")
    pad_cond = jnp.pad(conduct, ((0, 0), (0, 0), (1, 1), (1, 1)))
    pad_press = jnp.pad(pressure, ((0, 0), (0, 0), (1, 1), (1, 1)))
    flux_sum = face_term(conduct, pad_cond[:, :, 2:, 1:-1], pressure, pad_press[:, :, 2:, 1:-1])
    flux_sum = flux_sum + face_term(
        conduct, pad_cond[:, :, :-2, 1:-1], pressure, pad_press[:, :, :-2, 1:-1]
    )
    flux_sum = flux_sum + face_term(
        conduct, pad_cond[:, :, 1:-1, 2:], pressure, pad_press[:, :, 1:-1, 2:]
    )
    flux_sum = flux_sum + face_term(
        conduct, pad_cond[:, :, 1:-1, :-2], pressure, pad_press[:, :, 1:-1, :-2]
    )
    fields = jnp.stack([pressure, conduct], 1)
    padded = padded_2(fields.astype(jnp.bfloat16), (("space", 2),), 1).astype(fields.dtype)
    press_low = padded[:, 0, 0]
    press_high = padded[:, 0, -1]
    cond_low = padded[:, 1, 0]
    cond_high = padded[:, 1, -1]
    press_below = jnp.concatenate([press_low[:, None], pressure[:, :-1]], 1)
    cond_below = jnp.concatenate([cond_low[:, None], conduct[:, :-1]], 1)
    press_above = jnp.concatenate([pressure[:, 1:], press_high[:, None]], 1)
    cond_above = jnp.concatenate([conduct[:, 1:], cond_high[:, None]], 1)
    lower_terms = face_term(conduct, cond_below, pressure, press_below)
    upper_terms = face_term(conduct, cond_above, pressure, press_above)
    flux_sum = flux_sum + lower_terms + upper_terms
    well_x = well_cells // (NY * NZ) - space_index * planes
    well_y = well_cells // NZ % NY
    well_z = well_cells % NZ
    onehot_x = (well_x[:, :, None] == jnp.arange(planes, dtype=jnp.int32)[None, None, :]).astype(
        jnp.float32
    ) * well_rates[:, :, None]
    onehot_y = (well_y[:, :, None] == jnp.arange(NY, dtype=jnp.int32)[None, None, :]).astype(
        jnp.float32
    )
    onehot_z = (well_z[:, :, None] == jnp.arange(NZ, dtype=jnp.int32)[None, None, :]).astype(
        jnp.float32
    )
    plane_rows = (onehot_x[:, :, :, None] * onehot_y[:, :, None, :]).reshape(
        batches, WELLS, planes * NY
    )
    source = jnp.einsum(
        "bwa,bwz->baz", plane_rows, onehot_z, precision=lax.Precision.HIGHEST
    ).reshape(batches, planes, NY, NZ)
    return flux_sum - source


def local_general(
    features,
    log_perm,
    well_cells,
    well_rates,
    lift_in,
    lift_out,
    spec_weight,
    point_weight,
    dec_in,
    dec_out,
):
    batches = features.shape[0]
    planes = features.shape[2]
    space_index = lax.axis_index("space")
    block = spec_weight.shape[1]
    cell_count = planes * NY * NZ
    z_forward, z_inverse = z_tables()
    y_forward = forward_table(NY, MY)
    y_inverse = inverse_table(NY, MY)
    x_forward = forward_table(NX, MX)
    x_inverse = inverse_table(NX, MX)
    perm_b = log_perm.astype(jnp.bfloat16).reshape(batches, 1, cell_count)
    lift_input = jnp.concatenate([features.reshape(batches, FIN, cell_count), perm_b], 1)
    lift_hidden = jnp.einsum("bfn,fh->bhn", lift_input, lift_in, preferred_element_type=jnp.float32)
    lifted = gelu_tanh(lift_hidden).astype(jnp.bfloat16)
    hidden_state = jnp.einsum(
        "bhn,hc->bcn", lifted, lift_out, preferred_element_type=jnp.float32
    ).astype(jnp.bfloat16)
    for layer_idx in range(LAYERS):
        zspec = jnp.dot(hidden_state.reshape(-1, NZ), z_forward, preferred_element_type=jnp.float32)
        zspec = zspec.astype(jnp.bfloat16).reshape(batches * C * planes, NY, 2, MZ)
        yz_spec = jnp.einsum(
            "aypk,ypqj->aqjk", zspec, y_forward, preferred_element_type=jnp.float32
        )
        yz_spec = yz_spec.astype(jnp.bfloat16).reshape(batches, C, planes, 2, MY * MZ)
        mode_weights = spec_weight[layer_idx].reshape(block, C, MX, 2, C)
        spectrum = jnp.einsum(
            "bcxpm,xpqi->bcqim",
            lax.all_to_all(yz_spec, "space", split_axis=4, concat_axis=2, tiled=True),
            x_forward,
            preferred_element_type=jnp.float32,
        ).astype(jnp.bfloat16)
        products = jnp.einsum(
            "bcqim,mcipo->bimqpo", spectrum, mode_weights, preferred_element_type=jnp.float32
        )
        real_part = products[:, :, :, 0, 0] - products[:, :, :, 1, 1]
        imag_part = products[:, :, :, 0, 1] + products[:, :, :, 1, 0]
        mixed_modes = jnp.stack([real_part, imag_part], 3).astype(jnp.bfloat16)
        back_field = jnp.einsum(
            "bimqo,iqpx->boxpm", mixed_modes, x_inverse, preferred_element_type=jnp.float32
        ).astype(jnp.bfloat16)
        returned = lax.all_to_all(back_field, "space", split_axis=2, concat_axis=4, tiled=True)
        returned = returned.reshape(batches * C * planes, 2, MY, MZ)
        y_back = jnp.einsum(
            "aqjk,jqpy->aypk", returned, y_inverse, preferred_element_type=jnp.float32
        ).astype(jnp.bfloat16)
        spectral = jnp.dot(
            y_back.reshape(-1, 2 * MZ), z_inverse, preferred_element_type=jnp.float32
        ).reshape(batches, C, cell_count)
        local_term = jnp.einsum(
            "bcn,co->bon", hidden_state, point_weight[layer_idx], preferred_element_type=jnp.float32
        )
        hidden_state = gelu_tanh(spectral + local_term).astype(jnp.bfloat16)
    decoded = gelu_tanh(
        jnp.einsum("bcn,cd->bdn", hidden_state, dec_in, preferred_element_type=jnp.float32)
    ).astype(jnp.bfloat16)
    decoded_out = jnp.einsum("bdn,de->ben", decoded, dec_out, preferred_element_type=jnp.float32)
    pressure = decoded_out[:, 0].reshape(batches, planes, NY, NZ)
    saturation = jax.nn.sigmoid(decoded_out[:, 1]).reshape(batches, planes, NY, NZ)
    states = jnp.stack([pressure, saturation], 1)
    conduct = mobility_of(saturation, log_perm)
    return (states, darcy(pressure, conduct, well_cells, well_rates))


BF = jnp.bfloat16
F32 = jnp.float32
PAIRS = NY // 2
SKEW = 4
PITCH = PAIRS + SKEW
MODE_STEP = 8
ROWS = 8
LOOK = 4
LAG = 1
MID = 3
TB = 2
FB = 4
LANES = 128


def np_waves(length, kept, one_sided):
    index = np.arange(kept)
    freqs = index if one_sided else np.where(index < kept // 2, index, length - kept + index)
    angles = (freqs[:, None] * np.arange(length)[None, :] % length) * (2.0 * math.pi / length)
    norm = 1.0 / math.sqrt(length)
    return np.cos(angles) * norm, np.sin(angles) * norm


def np_forward(length, kept):
    cosine, sine = np_waves(length, kept, False)
    return np.stack([np.stack([cosine.T, -sine.T], 1), np.stack([sine.T, cosine.T], 1)], 1)


def np_inverse(length, kept):
    cosine, sine = np_waves(length, kept, False)
    return np.stack([np.stack([cosine, sine], 1), np.stack([-sine, cosine], 1)], 1)


def by_plane(table, axis, count):
    planes = NX // count
    order = np.arange(NX).reshape(count, planes).T.reshape(-1)
    return np.take(table, order, axis)


def tables_for(count):
    own = MY // count
    cosine, sine = np_waves(NZ, MZ, True)
    twice = np.where(np.arange(MZ) == 0, 1.0, 2.0)[:, None]
    z_forward = np.concatenate([cosine.T, -sine.T], 1)
    z_inverse = np.concatenate([twice * cosine, -twice * sine], 0)
    y_forward = np_forward(NY, MY).reshape(PAIRS, 2, 2, 2, count, own)
    y_inverse = np_inverse(NY, MY).reshape(count, own, 2, 2, PAIRS, 2)
    four = np.eye(4)
    z_forward = np.einsum("zpk,cd->czpdk", z_forward.reshape(NZ, 2, MZ), four)
    z_inverse = np.einsum("pkz,cd->pckdz", z_inverse.reshape(2, MZ, NZ), four)
    tables = {
        "zf": z_forward.reshape(4 * NZ, 8 * MZ),
        "zi": 0.5 * z_inverse.reshape(8 * MZ, 4 * NZ),
        "yf": y_forward.transpose(3, 5, 4, 1, 2, 0).reshape(2 * MY, 2 * NY),
        "yi": y_inverse.transpose(5, 3, 4, 2, 1, 0).reshape(2 * NY, 2 * MY),
        "xf": by_plane(np_forward(NX, MX).transpose(2, 3, 1, 0), 3, count).reshape(2 * MX, 2 * NX),
        "xi": by_plane(np_inverse(NX, MX).transpose(2, 3, 0, 1), 1, count).reshape(2 * NX, 2 * MX),
    }
    halves = tables["xi"].reshape(2, NX // count, 2, count // 2, 2 * MX)
    tables["xh"] = halves.transpose(2, 0, 1, 3, 4).reshape(2, NX, 2 * MX)
    return {name: jnp.asarray(table.astype(np.float32)).astype(BF) for name, table in tables.items()}


def dot32(a, b):
    return jnp.dot(a, b, preferred_element_type=F32)


def gelu_of_half(values):
    u = values.astype(BF)
    scale = math.sqrt(2.0 / math.pi)
    inner = u * (BF(2.0 * scale) + BF(8.0 * scale * 0.044715) * (u * u))
    return u + u * jnp.tanh(inner)


def send_plane(me, count, plane, send, recv, send_sem, recv_sem):
    for shift in range(1, count):
        target = lax.rem(me + shift, count)
        pltpu.make_async_remote_copy(
            src_ref=send.at[plane, target],
            dst_ref=recv.at[plane, me],
            send_sem=send_sem.at[plane],
            recv_sem=recv_sem.at[plane],
            device_id={"space": target},
            device_id_type=pl.DeviceIdType.MESH,
        ).start()
    recv[plane, me] = send[plane, me]


def wait_plane(parts, plane, buffer, sem):
    part = buffer.at[plane, pl.ds(0, parts)]
    pltpu.make_async_copy(part, part, sem.at[plane]).wait()


def to_modes(plane, count, zf_ref, yf_ref, zs, flat, send):
    tiles = C * MZ // LANES
    slots = 2 * MY // count * tiles
    halves = {}
    for first in range(0, tiles, 2 * TB):
        some = [(group, y2) for group in range(first, first + 2 * TB) for y2 in range(2)]
        left = [
            jnp.concatenate(
                [zs[y2, pl.ds((group * 4 + r) * PITCH, PAIRS), :] for r in range(4)], 1
            ).astype(BF)
            for group, y2 in some
        ]
        waves = dot32(jnp.concatenate(left, 0), zf_ref[...]).astype(BF)
        for n, key in enumerate(some):
            halves[key] = waves[n * PAIRS : (n + 1) * PAIRS, :]
    for pair in range(tiles // 2):
        columns = []
        for group in (pair * 2, pair * 2 + 1):
            parts = [
                halves[group, y2][:, p * LANES : (p + 1) * LANES] for y2 in range(2) for p in range(2)
            ]
            columns.append(jnp.concatenate(parts, 0))
        modes = dot32(yf_ref[...], jnp.concatenate(columns, 1))
        for s in range(2 * MY // count):
            for half in range(2):
                flat[pl.ds(s * tiles + pair * 2 + half, count, stride=slots + SKEW), :] = modes[
                    s * count : (s + 1) * count, half * LANES : (half + 1) * LANES
                ]
    for dst in range(count):
        send[plane, dst] = flat[pl.ds(dst * (slots + SKEW), slots), :].astype(BF)


def lay_out(zs, start, values):
    for y2 in range(2):
        for r in range(ROWS):
            zs[y2, pl.ds(start + r, C, stride=PITCH), :] = values[
                r * C : (r + 1) * C, y2 * NZ : (y2 + 1) * NZ
            ]


def hid_rows(index):
    return pl.ds(index * ROWS * C, ROWS * C)


def lift_plane(plane, feat_ref, perm_ref, in_ref, lo_ref, hid, plain, xs, zs):
    for f in range(FIN + 1):
        plain[...] = perm_ref[0, plane] if f == FIN else feat_ref[0, f, plane].astype(F32)
        for y2 in range(2):
            xs[y2, pl.ds(f, PAIRS, stride=8), :] = plain[pl.ds(y2, PAIRS, stride=2), :]
    width = lo_ref.shape[1]
    parts = in_ref.shape[0] // width
    total = PAIRS // ROWS * parts

    def first(n):
        u, r = n // parts, n % parts
        x = jnp.concatenate([xs[y2, pl.ds(u * ROWS * 8, ROWS * 8), :] for y2 in range(2)], 1)
        return dot32(in_ref[r * width : (r + 1) * width, :], x.astype(BF))

    ahead = {n: first(n) for n in range(LOOK)}
    raw = {}

    def finish(n):
        if n % parts == parts - 1:
            u = n // parts
            hidden = jnp.concatenate([raw.pop(u * parts + r) for r in range(parts)], 0)
            hid[plane, hid_rows(u), :] = hidden.astype(BF)
            lay_out(zs, u * ROWS, hidden)

    for n in range(total):
        if n + LOOK < total:
            ahead[n + LOOK] = first(n + LOOK)
        raw[n] = dot32(lo_ref[...], gelu_of_half(ahead.pop(n)))
        if n >= LAG:
            finish(n - LAG)
    for n in range(total - LAG, total):
        finish(n)


def from_modes(plane, count, recv, yi_ref, zi_ref, flat, sp):
    tiles = C * MZ // LANES
    slots = 2 * MY // count * tiles
    for src in range(count):
        flat[pl.ds(src * (slots + SKEW), slots), :] = recv[plane, src].astype(F32)

    def back_of(pair):
        rows = []
        for s in range(2 * MY // count):
            part = [
                flat[pl.ds(s * tiles + pair * 2 + half, count, stride=slots + SKEW), :]
                for half in range(2)
            ]
            rows.append(jnp.concatenate(part, 1))
        return dot32(yi_ref[...], jnp.concatenate(rows, 0).astype(BF)).astype(BF)

    for first in range(0, tiles // 2, FB):
        left, some = [], []
        for pair in range(first, first + FB):
            back = back_of(pair)
            for half in range(2):
                lanes = slice(half * LANES, (half + 1) * LANES)
                for y2 in range(2):
                    parts = [
                        back[(y2 * 2 + p) * PAIRS : (y2 * 2 + p + 1) * PAIRS, lanes] for p in range(2)
                    ]
                    left.append(jnp.concatenate(parts, 1))
                    some.append(((pair * 2 + half) * 4, y2))
        field = dot32(jnp.concatenate(left, 0), zi_ref[...])
        for n, (o, y2) in enumerate(some):
            for r in range(4):
                sp[y2, pl.ds(o + r, PAIRS, stride=C + SKEW), :] = field[
                    n * PAIRS : (n + 1) * PAIRS, r * NZ : (r + 1) * NZ
                ]


def field_rows(index, sp):
    halves = []
    for y2 in range(2):
        rows = [sp[y2, pl.ds((index * ROWS + r) * (C + SKEW), C), :] for r in range(ROWS)]
        halves.append(jnp.concatenate(rows, 0))
    return jnp.concatenate(halves, 1)


def middle_plane(plane, kp, hid, sp, zs):
    total = PAIRS // ROWS

    def local_term(index):
        return dot32(kp[...], hid[plane, hid_rows(index), :])

    ahead = {n: local_term(n) for n in range(MID)}
    for n in range(total):
        if n + MID < total:
            ahead[n + MID] = local_term(n + MID)
        hidden = gelu_of_half(ahead.pop(n) + field_rows(n, sp))
        hid[plane, hid_rows(n), :] = hidden
        lay_out(zs, n * ROWS, hidden.astype(F32))


def final_plane(plane, kp, di_ref, do_ref, perm_ref, hid, sp, st_ref):
    total = PAIRS // ROWS
    width = di_ref.shape[1]
    parts = di_ref.shape[0] // width

    def local_term(index):
        return dot32(kp[...], hid[plane, hid_rows(index), :])

    def mixed(n):
        return gelu_of_half(ahead.pop(n) + field_rows(n, sp))

    def decode(hidden, r):
        return dot32(di_ref[r * width : (r + 1) * width, :], hidden)

    def shrink(n, r):
        return dot32(do_ref[:, r * width : (r + 1) * width], gelu_of_half(raw.pop((n, r))))

    ahead = {n: local_term(n) for n in range(MID)}
    raw = {}
    hiddens = {0: mixed(0)}
    for r in range(parts):
        raw[0, r] = decode(hiddens[0], r)
    hiddens[1] = mixed(1)
    for n in range(total):
        if n + MID < total:
            ahead[n + MID] = local_term(n + MID)
        both = 0.0
        for r in range(parts):
            if n + 1 < total:
                raw[n + 1, r] = decode(hiddens[n + 1], r)
            both = both + shrink(n, r)
            if r == 0 and n + 2 < total:
                hiddens[n + 2] = mixed(n + 2)
        for y2 in range(2):
            lanes = slice(y2 * NZ, (y2 + 1) * NZ)
            where = pl.ds(n * ROWS * 2 + y2, ROWS, stride=2)
            st_ref[0, 0, plane, where, :] = both[:ROWS, lanes]
            st_ref[0, 1, plane, where, :] = both[ROWS:, lanes]

def residual_plane(plane, me, planes, perm_ref, cells, rates, ends, st_ref, res_ref, cond):
    sat = jax.nn.sigmoid(st_ref[0, 1, plane])
    st_ref[0, 1, plane] = sat
    conduct = mobility_of(sat, perm_ref[0, plane])
    cond[plane] = conduct
    pressure = st_ref[0, 0, plane]
    flux = 0.0
    for axis in range(2):
        length = pressure.shape[axis]
        inner = lax.broadcasted_iota(jnp.int32, pressure.shape, axis) < length - 1
        beyond = (pltpu.roll(field, length - 1, axis) for field in (conduct, pressure))
        cond_next, press_next = beyond
        face = jnp.where(inner, face_term(conduct, cond_next, pressure, press_next), 0.0)
        flux = flux + face - pltpu.roll(face, 1, axis)
    shape = (NY, cells.shape[1])
    here = cells[...] - (me * planes + plane) * (NY * NZ)
    starts = lax.broadcasted_iota(jnp.int32, shape, 0) * NZ
    offset = here - starts
    hit = (offset >= 0) & (offset < NZ)
    left = jnp.where(hit, rates[...], 0.0).astype(BF)
    dims = (((1,), (1,)), ((), ()))
    source = lax.dot_general(left, ends[...], dims, preferred_element_type=F32)
    res_ref[0, plane] = flux - source


def add_face(plane, st_ref, res_ref, cond):
    face = face_term(cond[plane], cond[plane + 1], st_ref[0, 0, plane], st_ref[0, 0, plane + 1])
    res_ref[0, plane] = res_ref[0, plane] + face
    res_ref[0, plane + 1] = res_ref[0, plane + 1] - face


def edge_copy(me, count, side, edge_send, edge_recv, es_sem, er_sem):
    return pltpu.make_async_remote_copy(
        src_ref=edge_send.at[side],
        dst_ref=edge_recv.at[1 - side],
        send_sem=es_sem.at[side],
        recv_sem=er_sem.at[1 - side],
        device_id={"space": lax.rem(me + (1 if side else count - 1), count)},
        device_id_type=pl.DeviceIdType.MESH,
    )


def wells_of(cells_ref, rates_ref, cells, rates, ends):
    rate = rates_ref[...]
    high = rate.astype(BF).astype(F32)
    middle = (rate - high).astype(BF).astype(F32)
    for n, part in enumerate((high, middle, rate - high - middle)):
        lanes = slice(n * WELLS, (n + 1) * WELLS)
        cells[:, lanes] = cells_ref[...]
        rates[:, lanes] = part
    column = lax.broadcasted_iota(jnp.int32, ends.shape, 0)
    ends[...] = jnp.where((cells[...] & (NZ - 1)) == column, 1.0, 0.0).astype(BF)


def mix_modes(planes, count, recv, wbuf, xf_ref, flat, spec, rows, mixed, turned):
    own = MY // count
    tiles = C * MZ // LANES
    slots = 2 * own * tiles
    pitch = slots + SKEW
    every = count * planes
    lane = lax.broadcasted_iota(jnp.int32, (1, LANES), 1)
    low = lane < 64
    even = lane % 64 < 32

    def unpack(plane, carry):
        for src in range(count):
            start = (plane * count + src) * pitch
            flat[pl.ds(start, slots), :] = recv[plane, src].astype(F32)
        return carry

    lax.fori_loop(0, planes, unpack, 0)

    def column(p, t):
        return flat[pl.ds(p * own * tiles + t, every, stride=pitch), :].astype(BF)

    for pair in range(own * tiles // 2):
        right = jnp.concatenate(
            [
                jnp.concatenate([column(p, pair * 2 + half) for half in range(2)], 1)
                for p in range(2)
            ],
            0,
        )
        total = dot32(xf_ref[...], right)
        for half in range(2):
            part = total[:, half * LANES : (half + 1) * LANES].T
            for r in range(4):
                first = (pair * 2 + half) * 4 + r
                spec[pl.ds(first * (MZ + SKEW), MZ), : 2 * MX] = part[r * MZ : (r + 1) * MZ, :]
    groups = own * MZ // MODE_STEP
    for group in range(groups):
        jj, k = group * MODE_STEP // MZ, group * MODE_STEP % MZ
        base = jj * C * (MZ + SKEW) + k
        picked = [
            spec[pl.ds(base + r, C, stride=MZ + SKEW), : 2 * MX] for r in range(MODE_STEP)
        ]
        rows[group] = jnp.concatenate(picked, 0).T
    wide = MODE_STEP * C
    own_mode = lax.broadcasted_iota(jnp.int32, (MODE_STEP, wide), 0) == (
        lax.broadcasted_iota(jnp.int32, (MODE_STEP, wide), 1) // C
    )
    per = wide // (2 * C)

    def step(group, carry):
        first = pl.multiple_of(group * MODE_STEP, MODE_STEP)
        for piece in range(MX // per):
            left = []
            for i in range(per):
                for q in range(2):
                    row = rows[group, pl.ds(q * MX + piece * per + i, MODE_STEP, stride=0), :]
                    left.append(jnp.where(own_mode, row, 0.0))
            lo = piece * wide
            weights = wbuf[pl.ds(first, MODE_STEP), :, lo : lo + wide].reshape(wide, wide)
            both = dot32(jnp.concatenate(left, 0).astype(BF), weights)

            def part(i, q, t):
                at = (i * 2 + q) * MODE_STEP
                return both[at : at + MODE_STEP, t * LANES : (t + 1) * LANES]

            for t in range(2):
                real, imag = (
                    jnp.where(low, part(2 * t, q, t), part(2 * t + 1, q, t)) for q in range(2)
                )
                turn = jnp.where(even, -pltpu.roll(imag, LANES - C, 1), pltpu.roll(imag, C, 1))
                mixed[pl.ds(first, MODE_STEP), lo + t * LANES : lo + (t + 1) * LANES] = real + turn
        return carry

    lax.fori_loop(0, groups, step, 0)
    for block in range(MX * 2 * C // LANES):
        part = mixed[:, block * LANES : (block + 1) * LANES].T
        for r in range(4):
            first = (block * 4 + r) * (C + SKEW)
            turned[pl.ds(first, C), : own * MZ] = part[r * C : (r + 1) * C, :]


def mixed_tile(pair, turned):
    lane = lax.broadcasted_iota(jnp.int32, (1, LANES), 1)
    low = lane < 64
    even = lane % 64 < 32
    right = [[], []]
    for half in range(2):
        o = (pair * 2 + half) * 4
        a = [turned[pl.ds(o + r, 2 * MX, stride=C + SKEW), :] for r in range(4)]
        b = jnp.where(low, a[0], pltpu.roll(a[2], 64, 1))
        c = jnp.where(low, a[1], pltpu.roll(a[3], 64, 1))
        right[0].append(jnp.where(even, b, pltpu.roll(c, 32, 1)))
        right[1].append(jnp.where(even, pltpu.roll(b, LANES - 32, 1), c))
    return [jnp.concatenate(part, 1).astype(BF) for part in right]


def to_planes(table, tile, jj, pair, count, flat):
    own = MY // count
    tiles = C * MZ // LANES
    pitch = 2 * own * tiles + SKEW
    back = dot32(table, tile)
    every = back.shape[0] // 2
    for p in range(2):
        for half in range(2):
            slot = (p * own + jj) * tiles + pair * 2 + half
            flat[pl.ds(slot, every, stride=pitch), :] = back[
                p * every : (p + 1) * every, half * LANES : (half + 1) * LANES
            ]


def pack_planes(planes, count, first, targets, flat, send):
    slots = 2 * MY // count * C * MZ // LANES
    pitch = slots + SKEW

    def pack(plane, carry):
        for dst in range(targets):
            start = (plane * targets + dst) * pitch
            send[plane, first + dst] = flat[pl.ds(start, slots), :].astype(BF)
        return carry

    lax.fori_loop(0, planes, pack, 0)


def send_half(me, count, plane, other, send, recv, send_sem, recv_sem):
    near = count // 2
    owner = lax.rem(me + other * near, count)
    for shift in range(1, near):
        place = lax.rem(me + shift, near)
        pltpu.make_async_remote_copy(
            src_ref=send.at[plane, other * near + place],
            dst_ref=recv.at[plane, owner],
            send_sem=send_sem.at[plane],
            recv_sem=recv_sem.at[plane],
            device_id={"space": me // near * near + place},
            device_id_type=pl.DeviceIdType.MESH,
        ).start()
    recv[plane, owner] = send[plane, other * near + lax.rem(me, near)]


def swap_tile(me, count, n, own, other, send_sem, recv_sem):
    return pltpu.make_async_remote_copy(
        src_ref=own.at[n],
        dst_ref=other.at[n],
        send_sem=send_sem.at[n],
        recv_sem=recv_sem.at[n],
        device_id={"space": lax.rem(me + count // 2, count)},
        device_id_type=pl.DeviceIdType.MESH,
    )


def whole_kernel(
    planes, count, feat_ref, perm_ref, lift_in, lift_out, point, dec_in, dec_out, zf_ref, zi_ref,
    yf_ref, yi_ref, xf_ref, xi_ref, xh_ref, cells_ref, rates_ref, w_hbm, st_ref, res_ref,
    hid, wbuf, send_f, recv_f, send_b, recv_b, flat, spec, rows, mixed, turned, zs, sp, xs, plain,
    in_ref, lo_ref, kp_ref, di_ref, do_ref, cond, cells, rates, ends, edge_send, edge_recv,
    own_mixed, other_mixed,
    w_sem, sf_sem, rf_sem, sb_sem, rb_sem, es_sem, er_sem, om_sem, rm_sem,
):
    me = lax.axis_index("space")
    barrier = pltpu.get_barrier_semaphore()
    for shift in range(1, count):
        pl.semaphore_signal(
            barrier,
            inc=1,
            device_id={"space": lax.rem(me + shift, count)},
            device_id_type=pl.DeviceIdType.MESH,
        )
    fetch = pltpu.make_async_copy(w_hbm.at[0], wbuf, w_sem.at[0])
    fetch.start()
    xs[...] = jnp.zeros_like(xs)
    in_ref[...] = diag_of(lift_in[...], ROWS, 8, 0.5)
    lo_ref[...] = diag_of(lift_out[...], 2, lift_out.shape[1], 1.0, True)
    for layer in range(LAYERS):
        kp_ref[layer] = diag_of(point[layer], ROWS, C, 0.5)
    di_ref[...] = diag_of(dec_in[...], ROWS, C, 0.5)
    dec = dec_out.shape[1]
    do_ref[...] = spread(
        dec_out[...],
        2 * ROWS,
        ROWS * dec,
        lambda i: i // ROWS,
        lambda j: j % dec,
        lambda i, j: i % ROWS == j // dec,
        1.0,
        True,
    )
    wells_of(cells_ref, rates_ref, cells, rates, ends)
    pl.semaphore_wait(barrier, count - 1)

    def over(body):
        def run(plane, carry):
            body(plane)
            return carry

        lax.fori_loop(0, planes, run, 0)

    def lift(plane):
        lift_plane(plane, feat_ref, perm_ref, in_ref, lo_ref, hid, plain, xs, zs)
        to_modes(plane, count, zf_ref, yf_ref, zs, flat, send_f)
        send_plane(me, count, plane, send_f, recv_f, sf_sem, rf_sem)

    over(lift)
    for layer in range(LAYERS):
        fetch.wait()
        over(lambda plane: wait_plane(count - 1, plane, recv_f, rf_sem))
        over(lambda plane: wait_plane(count - 1, plane, send_f, sf_sem))
        mix_modes(planes, count, recv_f, wbuf, xf_ref, flat, spec, rows, mixed, turned)
        if layer + 1 < LAYERS:
            fetch = pltpu.make_async_copy(w_hbm.at[layer + 1], wbuf, w_sem.at[layer + 1])
            fetch.start()
        last = layer + 1 == LAYERS

        def turn(index):
            return lax.rem(planes - index, planes) if last else index

        pairs = [(pair, jj) for pair in range(C * MZ // LANES // 2) for jj in range(MY // count)]
        if last:
            parts = count - 1
            for pair, jj in pairs:
                if jj == 0:
                    tile = mixed_tile(pair, turned)
                to_planes(xi_ref[...], tile[jj], jj, pair, count, flat)
            pack_planes(planes, count, 0, count, flat, send_b)
            over(lambda n: send_plane(me, count, turn(n), send_b, recv_b, sb_sem, rb_sem))
        else:
            near = count // 2
            parts = 2 * (near - 1)
            swaps = [
                swap_tile(me, count, n, own_mixed, other_mixed, om_sem, rm_sem)
                for n in range(len(pairs))
            ]
            for n, (pair, jj) in enumerate(pairs):
                if jj == 0:
                    tile = mixed_tile(pair, turned)
                own_mixed[n] = tile[jj]
                swaps[n].start()
            table = xh_ref.at[me // near]
            for other in range(2):
                for n, (pair, jj) in enumerate(pairs):
                    if other:
                        swaps[n].wait_recv()
                    tile = other_mixed[n] if other else own_mixed[n]
                    to_planes(table[...], tile, jj, pair, count, flat)
                pack_planes(planes, count, other * near, near, flat, send_b)
                over(lambda n: send_half(me, count, n, other, send_b, recv_b, sb_sem, rb_sem))
            for swap in swaps:
                swap.wait_send()
        kp = kp_ref.at[layer]

        def rest(index):
            plane = turn(index)
            wait_plane(parts, plane, recv_b, rb_sem)
            from_modes(plane, count, recv_b, yi_ref, zi_ref, flat, sp)
            if not last:
                middle_plane(plane, kp, hid, sp, zs)
                to_modes(plane, count, zf_ref, yf_ref, zs, flat, send_f)
                send_plane(me, count, plane, send_f, recv_f, sf_sem, rf_sem)
            else:
                final_plane(plane, kp, di_ref, do_ref, perm_ref, hid, sp, st_ref)
                residual_plane(
                    plane, me, planes, perm_ref, cells, rates, ends, st_ref, res_ref, cond
                )

                @pl.when(index == 1)
                def _():
                    for side in range(2):
                        edge_send[side, 0] = st_ref[0, 0, side * (planes - 1)].astype(BF)
                        edge_send[side, 1] = cond[side * (planes - 1)].astype(BF)
                        edge_copy(me, count, side, edge_send, edge_recv, es_sem, er_sem).start()

                @pl.when(index >= 2)
                def _():
                    add_face(plane, st_ref, res_ref, cond)

        over(rest)
        over(lambda plane: wait_plane(parts, plane, send_b, sb_sem))
    add_face(0, st_ref, res_ref, cond)
    for side in range(2):
        edge_copy(me, count, side, edge_send, edge_recv, es_sem, er_sem).wait()
    for side in range(2):
        plane = side * (planes - 1)
        press, conduct = (edge_recv[side, n].astype(F32) for n in range(2))
        face = face_term(cond[plane], conduct, st_ref[0, 0, plane], press)
        inside = me < count - 1 if side else me > 0
        res_ref[0, plane] = res_ref[0, plane] + jnp.where(inside, face, 0.0)


def ones_where(shape, test, value=1.0):
    row = lax.broadcasted_iota(jnp.int32, shape, 0)
    col = lax.broadcasted_iota(jnp.int32, shape, 1)
    return jnp.where(test(row, col), value, 0.0)


def spread(matrix, rows, cols, row_of, col_of, keep, value, turned):
    depth, height = matrix.shape[::-1] if turned else matrix.shape
    take = ones_where((rows, height), lambda i, j: row_of(i) == j).astype(BF)
    put = ones_where((depth, cols), lambda i, j: col_of(j) == i).astype(BF)
    dims = (((1,), (0 if turned else 1,)), ((), ()))
    part = lax.dot_general(take, matrix, dims, preferred_element_type=F32)
    return (dot32(part.astype(BF), put) * ones_where((rows, cols), keep, value)).astype(BF)


def diag_of(matrix, copies, width, value, turned=False):
    height = matrix.shape[0 if turned else 1]
    return spread(
        matrix,
        copies * height,
        copies * width,
        lambda i: i % height,
        lambda j: j % width,
        lambda i, j: i // height == j // width,
        value,
        turned,
    )


def local_fast(
    features,
    log_perm,
    well_cells,
    well_rates,
    lift_in,
    lift_out,
    spec_weight,
    point_weight,
    dec_in,
    dec_out,
):
    planes = features.shape[2]
    count = lax.axis_size("space")
    own = MY // count
    modes = own * MZ
    slots = 2 * modes * C // LANES
    tables = tables_for(count)
    lift, dec = lift_in.shape[1], dec_in.shape[1]
    operands = (
        features,
        log_perm,
        lift_in,
        lift_out.T,
        point_weight,
        dec_in,
        dec_out.T,
    ) + tuple(tables[name] for name in ("zf", "zi", "yf", "yi", "xf", "xi", "xh"))
    operands = operands + (well_cells, well_rates)
    vmem = pl.BlockSpec(memory_space=pltpu.VMEM)
    exchange = pltpu.VMEM((planes, count, slots, LANES), BF)
    return pl.pallas_call(
        lambda *refs: whole_kernel(planes, count, *refs),
        in_specs=[vmem] * len(operands) + [pl.BlockSpec(memory_space=pl.ANY)],
        out_specs=[vmem, vmem],
        out_shape=[
            jax.ShapeDtypeStruct((1, 2, planes, NY, NZ), F32),
            jax.ShapeDtypeStruct((1, planes, NY, NZ), F32),
        ],
        scratch_shapes=[
            pltpu.VMEM((planes, PAIRS * C, 2 * NZ), BF),
            pltpu.VMEM(spec_weight.shape[1:], BF),
            exchange,
            exchange,
            exchange,
            exchange,
            pltpu.VMEM((planes * count * (slots + SKEW), LANES), F32),
            pltpu.VMEM((own * C * (MZ + SKEW), LANES), F32),
            pltpu.VMEM((modes // MODE_STEP, 2 * MX, MODE_STEP * C), F32),
            pltpu.VMEM((modes, MX * 2 * C), F32),
            pltpu.VMEM((2 * MX * (C + SKEW), LANES), F32),
            pltpu.VMEM((2, C * PITCH, LANES), F32),
            pltpu.VMEM((2, PAIRS * (C + SKEW), LANES), F32),
            pltpu.VMEM((2, PAIRS * 8, NZ), F32),
            pltpu.VMEM((NY, NZ), F32),
            pltpu.VMEM((ROWS * lift, ROWS * 8), BF),
            pltpu.VMEM((2 * C, 2 * lift), BF),
            pltpu.VMEM((LAYERS, ROWS * C, ROWS * C), BF),
            pltpu.VMEM((ROWS * dec, ROWS * C), BF),
            pltpu.VMEM((2 * ROWS, ROWS * dec), BF),
            pltpu.VMEM((planes, NY, NZ), F32),
            pltpu.VMEM((1, 3 * WELLS), jnp.int32),
            pltpu.VMEM((1, 3 * WELLS), F32),
            pltpu.VMEM((NZ, 3 * WELLS), BF),
            pltpu.VMEM((2, 2, NY, NZ), BF),
            pltpu.VMEM((2, 2, NY, NZ), BF),
            pltpu.VMEM((modes * C // 256, 2 * MX, 256), BF),
            pltpu.VMEM((modes * C // 256, 2 * MX, 256), BF),
            pltpu.SemaphoreType.DMA((LAYERS,)),
        ]
        + [pltpu.SemaphoreType.DMA((planes,))] * 4
        + [pltpu.SemaphoreType.DMA((2,))] * 2
        + [pltpu.SemaphoreType.DMA((modes * C // 256,))] * 2,
        compiler_params=pltpu.CompilerParams(
            collective_id=0, has_side_effects=True, vmem_limit_bytes=60 * 1024 * 1024
        ),
        name="whole",
    )(*operands, spec_weight)


def local(features, log_perm, well_cells, well_rates, lift_in, lift_out, spec_weight, *rest):
    batches, planes = features.shape[0], features.shape[2]
    count = lax.axis_size("space")
    fits = batches == 1 and planes == 8 and count % 8 == 0 and MY == 2 * count
    run = local_fast if fits else local_general
    return run(
        features, log_perm, well_cells, well_rates, lift_in, lift_out, spec_weight, *rest
    )


def solution(mesh):
    return jax.shard_map(
        local,
        mesh=mesh,
        in_specs=(
            P("sample", None, "space", None, None),
            P("sample", "space", None, None),
            P("sample", None),
            P("sample", None),
            P(),
            P(),
            P(None, "space", None, None),
            P(),
            P(),
            P(),
        ),
        out_specs=(P("sample", None, "space", None, None), P("sample", "space", None, None)),
        check_vma=False,
    )
```

```python
import math

import jax
import jax.numpy as jnp
import numpy as np
from jax import lax
from jax.experimental import pallas as pl
from jax.experimental.pallas import tpu as pltpu
from jax.sharding import PartitionSpec as P

NX = 128
NY = 128
NZ = 128
MX = 32
MY = 32
MZ = 32
C = 32
FIN = 4
LAYERS = 2
WELLS = 32


def padded_2(block, sides, width):
    for axis, dim in sides:
        count = lax.axis_size(axis)
        forward = [(i, i + 1) for i in range(count - 1)]
        backward = [(target, source) for source, target in forward]
        low = lax.ppermute(
            lax.slice_in_dim(block, block.shape[dim] - width, None, axis=dim), axis, forward
        )
        high = lax.ppermute(lax.slice_in_dim(block, 0, width, axis=dim), axis, backward)
        block = jnp.concatenate([low, block, high], axis=dim)
    return block


def freq_table(length, kept, one_sided):
    indices = jnp.arange(kept, dtype=jnp.int32)
    if one_sided:
        return indices
    return jnp.where(indices < kept // 2, indices, length - kept + indices)


def wave_parts(length, kept, one_sided):
    freqs = freq_table(length, kept, one_sided)
    places = jnp.arange(length, dtype=jnp.int32)
    phase_turns = freqs[:, None] * places[None, :] % length
    angles = phase_turns.astype(jnp.float32) * (2.0 * math.pi / length)
    norm_scale = 1.0 / math.sqrt(length)
    return (jnp.cos(angles) * norm_scale, jnp.sin(angles) * norm_scale)


def forward_table(length, kept):
    cosine_vals, sine_vals = wave_parts(length, kept, False)
    return jnp.stack(
        [jnp.stack([cosine_vals.T, -sine_vals.T], 1), jnp.stack([sine_vals.T, cosine_vals.T], 1)], 1
    ).astype(jnp.bfloat16)


def inverse_table(length, kept):
    cosine_vals, sine_vals = wave_parts(length, kept, False)
    return jnp.stack(
        [jnp.stack([cosine_vals, sine_vals], 1), jnp.stack([-sine_vals, cosine_vals], 1)], 1
    ).astype(jnp.bfloat16)


def z_tables():
    cosine_vals, sine_vals = wave_parts(NZ, MZ, True)
    weights_k = jnp.where(jnp.arange(MZ) == 0, 1.0, 2.0).astype(jnp.float32)[:, None]
    z_forward = jnp.concatenate([cosine_vals.T, -sine_vals.T], 1).astype(jnp.bfloat16)
    z_inverse = jnp.concatenate([weights_k * cosine_vals, -weights_k * sine_vals], 0).astype(
        jnp.bfloat16
    )
    return (z_forward, z_inverse)


def gelu_tanh(values):
    return jax.nn.gelu(values, approximate=True)


def face_term(cond_a, cond_b, press_a, press_b):
    return 2.0 * cond_a * cond_b / (cond_a + cond_b) * (press_a - press_b)


def mobility_of(saturation, log_values):
    return jnp.exp(log_values) * (
        saturation * saturation + 0.5 * (1.0 - saturation) * (1.0 - saturation)
    )


def darcy(pressure, conduct, well_cells, well_rates):
    batches, planes = pressure.shape[0], pressure.shape[1]
    space_index = lax.axis_index("space")
    pad_cond = jnp.pad(conduct, ((0, 0), (0, 0), (1, 1), (1, 1)))
    pad_press = jnp.pad(pressure, ((0, 0), (0, 0), (1, 1), (1, 1)))
    flux_sum = face_term(conduct, pad_cond[:, :, 2:, 1:-1], pressure, pad_press[:, :, 2:, 1:-1])
    flux_sum = flux_sum + face_term(
        conduct, pad_cond[:, :, :-2, 1:-1], pressure, pad_press[:, :, :-2, 1:-1]
    )
    flux_sum = flux_sum + face_term(
        conduct, pad_cond[:, :, 1:-1, 2:], pressure, pad_press[:, :, 1:-1, 2:]
    )
    flux_sum = flux_sum + face_term(
        conduct, pad_cond[:, :, 1:-1, :-2], pressure, pad_press[:, :, 1:-1, :-2]
    )
    fields = jnp.stack([pressure, conduct], 1)
    padded = padded_2(fields.astype(jnp.bfloat16), (("space", 2),), 1).astype(fields.dtype)
    press_low = padded[:, 0, 0]
    press_high = padded[:, 0, -1]
    cond_low = padded[:, 1, 0]
    cond_high = padded[:, 1, -1]
    press_below = jnp.concatenate([press_low[:, None], pressure[:, :-1]], 1)
    cond_below = jnp.concatenate([cond_low[:, None], conduct[:, :-1]], 1)
    press_above = jnp.concatenate([pressure[:, 1:], press_high[:, None]], 1)
    cond_above = jnp.concatenate([conduct[:, 1:], cond_high[:, None]], 1)
    lower_terms = face_term(conduct, cond_below, pressure, press_below)
    upper_terms = face_term(conduct, cond_above, pressure, press_above)
    flux_sum = flux_sum + lower_terms + upper_terms
    well_x = well_cells // (NY * NZ) - space_index * planes
    well_y = well_cells // NZ % NY
    well_z = well_cells % NZ
    onehot_x = (well_x[:, :, None] == jnp.arange(planes, dtype=jnp.int32)[None, None, :]).astype(
        jnp.float32
    ) * well_rates[:, :, None]
    onehot_y = (well_y[:, :, None] == jnp.arange(NY, dtype=jnp.int32)[None, None, :]).astype(
        jnp.float32
    )
    onehot_z = (well_z[:, :, None] == jnp.arange(NZ, dtype=jnp.int32)[None, None, :]).astype(
        jnp.float32
    )
    plane_rows = (onehot_x[:, :, :, None] * onehot_y[:, :, None, :]).reshape(
        batches, WELLS, planes * NY
    )
    source = jnp.einsum(
        "bwa,bwz->baz", plane_rows, onehot_z, precision=lax.Precision.HIGHEST
    ).reshape(batches, planes, NY, NZ)
    return flux_sum - source


def local_general(
    features,
    log_perm,
    well_cells,
    well_rates,
    lift_in,
    lift_out,
    spec_weight,
    point_weight,
    dec_in,
    dec_out,
):
    batches = features.shape[0]
    planes = features.shape[2]
    space_index = lax.axis_index("space")
    block = spec_weight.shape[1]
    cell_count = planes * NY * NZ
    z_forward, z_inverse = z_tables()
    y_forward = forward_table(NY, MY)
    y_inverse = inverse_table(NY, MY)
    x_forward = forward_table(NX, MX)
    x_inverse = inverse_table(NX, MX)
    perm_b = log_perm.astype(jnp.bfloat16).reshape(batches, 1, cell_count)
    lift_input = jnp.concatenate([features.reshape(batches, FIN, cell_count), perm_b], 1)
    lift_hidden = jnp.einsum("bfn,fh->bhn", lift_input, lift_in, preferred_element_type=jnp.float32)
    lifted = gelu_tanh(lift_hidden).astype(jnp.bfloat16)
    hidden_state = jnp.einsum(
        "bhn,hc->bcn", lifted, lift_out, preferred_element_type=jnp.float32
    ).astype(jnp.bfloat16)
    for layer_idx in range(LAYERS):
        zspec = jnp.dot(hidden_state.reshape(-1, NZ), z_forward, preferred_element_type=jnp.float32)
        zspec = zspec.astype(jnp.bfloat16).reshape(batches * C * planes, NY, 2, MZ)
        yz_spec = jnp.einsum(
            "aypk,ypqj->aqjk", zspec, y_forward, preferred_element_type=jnp.float32
        )
        yz_spec = yz_spec.astype(jnp.bfloat16).reshape(batches, C, planes, 2, MY * MZ)
        mode_weights = spec_weight[layer_idx].reshape(block, C, MX, 2, C)
        spectrum = jnp.einsum(
            "bcxpm,xpqi->bcqim",
            lax.all_to_all(yz_spec, "space", split_axis=4, concat_axis=2, tiled=True),
            x_forward,
            preferred_element_type=jnp.float32,
        ).astype(jnp.bfloat16)
        products = jnp.einsum(
            "bcqim,mcipo->bimqpo", spectrum, mode_weights, preferred_element_type=jnp.float32
        )
        real_part = products[:, :, :, 0, 0] - products[:, :, :, 1, 1]
        imag_part = products[:, :, :, 0, 1] + products[:, :, :, 1, 0]
        mixed_modes = jnp.stack([real_part, imag_part], 3).astype(jnp.bfloat16)
        back_field = jnp.einsum(
            "bimqo,iqpx->boxpm", mixed_modes, x_inverse, preferred_element_type=jnp.float32
        ).astype(jnp.bfloat16)
        returned = lax.all_to_all(back_field, "space", split_axis=2, concat_axis=4, tiled=True)
        returned = returned.reshape(batches * C * planes, 2, MY, MZ)
        y_back = jnp.einsum(
            "aqjk,jqpy->aypk", returned, y_inverse, preferred_element_type=jnp.float32
        ).astype(jnp.bfloat16)
        spectral = jnp.dot(
            y_back.reshape(-1, 2 * MZ), z_inverse, preferred_element_type=jnp.float32
        ).reshape(batches, C, cell_count)
        local_term = jnp.einsum(
            "bcn,co->bon", hidden_state, point_weight[layer_idx], preferred_element_type=jnp.float32
        )
        hidden_state = gelu_tanh(spectral + local_term).astype(jnp.bfloat16)
    decoded = gelu_tanh(
        jnp.einsum("bcn,cd->bdn", hidden_state, dec_in, preferred_element_type=jnp.float32)
    ).astype(jnp.bfloat16)
    decoded_out = jnp.einsum("bdn,de->ben", decoded, dec_out, preferred_element_type=jnp.float32)
    pressure = decoded_out[:, 0].reshape(batches, planes, NY, NZ)
    saturation = jax.nn.sigmoid(decoded_out[:, 1]).reshape(batches, planes, NY, NZ)
    states = jnp.stack([pressure, saturation], 1)
    conduct = mobility_of(saturation, log_perm)
    return (states, darcy(pressure, conduct, well_cells, well_rates))


BF = jnp.bfloat16
F32 = jnp.float32
PAIRS = NY // 2
SKEW = 4
PITCH = PAIRS + SKEW
MODE_STEP = 8
ROWS = 8
LOOK = 4
LAG = 1
MID = 3
TB = 2
FB = 4
LANES = 128


def np_waves(length, kept, one_sided):
    index = np.arange(kept)
    freqs = index if one_sided else np.where(index < kept // 2, index, length - kept + index)
    angles = (freqs[:, None] * np.arange(length)[None, :] % length) * (2.0 * math.pi / length)
    norm = 1.0 / math.sqrt(length)
    return np.cos(angles) * norm, np.sin(angles) * norm


def np_forward(length, kept):
    cosine, sine = np_waves(length, kept, False)
    return np.stack([np.stack([cosine.T, -sine.T], 1), np.stack([sine.T, cosine.T], 1)], 1)


def np_inverse(length, kept):
    cosine, sine = np_waves(length, kept, False)
    return np.stack([np.stack([cosine, sine], 1), np.stack([-sine, cosine], 1)], 1)


def by_plane(table, axis, count):
    planes = NX // count
    order = np.arange(NX).reshape(count, planes).T.reshape(-1)
    return np.take(table, order, axis)


def tables_for(count):
    own = MY // count
    cosine, sine = np_waves(NZ, MZ, True)
    twice = np.where(np.arange(MZ) == 0, 1.0, 2.0)[:, None]
    z_forward = np.concatenate([cosine.T, -sine.T], 1)
    z_inverse = np.concatenate([twice * cosine, -twice * sine], 0)
    y_forward = np_forward(NY, MY).reshape(PAIRS, 2, 2, 2, count, own)
    y_inverse = np_inverse(NY, MY).reshape(count, own, 2, 2, PAIRS, 2)
    four = np.eye(4)
    z_forward = np.einsum("zpk,cd->czpdk", z_forward.reshape(NZ, 2, MZ), four)
    z_inverse = np.einsum("pkz,cd->pckdz", z_inverse.reshape(2, MZ, NZ), four)
    tables = {
        "zf": z_forward.reshape(4 * NZ, 8 * MZ),
        "zi": 0.5 * z_inverse.reshape(8 * MZ, 4 * NZ),
        "yf": y_forward.transpose(3, 5, 4, 1, 2, 0).reshape(2 * MY, 2 * NY),
        "yi": y_inverse.transpose(5, 3, 4, 2, 1, 0).reshape(2 * NY, 2 * MY),
        "xf": by_plane(np_forward(NX, MX).transpose(2, 3, 1, 0), 3, count).reshape(2 * MX, 2 * NX),
        "xi": by_plane(np_inverse(NX, MX).transpose(2, 3, 0, 1), 1, count).reshape(2 * NX, 2 * MX),
    }
    halves = tables["xi"].reshape(2, NX // count, 2, count // 2, 2 * MX)
    tables["xh"] = halves.transpose(2, 0, 1, 3, 4).reshape(2, NX, 2 * MX)
    return {name: jnp.asarray(table.astype(np.float32)).astype(BF) for name, table in tables.items()}


def dot32(a, b):
    return jnp.dot(a, b, preferred_element_type=F32)


def gelu_of_half(values):
    u = values.astype(BF)
    scale = math.sqrt(2.0 / math.pi)
    inner = u * (BF(2.0 * scale) + BF(8.0 * scale * 0.044715) * (u * u))
    return u + u * jnp.tanh(inner)


def send_plane(me, count, plane, send, recv, send_sem, recv_sem):
    for shift in range(1, count):
        target = lax.rem(me + shift, count)
        pltpu.make_async_remote_copy(
            src_ref=send.at[plane, target],
            dst_ref=recv.at[plane, me],
            send_sem=send_sem.at[plane],
            recv_sem=recv_sem.at[plane],
            device_id={"space": target},
            device_id_type=pl.DeviceIdType.MESH,
        ).start()
    recv[plane, me] = send[plane, me]


def wait_plane(parts, plane, buffer, sem):
    part = buffer.at[plane, pl.ds(0, parts)]
    pltpu.make_async_copy(part, part, sem.at[plane]).wait()


def to_modes(plane, count, zf_ref, yf_ref, zs, flat, send):
    tiles = C * MZ // LANES
    slots = 2 * MY // count * tiles
    halves = {}
    for first in range(0, tiles, 2 * TB):
        some = [(group, y2) for group in range(first, first + 2 * TB) for y2 in range(2)]
        left = [
            jnp.concatenate(
                [zs[y2, pl.ds((group * 4 + r) * PITCH, PAIRS), :] for r in range(4)], 1
            ).astype(BF)
            for group, y2 in some
        ]
        waves = dot32(jnp.concatenate(left, 0), zf_ref[...]).astype(BF)
        for n, key in enumerate(some):
            halves[key] = waves[n * PAIRS : (n + 1) * PAIRS, :]
    for pair in range(tiles // 2):
        columns = []
        for group in (pair * 2, pair * 2 + 1):
            parts = [
                halves[group, y2][:, p * LANES : (p + 1) * LANES] for y2 in range(2) for p in range(2)
            ]
            columns.append(jnp.concatenate(parts, 0))
        modes = dot32(yf_ref[...], jnp.concatenate(columns, 1))
        for s in range(2 * MY // count):
            for half in range(2):
                flat[pl.ds(s * tiles + pair * 2 + half, count, stride=slots + SKEW), :] = modes[
                    s * count : (s + 1) * count, half * LANES : (half + 1) * LANES
                ]
    for dst in range(count):
        send[plane, dst] = flat[pl.ds(dst * (slots + SKEW), slots), :].astype(BF)


def lay_out(zs, start, values):
    for y2 in range(2):
        for r in range(ROWS):
            zs[y2, pl.ds(start + r, C, stride=PITCH), :] = values[
                r * C : (r + 1) * C, y2 * NZ : (y2 + 1) * NZ
            ]


def hid_rows(index):
    return pl.ds(index * ROWS * C, ROWS * C)


def lift_plane(plane, feat_ref, perm_ref, in_ref, lo_ref, hid, plain, xs, zs):
    for f in range(FIN + 1):
        plain[...] = perm_ref[0, plane] if f == FIN else feat_ref[0, f, plane].astype(F32)
        for y2 in range(2):
            xs[y2, pl.ds(f, PAIRS, stride=8), :] = plain[pl.ds(y2, PAIRS, stride=2), :]
    width = lo_ref.shape[1]
    parts = in_ref.shape[0] // width
    total = PAIRS // ROWS * parts

    def first(n):
        u, r = n // parts, n % parts
        x = jnp.concatenate([xs[y2, pl.ds(u * ROWS * 8, ROWS * 8), :] for y2 in range(2)], 1)
        return dot32(in_ref[r * width : (r + 1) * width, :], x.astype(BF))

    ahead = {n: first(n) for n in range(LOOK)}
    raw = {}

    def finish(n):
        if n % parts == parts - 1:
            u = n // parts
            hidden = jnp.concatenate([raw.pop(u * parts + r) for r in range(parts)], 0)
            hid[plane, hid_rows(u), :] = hidden.astype(BF)
            lay_out(zs, u * ROWS, hidden)

    for n in range(total):
        if n + LOOK < total:
            ahead[n + LOOK] = first(n + LOOK)
        raw[n] = dot32(lo_ref[...], gelu_of_half(ahead.pop(n)))
        if n >= LAG:
            finish(n - LAG)
    for n in range(total - LAG, total):
        finish(n)


def from_modes(plane, count, recv, yi_ref, zi_ref, flat, sp):
    tiles = C * MZ // LANES
    slots = 2 * MY // count * tiles
    for src in range(count):
        flat[pl.ds(src * (slots + SKEW), slots), :] = recv[plane, src].astype(F32)

    def back_of(pair):
        rows = []
        for s in range(2 * MY // count):
            part = [
                flat[pl.ds(s * tiles + pair * 2 + half, count, stride=slots + SKEW), :]
                for half in range(2)
            ]
            rows.append(jnp.concatenate(part, 1))
        return dot32(yi_ref[...], jnp.concatenate(rows, 0).astype(BF)).astype(BF)

    for first in range(0, tiles // 2, FB):
        left, some = [], []
        for pair in range(first, first + FB):
            back = back_of(pair)
            for half in range(2):
                lanes = slice(half * LANES, (half + 1) * LANES)
                for y2 in range(2):
                    parts = [
                        back[(y2 * 2 + p) * PAIRS : (y2 * 2 + p + 1) * PAIRS, lanes] for p in range(2)
                    ]
                    left.append(jnp.concatenate(parts, 1))
                    some.append(((pair * 2 + half) * 4, y2))
        field = dot32(jnp.concatenate(left, 0), zi_ref[...])
        for n, (o, y2) in enumerate(some):
            for r in range(4):
                sp[y2, pl.ds(o + r, PAIRS, stride=C + SKEW), :] = field[
                    n * PAIRS : (n + 1) * PAIRS, r * NZ : (r + 1) * NZ
                ]


def field_rows(index, sp):
    halves = []
    for y2 in range(2):
        rows = [sp[y2, pl.ds((index * ROWS + r) * (C + SKEW), C), :] for r in range(ROWS)]
        halves.append(jnp.concatenate(rows, 0))
    return jnp.concatenate(halves, 1)


def middle_plane(plane, kp, hid, sp, zs):
    total = PAIRS // ROWS

    def local_term(index):
        return dot32(kp[...], hid[plane, hid_rows(index), :])

    ahead = {n: local_term(n) for n in range(MID)}
    for n in range(total):
        if n + MID < total:
            ahead[n + MID] = local_term(n + MID)
        hidden = gelu_of_half(ahead.pop(n) + field_rows(n, sp))
        hid[plane, hid_rows(n), :] = hidden
        lay_out(zs, n * ROWS, hidden.astype(F32))


def final_plane(plane, kp, di_ref, do_ref, perm_ref, hid, sp, st_ref):
    total = PAIRS // ROWS
    width = di_ref.shape[1]
    parts = di_ref.shape[0] // width

    def local_term(index):
        return dot32(kp[...], hid[plane, hid_rows(index), :])

    def mixed(n):
        return gelu_of_half(ahead.pop(n) + field_rows(n, sp))

    def decode(hidden, r):
        return dot32(di_ref[r * width : (r + 1) * width, :], hidden)

    def shrink(n, r):
        return dot32(do_ref[:, r * width : (r + 1) * width], gelu_of_half(raw.pop((n, r))))

    ahead = {n: local_term(n) for n in range(MID)}
    raw = {}
    hiddens = {0: mixed(0)}
    for r in range(parts):
        raw[0, r] = decode(hiddens[0], r)
    hiddens[1] = mixed(1)
    for n in range(total):
        if n + MID < total:
            ahead[n + MID] = local_term(n + MID)
        both = 0.0
        for r in range(parts):
            if n + 1 < total:
                raw[n + 1, r] = decode(hiddens[n + 1], r)
            both = both + shrink(n, r)
            if r == 0 and n + 2 < total:
                hiddens[n + 2] = mixed(n + 2)
        for y2 in range(2):
            lanes = slice(y2 * NZ, (y2 + 1) * NZ)
            where = pl.ds(n * ROWS * 2 + y2, ROWS, stride=2)
            st_ref[0, 0, plane, where, :] = both[:ROWS, lanes]
            st_ref[0, 1, plane, where, :] = both[ROWS:, lanes]

def residual_plane(plane, me, planes, perm_ref, cells, rates, ends, st_ref, res_ref, cond):
    sat = jax.nn.sigmoid(st_ref[0, 1, plane])
    st_ref[0, 1, plane] = sat
    conduct = mobility_of(sat, perm_ref[0, plane])
    cond[plane] = conduct
    pressure = st_ref[0, 0, plane]
    flux = 0.0
    for axis in range(2):
        length = pressure.shape[axis]
        inner = lax.broadcasted_iota(jnp.int32, pressure.shape, axis) < length - 1
        beyond = (pltpu.roll(field, length - 1, axis) for field in (conduct, pressure))
        cond_next, press_next = beyond
        face = jnp.where(inner, face_term(conduct, cond_next, pressure, press_next), 0.0)
        flux = flux + face - pltpu.roll(face, 1, axis)
    shape = (NY, cells.shape[1])
    here = cells[...] - (me * planes + plane) * (NY * NZ)
    starts = lax.broadcasted_iota(jnp.int32, shape, 0) * NZ
    offset = here - starts
    hit = (offset >= 0) & (offset < NZ)
    left = jnp.where(hit, rates[...], 0.0).astype(BF)
    dims = (((1,), (1,)), ((), ()))
    source = lax.dot_general(left, ends[...], dims, preferred_element_type=F32)
    res_ref[0, plane] = flux - source


def add_face(plane, st_ref, res_ref, cond):
    face = face_term(cond[plane], cond[plane + 1], st_ref[0, 0, plane], st_ref[0, 0, plane + 1])
    res_ref[0, plane] = res_ref[0, plane] + face
    res_ref[0, plane + 1] = res_ref[0, plane + 1] - face


def edge_copy(me, count, side, edge_send, edge_recv, es_sem, er_sem):
    return pltpu.make_async_remote_copy(
        src_ref=edge_send.at[side],
        dst_ref=edge_recv.at[1 - side],
        send_sem=es_sem.at[side],
        recv_sem=er_sem.at[1 - side],
        device_id={"space": lax.rem(me + (1 if side else count - 1), count)},
        device_id_type=pl.DeviceIdType.MESH,
    )


def wells_of(cells_ref, rates_ref, cells, rates, ends):
    rate = rates_ref[...]
    high = rate.astype(BF).astype(F32)
    middle = (rate - high).astype(BF).astype(F32)
    for n, part in enumerate((high, middle, rate - high - middle)):
        lanes = slice(n * WELLS, (n + 1) * WELLS)
        cells[:, lanes] = cells_ref[...]
        rates[:, lanes] = part
    column = lax.broadcasted_iota(jnp.int32, ends.shape, 0)
    ends[...] = jnp.where((cells[...] & (NZ - 1)) == column, 1.0, 0.0).astype(BF)


def mix_modes(planes, count, recv, wbuf, xf_ref, flat, spec, rows, mixed, turned):
    own = MY // count
    tiles = C * MZ // LANES
    slots = 2 * own * tiles
    pitch = slots + SKEW
    every = count * planes
    lane = lax.broadcasted_iota(jnp.int32, (1, LANES), 1)
    low = lane < 64
    even = lane % 64 < 32

    def unpack(plane, carry):
        for src in range(count):
            start = (plane * count + src) * pitch
            flat[pl.ds(start, slots), :] = recv[plane, src].astype(F32)
        return carry

    lax.fori_loop(0, planes, unpack, 0)

    def column(p, t):
        return flat[pl.ds(p * own * tiles + t, every, stride=pitch), :].astype(BF)

    for pair in range(own * tiles // 2):
        right = jnp.concatenate(
            [
                jnp.concatenate([column(p, pair * 2 + half) for half in range(2)], 1)
                for p in range(2)
            ],
            0,
        )
        total = dot32(xf_ref[...], right)
        for half in range(2):
            part = total[:, half * LANES : (half + 1) * LANES].T
            for r in range(4):
                first = (pair * 2 + half) * 4 + r
                spec[pl.ds(first * (MZ + SKEW), MZ), : 2 * MX] = part[r * MZ : (r + 1) * MZ, :]
    groups = own * MZ // MODE_STEP
    for group in range(groups):
        jj, k = group * MODE_STEP // MZ, group * MODE_STEP % MZ
        base = jj * C * (MZ + SKEW) + k
        picked = [
            spec[pl.ds(base + r, C, stride=MZ + SKEW), : 2 * MX] for r in range(MODE_STEP)
        ]
        rows[group] = jnp.concatenate(picked, 0).T
    wide = MODE_STEP * C
    own_mode = lax.broadcasted_iota(jnp.int32, (MODE_STEP, wide), 0) == (
        lax.broadcasted_iota(jnp.int32, (MODE_STEP, wide), 1) // C
    )
    per = wide // (2 * C)

    def step(group, carry):
        first = pl.multiple_of(group * MODE_STEP, MODE_STEP)
        for piece in range(MX // per):
            left = []
            for i in range(per):
                for q in range(2):
                    row = rows[group, pl.ds(q * MX + piece * per + i, MODE_STEP, stride=0), :]
                    left.append(jnp.where(own_mode, row, 0.0))
            lo = piece * wide
            weights = wbuf[pl.ds(first, MODE_STEP), :, lo : lo + wide].reshape(wide, wide)
            both = dot32(jnp.concatenate(left, 0).astype(BF), weights)

            def part(i, q, t):
                at = (i * 2 + q) * MODE_STEP
                return both[at : at + MODE_STEP, t * LANES : (t + 1) * LANES]

            for t in range(2):
                real, imag = (
                    jnp.where(low, part(2 * t, q, t), part(2 * t + 1, q, t)) for q in range(2)
                )
                turn = jnp.where(even, -pltpu.roll(imag, LANES - C, 1), pltpu.roll(imag, C, 1))
                mixed[pl.ds(first, MODE_STEP), lo + t * LANES : lo + (t + 1) * LANES] = real + turn
        return carry

    lax.fori_loop(0, groups, step, 0)
    for block in range(MX * 2 * C // LANES):
        part = mixed[:, block * LANES : (block + 1) * LANES].T
        for r in range(4):
            first = (block * 4 + r) * (C + SKEW)
            turned[pl.ds(first, C), : own * MZ] = part[r * C : (r + 1) * C, :]


def mixed_tile(pair, turned):
    lane = lax.broadcasted_iota(jnp.int32, (1, LANES), 1)
    low = lane < 64
    even = lane % 64 < 32
    right = [[], []]
    for half in range(2):
        o = (pair * 2 + half) * 4
        a = [turned[pl.ds(o + r, 2 * MX, stride=C + SKEW), :] for r in range(4)]
        b = jnp.where(low, a[0], pltpu.roll(a[2], 64, 1))
        c = jnp.where(low, a[1], pltpu.roll(a[3], 64, 1))
        right[0].append(jnp.where(even, b, pltpu.roll(c, 32, 1)))
        right[1].append(jnp.where(even, pltpu.roll(b, LANES - 32, 1), c))
    return [jnp.concatenate(part, 1).astype(BF) for part in right]


def to_planes(table, tile, jj, pair, count, flat):
    own = MY // count
    tiles = C * MZ // LANES
    pitch = 2 * own * tiles + SKEW
    back = dot32(table, tile)
    every = back.shape[0] // 2
    for p in range(2):
        for half in range(2):
            slot = (p * own + jj) * tiles + pair * 2 + half
            flat[pl.ds(slot, every, stride=pitch), :] = back[
                p * every : (p + 1) * every, half * LANES : (half + 1) * LANES
            ]


def pack_planes(planes, count, first, targets, flat, send):
    slots = 2 * MY // count * C * MZ // LANES
    pitch = slots + SKEW

    def pack(plane, carry):
        for dst in range(targets):
            start = (plane * targets + dst) * pitch
            send[plane, first + dst] = flat[pl.ds(start, slots), :].astype(BF)
        return carry

    lax.fori_loop(0, planes, pack, 0)


def send_half(me, count, plane, other, send, recv, send_sem, recv_sem):
    near = count // 2
    owner = lax.rem(me + other * near, count)
    for shift in range(1, near):
        place = lax.rem(me + shift, near)
        pltpu.make_async_remote_copy(
            src_ref=send.at[plane, other * near + place],
            dst_ref=recv.at[plane, owner],
            send_sem=send_sem.at[plane],
            recv_sem=recv_sem.at[plane],
            device_id={"space": me // near * near + place},
            device_id_type=pl.DeviceIdType.MESH,
        ).start()
    recv[plane, owner] = send[plane, other * near + lax.rem(me, near)]


def swap_tile(me, count, n, own, other, send_sem, recv_sem):
    return pltpu.make_async_remote_copy(
        src_ref=own.at[n],
        dst_ref=other.at[n],
        send_sem=send_sem.at[n],
        recv_sem=recv_sem.at[n],
        device_id={"space": lax.rem(me + count // 2, count)},
        device_id_type=pl.DeviceIdType.MESH,
    )


def whole_kernel(
    planes, count, feat_ref, perm_ref, lift_in, lift_out, point, dec_in, dec_out, zf_ref, zi_ref,
    yf_ref, yi_ref, xf_ref, xi_ref, xh_ref, cells_ref, rates_ref, w_hbm, st_ref, res_ref,
    hid, wbuf, send_f, recv_f, send_b, recv_b, flat, spec, rows, mixed, turned, zs, sp, xs, plain,
    in_ref, lo_ref, kp_ref, di_ref, do_ref, cond, cells, rates, ends, edge_send, edge_recv,
    own_mixed, other_mixed,
    w_sem, sf_sem, rf_sem, sb_sem, rb_sem, es_sem, er_sem, om_sem, rm_sem,
):
    me = lax.axis_index("space")
    barrier = pltpu.get_barrier_semaphore()
    for shift in range(1, count):
        pl.semaphore_signal(
            barrier,
            inc=1,
            device_id={"space": lax.rem(me + shift, count)},
            device_id_type=pl.DeviceIdType.MESH,
        )
    fetch = pltpu.make_async_copy(w_hbm.at[0], wbuf, w_sem.at[0])
    fetch.start()
    xs[...] = jnp.zeros_like(xs)
    in_ref[...] = diag_of(lift_in[...], ROWS, 8, 0.5)
    lo_ref[...] = diag_of(lift_out[...], 2, lift_out.shape[1], 1.0, True)
    for layer in range(LAYERS):
        kp_ref[layer] = diag_of(point[layer], ROWS, C, 0.5)
    di_ref[...] = diag_of(dec_in[...], ROWS, C, 0.5)
    dec = dec_out.shape[1]
    do_ref[...] = spread(
        dec_out[...],
        2 * ROWS,
        ROWS * dec,
        lambda i: i // ROWS,
        lambda j: j % dec,
        lambda i, j: i % ROWS == j // dec,
        1.0,
        True,
    )
    wells_of(cells_ref, rates_ref, cells, rates, ends)
    pl.semaphore_wait(barrier, count - 1)

    def over(body):
        def run(plane, carry):
            body(plane)
            return carry

        lax.fori_loop(0, planes, run, 0)

    def lift(plane):
        lift_plane(plane, feat_ref, perm_ref, in_ref, lo_ref, hid, plain, xs, zs)
        to_modes(plane, count, zf_ref, yf_ref, zs, flat, send_f)
        send_plane(me, count, plane, send_f, recv_f, sf_sem, rf_sem)

    over(lift)
    for layer in range(LAYERS):
        fetch.wait()
        over(lambda plane: wait_plane(count - 1, plane, recv_f, rf_sem))
        over(lambda plane: wait_plane(count - 1, plane, send_f, sf_sem))
        mix_modes(planes, count, recv_f, wbuf, xf_ref, flat, spec, rows, mixed, turned)
        if layer + 1 < LAYERS:
            fetch = pltpu.make_async_copy(w_hbm.at[layer + 1], wbuf, w_sem.at[layer + 1])
            fetch.start()
        last = layer + 1 == LAYERS

        def turn(index):
            return lax.rem(planes - index, planes) if last else index

        pairs = [(pair, jj) for pair in range(C * MZ // LANES // 2) for jj in range(MY // count)]
        if last:
            parts = count - 1
            for pair, jj in pairs:
                if jj == 0:
                    tile = mixed_tile(pair, turned)
                to_planes(xi_ref[...], tile[jj], jj, pair, count, flat)
            pack_planes(planes, count, 0, count, flat, send_b)
            over(lambda n: send_plane(me, count, turn(n), send_b, recv_b, sb_sem, rb_sem))
        else:
            near = count // 2
            parts = 2 * (near - 1)
            swaps = [
                swap_tile(me, count, n, own_mixed, other_mixed, om_sem, rm_sem)
                for n in range(len(pairs))
            ]
            for n, (pair, jj) in enumerate(pairs):
                if jj == 0:
                    tile = mixed_tile(pair, turned)
                own_mixed[n] = tile[jj]
                swaps[n].start()
            table = xh_ref.at[me // near]
            for other in range(2):
                for n, (pair, jj) in enumerate(pairs):
                    if other:
                        swaps[n].wait_recv()
                    tile = other_mixed[n] if other else own_mixed[n]
                    to_planes(table[...], tile, jj, pair, count, flat)
                pack_planes(planes, count, other * near, near, flat, send_b)
                over(lambda n: send_half(me, count, n, other, send_b, recv_b, sb_sem, rb_sem))
            for swap in swaps:
                swap.wait_send()
        kp = kp_ref.at[layer]

        def rest(index):
            plane = turn(index)
            wait_plane(parts, plane, recv_b, rb_sem)
            from_modes(plane, count, recv_b, yi_ref, zi_ref, flat, sp)
            if not last:
                middle_plane(plane, kp, hid, sp, zs)
                to_modes(plane, count, zf_ref, yf_ref, zs, flat, send_f)
                send_plane(me, count, plane, send_f, recv_f, sf_sem, rf_sem)
            else:
                final_plane(plane, kp, di_ref, do_ref, perm_ref, hid, sp, st_ref)
                residual_plane(
                    plane, me, planes, perm_ref, cells, rates, ends, st_ref, res_ref, cond
                )

                @pl.when(index == 1)
                def _():
                    for side in range(2):
                        edge_send[side, 0] = st_ref[0, 0, side * (planes - 1)].astype(BF)
                        edge_send[side, 1] = cond[side * (planes - 1)].astype(BF)
                        edge_copy(me, count, side, edge_send, edge_recv, es_sem, er_sem).start()

                @pl.when(index >= 2)
                def _():
                    add_face(plane, st_ref, res_ref, cond)

        over(rest)
        over(lambda plane: wait_plane(parts, plane, send_b, sb_sem))
    add_face(0, st_ref, res_ref, cond)
    for side in range(2):
        edge_copy(me, count, side, edge_send, edge_recv, es_sem, er_sem).wait()
    for side in range(2):
        plane = side * (planes - 1)
        press, conduct = (edge_recv[side, n].astype(F32) for n in range(2))
        face = face_term(cond[plane], conduct, st_ref[0, 0, plane], press)
        inside = me < count - 1 if side else me > 0
        res_ref[0, plane] = res_ref[0, plane] + jnp.where(inside, face, 0.0)


def ones_where(shape, test, value=1.0):
    row = lax.broadcasted_iota(jnp.int32, shape, 0)
    col = lax.broadcasted_iota(jnp.int32, shape, 1)
    return jnp.where(test(row, col), value, 0.0)


def spread(matrix, rows, cols, row_of, col_of, keep, value, turned):
    depth, height = matrix.shape[::-1] if turned else matrix.shape
    take = ones_where((rows, height), lambda i, j: row_of(i) == j).astype(BF)
    put = ones_where((depth, cols), lambda i, j: col_of(j) == i).astype(BF)
    dims = (((1,), (0 if turned else 1,)), ((), ()))
    part = lax.dot_general(take, matrix, dims, preferred_element_type=F32)
    return (dot32(part.astype(BF), put) * ones_where((rows, cols), keep, value)).astype(BF)


def diag_of(matrix, copies, width, value, turned=False):
    height = matrix.shape[0 if turned else 1]
    return spread(
        matrix,
        copies * height,
        copies * width,
        lambda i: i % height,
        lambda j: j % width,
        lambda i, j: i // height == j // width,
        value,
        turned,
    )


def local_fast(
    features,
    log_perm,
    well_cells,
    well_rates,
    lift_in,
    lift_out,
    spec_weight,
    point_weight,
    dec_in,
    dec_out,
):
    planes = features.shape[2]
    count = lax.axis_size("space")
    own = MY // count
    modes = own * MZ
    slots = 2 * modes * C // LANES
    tables = tables_for(count)
    lift, dec = lift_in.shape[1], dec_in.shape[1]
    operands = (
        features,
        log_perm,
        lift_in,
        lift_out.T,
        point_weight,
        dec_in,
        dec_out.T,
    ) + tuple(tables[name] for name in ("zf", "zi", "yf", "yi", "xf", "xi", "xh"))
    operands = operands + (well_cells, well_rates)
    vmem = pl.BlockSpec(memory_space=pltpu.VMEM)
    exchange = pltpu.VMEM((planes, count, slots, LANES), BF)
    results = pl.pallas_call(
        lambda *refs: whole_kernel(planes, count, *refs),
        in_specs=[vmem] * len(operands) + [pl.BlockSpec(memory_space=pl.ANY)],
        out_specs=[vmem, vmem],
        out_shape=[
            jax.ShapeDtypeStruct((1, 2, planes, NY, NZ), F32),
            jax.ShapeDtypeStruct((1, planes, NY, NZ), F32),
        ],
        scratch_shapes=[
            pltpu.VMEM((planes, PAIRS * C, 2 * NZ), BF),
            pltpu.VMEM(spec_weight.shape[1:], BF),
            exchange,
            exchange,
            exchange,
            exchange,
            pltpu.VMEM((planes * count * (slots + SKEW), LANES), F32),
            pltpu.VMEM((own * C * (MZ + SKEW), LANES), F32),
            pltpu.VMEM((modes // MODE_STEP, 2 * MX, MODE_STEP * C), F32),
            pltpu.VMEM((modes, MX * 2 * C), F32),
            pltpu.VMEM((2 * MX * (C + SKEW), LANES), F32),
            pltpu.VMEM((2, C * PITCH, LANES), F32),
            pltpu.VMEM((2, PAIRS * (C + SKEW), LANES), F32),
            pltpu.VMEM((2, PAIRS * 8, NZ), F32),
            pltpu.VMEM((NY, NZ), F32),
            pltpu.VMEM((ROWS * lift, ROWS * 8), BF),
            pltpu.VMEM((2 * C, 2 * lift), BF),
            pltpu.VMEM((LAYERS, ROWS * C, ROWS * C), BF),
            pltpu.VMEM((ROWS * dec, ROWS * C), BF),
            pltpu.VMEM((2 * ROWS, ROWS * dec), BF),
            pltpu.VMEM((planes, NY, NZ), F32),
            pltpu.VMEM((1, 3 * WELLS), jnp.int32),
            pltpu.VMEM((1, 3 * WELLS), F32),
            pltpu.VMEM((NZ, 3 * WELLS), BF),
            pltpu.VMEM((2, 2, NY, NZ), BF),
            pltpu.VMEM((2, 2, NY, NZ), BF),
            pltpu.VMEM((modes * C // 256, 2 * MX, 256), BF),
            pltpu.VMEM((modes * C // 256, 2 * MX, 256), BF),
            pltpu.SemaphoreType.DMA((LAYERS,)),
        ]
        + [pltpu.SemaphoreType.DMA((planes,))] * 4
        + [pltpu.SemaphoreType.DMA((2,))] * 2
        + [pltpu.SemaphoreType.DMA((modes * C // 256,))] * 2,
        compiler_params=pltpu.CompilerParams(
            collective_id=0, has_side_effects=True, vmem_limit_bytes=60 * 1024 * 1024
        ),
        name="whole",
    )(*operands, spec_weight)
    return handed_on(results)


def handed_on(results):
    pieces = [
        (n, at) for n, each in enumerate(results) for at in np.ndindex(*each.shape[:-2])
    ]

    def body(*refs):
        source, target, held = refs[:2], refs[2:4], refs[4:6]
        in_sem, out_sem = refs[6:]
        loads = [
            pltpu.make_async_copy(source[n].at[at], held[n].at[at], in_sem.at[k])
            for k, (n, at) in enumerate(pieces)
        ]
        stores = [
            pltpu.make_async_copy(held[n].at[at], target[n].at[at], out_sem.at[k])
            for k, (n, at) in enumerate(pieces)
        ]
        for load in loads:
            load.start()
        for load, store in zip(loads, stores):
            load.wait()
            store.start()
        for store in stores:
            store.wait()

    whole = pl.BlockSpec(memory_space=pl.ANY)
    return pl.pallas_call(
        body,
        in_specs=[whole] * 2,
        out_specs=[whole] * 2,
        out_shape=[jax.ShapeDtypeStruct(each.shape, each.dtype) for each in results],
        scratch_shapes=[pltpu.VMEM(each.shape, each.dtype) for each in results]
        + [pltpu.SemaphoreType.DMA((len(pieces),))] * 2,
        compiler_params=pltpu.CompilerParams(vmem_limit_bytes=60 * 1024 * 1024),
        name="handed_on",
    )(*results)


def local(features, log_perm, well_cells, well_rates, lift_in, lift_out, spec_weight, *rest):
    batches, planes = features.shape[0], features.shape[2]
    count = lax.axis_size("space")
    fits = batches == 1 and planes == 8 and count % 8 == 0 and MY == 2 * count
    run = local_fast if fits else local_general
    return run(
        features, log_perm, well_cells, well_rates, lift_in, lift_out, spec_weight, *rest
    )


def solution(mesh):
    return jax.shard_map(
        local,
        mesh=mesh,
        in_specs=(
            P("sample", None, "space", None, None),
            P("sample", "space", None, None),
            P("sample", None),
            P("sample", None),
            P(),
            P(),
            P(None, "space", None, None),
            P(),
            P(),
            P(),
        ),
        out_specs=(P("sample", None, "space", None, None), P("sample", "space", None, None)),
        check_vma=False,
    )
```

```python
import math

import jax
import jax.numpy as jnp
import numpy as np
from jax import lax
from jax.experimental import pallas as pl
from jax.experimental.pallas import tpu as pltpu
from jax.sharding import PartitionSpec as P

NX = 128
NY = 128
NZ = 128
MX = 32
MY = 32
MZ = 32
C = 32
FIN = 4
LAYERS = 2
WELLS = 32


def padded_2(block, sides, width):
    for axis, dim in sides:
        count = lax.axis_size(axis)
        forward = [(i, i + 1) for i in range(count - 1)]
        backward = [(target, source) for source, target in forward]
        low = lax.ppermute(
            lax.slice_in_dim(block, block.shape[dim] - width, None, axis=dim), axis, forward
        )
        high = lax.ppermute(lax.slice_in_dim(block, 0, width, axis=dim), axis, backward)
        block = jnp.concatenate([low, block, high], axis=dim)
    return block


def freq_table(length, kept, one_sided):
    indices = jnp.arange(kept, dtype=jnp.int32)
    if one_sided:
        return indices
    return jnp.where(indices < kept // 2, indices, length - kept + indices)


def wave_parts(length, kept, one_sided):
    freqs = freq_table(length, kept, one_sided)
    places = jnp.arange(length, dtype=jnp.int32)
    phase_turns = freqs[:, None] * places[None, :] % length
    angles = phase_turns.astype(jnp.float32) * (2.0 * math.pi / length)
    norm_scale = 1.0 / math.sqrt(length)
    return (jnp.cos(angles) * norm_scale, jnp.sin(angles) * norm_scale)


def forward_table(length, kept):
    cosine_vals, sine_vals = wave_parts(length, kept, False)
    return jnp.stack(
        [jnp.stack([cosine_vals.T, -sine_vals.T], 1), jnp.stack([sine_vals.T, cosine_vals.T], 1)], 1
    ).astype(jnp.bfloat16)


def inverse_table(length, kept):
    cosine_vals, sine_vals = wave_parts(length, kept, False)
    return jnp.stack(
        [jnp.stack([cosine_vals, sine_vals], 1), jnp.stack([-sine_vals, cosine_vals], 1)], 1
    ).astype(jnp.bfloat16)


def z_tables():
    cosine_vals, sine_vals = wave_parts(NZ, MZ, True)
    weights_k = jnp.where(jnp.arange(MZ) == 0, 1.0, 2.0).astype(jnp.float32)[:, None]
    z_forward = jnp.concatenate([cosine_vals.T, -sine_vals.T], 1).astype(jnp.bfloat16)
    z_inverse = jnp.concatenate([weights_k * cosine_vals, -weights_k * sine_vals], 0).astype(
        jnp.bfloat16
    )
    return (z_forward, z_inverse)


def gelu_tanh(values):
    return jax.nn.gelu(values, approximate=True)


def face_term(cond_a, cond_b, press_a, press_b):
    return 2.0 * cond_a * cond_b / (cond_a + cond_b) * (press_a - press_b)


def mobility_of(saturation, log_values):
    return jnp.exp(log_values) * (
        saturation * saturation + 0.5 * (1.0 - saturation) * (1.0 - saturation)
    )


def darcy(pressure, conduct, well_cells, well_rates):
    batches, planes = pressure.shape[0], pressure.shape[1]
    space_index = lax.axis_index("space")
    pad_cond = jnp.pad(conduct, ((0, 0), (0, 0), (1, 1), (1, 1)))
    pad_press = jnp.pad(pressure, ((0, 0), (0, 0), (1, 1), (1, 1)))
    flux_sum = face_term(conduct, pad_cond[:, :, 2:, 1:-1], pressure, pad_press[:, :, 2:, 1:-1])
    flux_sum = flux_sum + face_term(
        conduct, pad_cond[:, :, :-2, 1:-1], pressure, pad_press[:, :, :-2, 1:-1]
    )
    flux_sum = flux_sum + face_term(
        conduct, pad_cond[:, :, 1:-1, 2:], pressure, pad_press[:, :, 1:-1, 2:]
    )
    flux_sum = flux_sum + face_term(
        conduct, pad_cond[:, :, 1:-1, :-2], pressure, pad_press[:, :, 1:-1, :-2]
    )
    fields = jnp.stack([pressure, conduct], 1)
    padded = padded_2(fields.astype(jnp.bfloat16), (("space", 2),), 1).astype(fields.dtype)
    press_low = padded[:, 0, 0]
    press_high = padded[:, 0, -1]
    cond_low = padded[:, 1, 0]
    cond_high = padded[:, 1, -1]
    press_below = jnp.concatenate([press_low[:, None], pressure[:, :-1]], 1)
    cond_below = jnp.concatenate([cond_low[:, None], conduct[:, :-1]], 1)
    press_above = jnp.concatenate([pressure[:, 1:], press_high[:, None]], 1)
    cond_above = jnp.concatenate([conduct[:, 1:], cond_high[:, None]], 1)
    lower_terms = face_term(conduct, cond_below, pressure, press_below)
    upper_terms = face_term(conduct, cond_above, pressure, press_above)
    flux_sum = flux_sum + lower_terms + upper_terms
    well_x = well_cells // (NY * NZ) - space_index * planes
    well_y = well_cells // NZ % NY
    well_z = well_cells % NZ
    onehot_x = (well_x[:, :, None] == jnp.arange(planes, dtype=jnp.int32)[None, None, :]).astype(
        jnp.float32
    ) * well_rates[:, :, None]
    onehot_y = (well_y[:, :, None] == jnp.arange(NY, dtype=jnp.int32)[None, None, :]).astype(
        jnp.float32
    )
    onehot_z = (well_z[:, :, None] == jnp.arange(NZ, dtype=jnp.int32)[None, None, :]).astype(
        jnp.float32
    )
    plane_rows = (onehot_x[:, :, :, None] * onehot_y[:, :, None, :]).reshape(
        batches, WELLS, planes * NY
    )
    source = jnp.einsum(
        "bwa,bwz->baz", plane_rows, onehot_z, precision=lax.Precision.HIGHEST
    ).reshape(batches, planes, NY, NZ)
    return flux_sum - source


def local_general(
    features,
    log_perm,
    well_cells,
    well_rates,
    lift_in,
    lift_out,
    spec_weight,
    point_weight,
    dec_in,
    dec_out,
):
    batches = features.shape[0]
    planes = features.shape[2]
    space_index = lax.axis_index("space")
    block = spec_weight.shape[1]
    cell_count = planes * NY * NZ
    z_forward, z_inverse = z_tables()
    y_forward = forward_table(NY, MY)
    y_inverse = inverse_table(NY, MY)
    x_forward = forward_table(NX, MX)
    x_inverse = inverse_table(NX, MX)
    perm_b = log_perm.astype(jnp.bfloat16).reshape(batches, 1, cell_count)
    lift_input = jnp.concatenate([features.reshape(batches, FIN, cell_count), perm_b], 1)
    lift_hidden = jnp.einsum("bfn,fh->bhn", lift_input, lift_in, preferred_element_type=jnp.float32)
    lifted = gelu_tanh(lift_hidden).astype(jnp.bfloat16)
    hidden_state = jnp.einsum(
        "bhn,hc->bcn", lifted, lift_out, preferred_element_type=jnp.float32
    ).astype(jnp.bfloat16)
    for layer_idx in range(LAYERS):
        zspec = jnp.dot(hidden_state.reshape(-1, NZ), z_forward, preferred_element_type=jnp.float32)
        zspec = zspec.astype(jnp.bfloat16).reshape(batches * C * planes, NY, 2, MZ)
        yz_spec = jnp.einsum(
            "aypk,ypqj->aqjk", zspec, y_forward, preferred_element_type=jnp.float32
        )
        yz_spec = yz_spec.astype(jnp.bfloat16).reshape(batches, C, planes, 2, MY * MZ)
        mode_weights = spec_weight[layer_idx].reshape(block, C, MX, 2, C)
        spectrum = jnp.einsum(
            "bcxpm,xpqi->bcqim",
            lax.all_to_all(yz_spec, "space", split_axis=4, concat_axis=2, tiled=True),
            x_forward,
            preferred_element_type=jnp.float32,
        ).astype(jnp.bfloat16)
        products = jnp.einsum(
            "bcqim,mcipo->bimqpo", spectrum, mode_weights, preferred_element_type=jnp.float32
        )
        real_part = products[:, :, :, 0, 0] - products[:, :, :, 1, 1]
        imag_part = products[:, :, :, 0, 1] + products[:, :, :, 1, 0]
        mixed_modes = jnp.stack([real_part, imag_part], 3).astype(jnp.bfloat16)
        back_field = jnp.einsum(
            "bimqo,iqpx->boxpm", mixed_modes, x_inverse, preferred_element_type=jnp.float32
        ).astype(jnp.bfloat16)
        returned = lax.all_to_all(back_field, "space", split_axis=2, concat_axis=4, tiled=True)
        returned = returned.reshape(batches * C * planes, 2, MY, MZ)
        y_back = jnp.einsum(
            "aqjk,jqpy->aypk", returned, y_inverse, preferred_element_type=jnp.float32
        ).astype(jnp.bfloat16)
        spectral = jnp.dot(
            y_back.reshape(-1, 2 * MZ), z_inverse, preferred_element_type=jnp.float32
        ).reshape(batches, C, cell_count)
        local_term = jnp.einsum(
            "bcn,co->bon", hidden_state, point_weight[layer_idx], preferred_element_type=jnp.float32
        )
        hidden_state = gelu_tanh(spectral + local_term).astype(jnp.bfloat16)
    decoded = gelu_tanh(
        jnp.einsum("bcn,cd->bdn", hidden_state, dec_in, preferred_element_type=jnp.float32)
    ).astype(jnp.bfloat16)
    decoded_out = jnp.einsum("bdn,de->ben", decoded, dec_out, preferred_element_type=jnp.float32)
    pressure = decoded_out[:, 0].reshape(batches, planes, NY, NZ)
    saturation = jax.nn.sigmoid(decoded_out[:, 1]).reshape(batches, planes, NY, NZ)
    states = jnp.stack([pressure, saturation], 1)
    conduct = mobility_of(saturation, log_perm)
    return (states, darcy(pressure, conduct, well_cells, well_rates))


BF = jnp.bfloat16
F32 = jnp.float32
PAIRS = NY // 2
SKEW = 4
PITCH = PAIRS + SKEW
MODE_STEP = 8
SOON = (5, 3)
ROWS = 8
LOOK = 4
LAG = 1
MID = 3
TB = 2
FB = 4
LANES = 128


def np_waves(length, kept, one_sided):
    index = np.arange(kept)
    freqs = index if one_sided else np.where(index < kept // 2, index, length - kept + index)
    angles = (freqs[:, None] * np.arange(length)[None, :] % length) * (2.0 * math.pi / length)
    norm = 1.0 / math.sqrt(length)
    return np.cos(angles) * norm, np.sin(angles) * norm


def np_forward(length, kept):
    cosine, sine = np_waves(length, kept, False)
    return np.stack([np.stack([cosine.T, -sine.T], 1), np.stack([sine.T, cosine.T], 1)], 1)


def np_inverse(length, kept):
    cosine, sine = np_waves(length, kept, False)
    return np.stack([np.stack([cosine, sine], 1), np.stack([-sine, cosine], 1)], 1)


def by_plane(table, axis, count):
    planes = NX // count
    order = np.arange(NX).reshape(count, planes).T.reshape(-1)
    return np.take(table, order, axis)


def tables_for(count):
    own = MY // count
    cosine, sine = np_waves(NZ, MZ, True)
    twice = np.where(np.arange(MZ) == 0, 1.0, 2.0)[:, None]
    z_forward = np.concatenate([cosine.T, -sine.T], 1)
    z_inverse = np.concatenate([twice * cosine, -twice * sine], 0)
    y_forward = np_forward(NY, MY).reshape(PAIRS, 2, 2, 2, count, own)
    y_inverse = np_inverse(NY, MY).reshape(count, own, 2, 2, PAIRS, 2)
    four = np.eye(4)
    z_forward = np.einsum("zpk,cd->czpdk", z_forward.reshape(NZ, 2, MZ), four)
    z_inverse = np.einsum("pkz,cd->pckdz", z_inverse.reshape(2, MZ, NZ), four)
    tables = {
        "zf": z_forward.reshape(4 * NZ, 8 * MZ),
        "zi": 0.5 * z_inverse.reshape(8 * MZ, 4 * NZ),
        "yf": y_forward.transpose(3, 5, 4, 1, 2, 0).reshape(2 * MY, 2 * NY),
        "yi": y_inverse.transpose(5, 3, 4, 2, 1, 0).reshape(2 * NY, 2 * MY),
        "xf": by_plane(np_forward(NX, MX).transpose(2, 3, 1, 0), 3, count).reshape(2 * MX, 2 * NX),
        "xi": by_plane(np_inverse(NX, MX).transpose(2, 3, 0, 1), 1, count).reshape(2 * NX, 2 * MX),
    }
    halves = tables["xi"].reshape(2, NX // count, 2, count // 2, 2 * MX)
    tables["xh"] = halves.transpose(2, 0, 1, 3, 4).reshape(2, NX, 2 * MX)
    return {name: jnp.asarray(table.astype(np.float32)).astype(BF) for name, table in tables.items()}


def dot32(a, b):
    return jnp.dot(a, b, preferred_element_type=F32)


def gelu_of_half(values):
    u = values.astype(BF)
    scale = math.sqrt(2.0 / math.pi)
    inner = u * (BF(2.0 * scale) + BF(8.0 * scale * 0.044715) * (u * u))
    return u + u * jnp.tanh(inner)


def send_plane(me, count, plane, send, recv, send_sem, recv_sem):
    for shift in range(1, count):
        target = lax.rem(me + shift, count)
        pltpu.make_async_remote_copy(
            src_ref=send.at[plane, target],
            dst_ref=recv.at[plane, me],
            send_sem=send_sem.at[plane],
            recv_sem=recv_sem.at[plane],
            device_id={"space": target},
            device_id_type=pl.DeviceIdType.MESH,
        ).start()
    recv[plane, me] = send[plane, me]


def mode_half(jj, count):
    span = 2 * C * MZ // LANES
    return pl.ds(jj * span, span)


def send_modes(me, count, plane, jj, send, recv, send_sem, recv_sem):
    part = mode_half(jj, count)
    for shift in range(1, count):
        target = lax.rem(me + shift, count)
        pltpu.make_async_remote_copy(
            src_ref=send.at[plane, target, part],
            dst_ref=recv.at[plane, me, part],
            send_sem=send_sem.at[plane, jj],
            recv_sem=recv_sem.at[plane, jj],
            device_id={"space": target},
            device_id_type=pl.DeviceIdType.MESH,
        ).start()
    recv[plane, me, part] = send[plane, me, part]


def wait_modes(count, plane, jj, buffer, sem):
    part = buffer.at[plane, pl.ds(0, count - 1), mode_half(jj, count)]
    pltpu.make_async_copy(part, part, sem.at[plane, jj]).wait()


def wait_plane(parts, plane, buffer, sem):
    part = buffer.at[plane, pl.ds(0, parts)]
    pltpu.make_async_copy(part, part, sem.at[plane]).wait()


def slot_of(s, count):
    own = MY // count
    return (s % own * 2 + s // own) * (C * MZ // LANES)


def to_modes(plane, count, zf_ref, yf_ref, zs, flat, send):
    tiles = C * MZ // LANES
    slots = 2 * MY // count * tiles
    halves = {}
    for first in range(0, tiles, 2 * TB):
        some = [(group, y2) for group in range(first, first + 2 * TB) for y2 in range(2)]
        left = [
            jnp.concatenate(
                [zs[y2, pl.ds((group * 4 + r) * PITCH, PAIRS), :] for r in range(4)], 1
            ).astype(BF)
            for group, y2 in some
        ]
        waves = dot32(jnp.concatenate(left, 0), zf_ref[...]).astype(BF)
        for n, key in enumerate(some):
            halves[key] = waves[n * PAIRS : (n + 1) * PAIRS, :]
    for pair in range(tiles // 2):
        columns = []
        for group in (pair * 2, pair * 2 + 1):
            parts = [
                halves[group, y2][:, p * LANES : (p + 1) * LANES] for y2 in range(2) for p in range(2)
            ]
            columns.append(jnp.concatenate(parts, 0))
        modes = dot32(yf_ref[...], jnp.concatenate(columns, 1))
        for s in range(2 * MY // count):
            for half in range(2):
                slot = slot_of(s, count) + pair * 2 + half
                flat[pl.ds(slot, count, stride=slots + SKEW), :] = modes[
                    s * count : (s + 1) * count, half * LANES : (half + 1) * LANES
                ]
    for dst in range(count):
        send[plane, dst] = flat[pl.ds(dst * (slots + SKEW), slots), :].astype(BF)


def lay_out(zs, start, values):
    for y2 in range(2):
        for r in range(ROWS):
            zs[y2, pl.ds(start + r, C, stride=PITCH), :] = values[
                r * C : (r + 1) * C, y2 * NZ : (y2 + 1) * NZ
            ]


def hid_rows(index):
    return pl.ds(index * ROWS * C, ROWS * C)


def lift_plane(plane, feat_ref, perm_ref, in_ref, lo_ref, hid, plain, xs, zs):
    for f in range(FIN + 1):
        plain[...] = perm_ref[0, plane] if f == FIN else feat_ref[0, f, plane].astype(F32)
        for y2 in range(2):
            xs[y2, pl.ds(f, PAIRS, stride=8), :] = plain[pl.ds(y2, PAIRS, stride=2), :]
    width = lo_ref.shape[1]
    parts = in_ref.shape[0] // width
    total = PAIRS // ROWS * parts

    def first(n):
        u, r = n // parts, n % parts
        x = jnp.concatenate([xs[y2, pl.ds(u * ROWS * 8, ROWS * 8), :] for y2 in range(2)], 1)
        return dot32(in_ref[r * width : (r + 1) * width, :], x.astype(BF))

    ahead = {n: first(n) for n in range(LOOK)}
    raw = {}

    def finish(n):
        if n % parts == parts - 1:
            u = n // parts
            hidden = jnp.concatenate([raw.pop(u * parts + r) for r in range(parts)], 0)
            hid[plane, hid_rows(u), :] = hidden.astype(BF)
            lay_out(zs, u * ROWS, hidden)

    for n in range(total):
        if n + LOOK < total:
            ahead[n + LOOK] = first(n + LOOK)
        raw[n] = dot32(lo_ref[...], gelu_of_half(ahead.pop(n)))
        if n >= LAG:
            finish(n - LAG)
    for n in range(total - LAG, total):
        finish(n)


def from_modes(plane, count, recv, yi_ref, zi_ref, flat, sp):
    tiles = C * MZ // LANES
    slots = 2 * MY // count * tiles
    for src in range(count):
        flat[pl.ds(src * (slots + SKEW), slots), :] = recv[plane, src].astype(F32)

    def back_of(pair):
        rows = []
        for s in range(2 * MY // count):
            part = [
                flat[pl.ds(slot_of(s, count) + pair * 2 + half, count, stride=slots + SKEW), :]
                for half in range(2)
            ]
            rows.append(jnp.concatenate(part, 1))
        return dot32(yi_ref[...], jnp.concatenate(rows, 0).astype(BF)).astype(BF)

    for first in range(0, tiles // 2, FB):
        left, some = [], []
        for pair in range(first, first + FB):
            back = back_of(pair)
            for half in range(2):
                lanes = slice(half * LANES, (half + 1) * LANES)
                for y2 in range(2):
                    parts = [
                        back[(y2 * 2 + p) * PAIRS : (y2 * 2 + p + 1) * PAIRS, lanes] for p in range(2)
                    ]
                    left.append(jnp.concatenate(parts, 1))
                    some.append(((pair * 2 + half) * 4, y2))
        field = dot32(jnp.concatenate(left, 0), zi_ref[...])
        for n, (o, y2) in enumerate(some):
            for r in range(4):
                sp[y2, pl.ds(o + r, PAIRS, stride=C + SKEW), :] = field[
                    n * PAIRS : (n + 1) * PAIRS, r * NZ : (r + 1) * NZ
                ]


def field_rows(index, sp):
    halves = []
    for y2 in range(2):
        rows = [sp[y2, pl.ds((index * ROWS + r) * (C + SKEW), C), :] for r in range(ROWS)]
        halves.append(jnp.concatenate(rows, 0))
    return jnp.concatenate(halves, 1)


def middle_plane(plane, kp, hid, sp, zs):
    total = PAIRS // ROWS

    def local_term(index):
        return dot32(kp[...], hid[plane, hid_rows(index), :])

    ahead = {n: local_term(n) for n in range(MID)}
    for n in range(total):
        if n + MID < total:
            ahead[n + MID] = local_term(n + MID)
        hidden = gelu_of_half(ahead.pop(n) + field_rows(n, sp))
        hid[plane, hid_rows(n), :] = hidden
        lay_out(zs, n * ROWS, hidden.astype(F32))


def final_plane(plane, kp, di_ref, do_ref, perm_ref, hid, sp, st_ref):
    total = PAIRS // ROWS
    width = di_ref.shape[1]
    parts = di_ref.shape[0] // width

    def local_term(index):
        return dot32(kp[...], hid[plane, hid_rows(index), :])

    def mixed(n):
        return gelu_of_half(ahead.pop(n) + field_rows(n, sp))

    def decode(hidden, r):
        return dot32(di_ref[r * width : (r + 1) * width, :], hidden)

    def shrink(n, r):
        return dot32(do_ref[:, r * width : (r + 1) * width], gelu_of_half(raw.pop((n, r))))

    ahead = {n: local_term(n) for n in range(MID)}
    raw = {}
    hiddens = {0: mixed(0)}
    for r in range(parts):
        raw[0, r] = decode(hiddens[0], r)
    hiddens[1] = mixed(1)
    for n in range(total):
        if n + MID < total:
            ahead[n + MID] = local_term(n + MID)
        both = 0.0
        for r in range(parts):
            if n + 1 < total:
                raw[n + 1, r] = decode(hiddens[n + 1], r)
            both = both + shrink(n, r)
            if r == 0 and n + 2 < total:
                hiddens[n + 2] = mixed(n + 2)
        for y2 in range(2):
            lanes = slice(y2 * NZ, (y2 + 1) * NZ)
            where = pl.ds(n * ROWS * 2 + y2, ROWS, stride=2)
            st_ref[0, 0, plane, where, :] = both[:ROWS, lanes]
            st_ref[0, 1, plane, where, :] = both[ROWS:, lanes]

def residual_plane(plane, me, planes, perm_ref, cells, rates, ends, st_ref, res_ref, cond):
    sat = jax.nn.sigmoid(st_ref[0, 1, plane])
    st_ref[0, 1, plane] = sat
    conduct = mobility_of(sat, perm_ref[0, plane])
    cond[plane] = conduct
    pressure = st_ref[0, 0, plane]
    flux = 0.0
    for axis in range(2):
        length = pressure.shape[axis]
        inner = lax.broadcasted_iota(jnp.int32, pressure.shape, axis) < length - 1
        beyond = (pltpu.roll(field, length - 1, axis) for field in (conduct, pressure))
        cond_next, press_next = beyond
        face = jnp.where(inner, face_term(conduct, cond_next, pressure, press_next), 0.0)
        flux = flux + face - pltpu.roll(face, 1, axis)
    shape = (NY, cells.shape[1])
    here = cells[...] - (me * planes + plane) * (NY * NZ)
    starts = lax.broadcasted_iota(jnp.int32, shape, 0) * NZ
    offset = here - starts
    hit = (offset >= 0) & (offset < NZ)
    left = jnp.where(hit, rates[...], 0.0).astype(BF)
    dims = (((1,), (1,)), ((), ()))
    source = lax.dot_general(left, ends[...], dims, preferred_element_type=F32)
    res_ref[0, plane] = flux - source


def add_face(plane, st_ref, res_ref, cond):
    face = face_term(cond[plane], cond[plane + 1], st_ref[0, 0, plane], st_ref[0, 0, plane + 1])
    res_ref[0, plane] = res_ref[0, plane] + face
    res_ref[0, plane + 1] = res_ref[0, plane + 1] - face


def edge_copy(me, count, side, edge_send, edge_recv, es_sem, er_sem):
    return pltpu.make_async_remote_copy(
        src_ref=edge_send.at[side],
        dst_ref=edge_recv.at[1 - side],
        send_sem=es_sem.at[side],
        recv_sem=er_sem.at[1 - side],
        device_id={"space": lax.rem(me + (1 if side else count - 1), count)},
        device_id_type=pl.DeviceIdType.MESH,
    )


def wells_of(cells_ref, rates_ref, cells, rates, ends):
    rate = rates_ref[...]
    high = rate.astype(BF).astype(F32)
    middle = (rate - high).astype(BF).astype(F32)
    for n, part in enumerate((high, middle, rate - high - middle)):
        lanes = slice(n * WELLS, (n + 1) * WELLS)
        cells[:, lanes] = cells_ref[...]
        rates[:, lanes] = part
    column = lax.broadcasted_iota(jnp.int32, ends.shape, 0)
    ends[...] = jnp.where((cells[...] & (NZ - 1)) == column, 1.0, 0.0).astype(BF)


def mix_modes(planes, count, jj, recv, wbuf, xf_ref, flat, spec, rows, mixed, turned):
    own = MY // count
    tiles = C * MZ // LANES
    slots = 2 * own * tiles
    pitch = slots + SKEW
    every = count * planes
    lane = lax.broadcasted_iota(jnp.int32, (1, LANES), 1)
    low = lane < 64
    even = lane % 64 < 32

    def unpack(plane, carry):
        for src in range(count):
            start = (plane * count + src) * pitch + jj * 2 * tiles
            flat[pl.ds(start, 2 * tiles), :] = recv[plane, src, mode_half(jj, count)].astype(F32)
        return carry

    lax.fori_loop(0, planes, unpack, 0)

    def column(p, t):
        return flat[pl.ds((jj * 2 + p) * tiles + t, every, stride=pitch), :].astype(BF)

    for pair in range(tiles // 2):
        right = jnp.concatenate(
            [
                jnp.concatenate([column(p, pair * 2 + half) for half in range(2)], 1)
                for p in range(2)
            ],
            0,
        )
        total = dot32(xf_ref[...], right)
        for half in range(2):
            part = total[:, half * LANES : (half + 1) * LANES].T
            for r in range(4):
                first = (pair * 2 + half) * 4 + r
                spec[pl.ds(first * (MZ + SKEW), MZ), : 2 * MX] = part[r * MZ : (r + 1) * MZ, :]
    groups = MZ // MODE_STEP
    for group in range(groups):
        base = group * MODE_STEP
        picked = [
            spec[pl.ds(base + r, C, stride=MZ + SKEW), : 2 * MX] for r in range(MODE_STEP)
        ]
        rows[group] = jnp.concatenate(picked, 0).T
    wide = MODE_STEP * C
    own_mode = lax.broadcasted_iota(jnp.int32, (MODE_STEP, wide), 0) == (
        lax.broadcasted_iota(jnp.int32, (MODE_STEP, wide), 1) // C
    )
    per = wide // (2 * C)

    def step(group, carry):
        first = pl.multiple_of(group * MODE_STEP, MODE_STEP)
        wfirst = pl.multiple_of(jj * MZ + group * MODE_STEP, MODE_STEP)
        for piece in range(MX // per):
            left = []
            for i in range(per):
                for q in range(2):
                    row = rows[group, pl.ds(q * MX + piece * per + i, MODE_STEP, stride=0), :]
                    left.append(jnp.where(own_mode, row, 0.0))
            lo = piece * wide
            weights = wbuf[pl.ds(wfirst, MODE_STEP), :, lo : lo + wide].reshape(wide, wide)
            both = dot32(jnp.concatenate(left, 0).astype(BF), weights)

            def part(i, q, t):
                at = (i * 2 + q) * MODE_STEP
                return both[at : at + MODE_STEP, t * LANES : (t + 1) * LANES]

            for t in range(2):
                real, imag = (
                    jnp.where(low, part(2 * t, q, t), part(2 * t + 1, q, t)) for q in range(2)
                )
                turn = jnp.where(even, -pltpu.roll(imag, LANES - C, 1), pltpu.roll(imag, C, 1))
                mixed[pl.ds(first, MODE_STEP), lo + t * LANES : lo + (t + 1) * LANES] = real + turn
        return carry

    lax.fori_loop(0, groups, step, 0)
    for block in range(MX * 2 * C // LANES):
        part = mixed[:, block * LANES : (block + 1) * LANES].T
        for r in range(4):
            first = (block * 4 + r) * (C + SKEW)
            turned[pl.ds(first, C), :MZ] = part[r * C : (r + 1) * C, :]


def mixed_tile(pair, turned):
    lane = lax.broadcasted_iota(jnp.int32, (1, LANES), 1)
    low = lane < 64
    even = lane % 64 < 32
    right = []
    for half in range(2):
        o = (pair * 2 + half) * 4
        a = [turned[pl.ds(o + r, 2 * MX, stride=C + SKEW), :] for r in range(4)]
        b = jnp.where(low, a[0], pltpu.roll(a[2], 64, 1))
        c = jnp.where(low, a[1], pltpu.roll(a[3], 64, 1))
        right.append(jnp.where(even, b, pltpu.roll(c, 32, 1)))
    return jnp.concatenate(right, 1).astype(BF)


def to_planes(table, tile, jj, pair, count, flat):
    own = MY // count
    tiles = C * MZ // LANES
    pitch = 2 * own * tiles + SKEW
    back = dot32(table, tile)
    every = back.shape[0] // 2
    for p in range(2):
        for half in range(2):
            slot = (jj * 2 + p) * tiles + pair * 2 + half
            flat[pl.ds(slot, every, stride=pitch), :] = back[
                p * every : (p + 1) * every, half * LANES : (half + 1) * LANES
            ]


def pack_planes(planes, count, first, targets, flat, send):
    slots = 2 * MY // count * C * MZ // LANES
    pitch = slots + SKEW

    def pack(plane, carry):
        for dst in range(targets):
            start = (plane * targets + dst) * pitch
            send[plane, first + dst] = flat[pl.ds(start, slots), :].astype(BF)
        return carry

    lax.fori_loop(0, planes, pack, 0)


def send_half(me, count, plane, other, send, recv, send_sem, recv_sem):
    near = count // 2
    owner = lax.rem(me + other * near, count)
    for shift in range(1, near):
        place = lax.rem(me + shift, near)
        pltpu.make_async_remote_copy(
            src_ref=send.at[plane, other * near + place],
            dst_ref=recv.at[plane, owner],
            send_sem=send_sem.at[plane],
            recv_sem=recv_sem.at[plane],
            device_id={"space": me // near * near + place},
            device_id_type=pl.DeviceIdType.MESH,
        ).start()
    recv[plane, owner] = send[plane, other * near + lax.rem(me, near)]


def swap_tile(me, count, n, own, other, send_sem, recv_sem):
    return pltpu.make_async_remote_copy(
        src_ref=own.at[n],
        dst_ref=other.at[n],
        send_sem=send_sem.at[n],
        recv_sem=recv_sem.at[n],
        device_id={"space": lax.rem(me + count // 2, count)},
        device_id_type=pl.DeviceIdType.MESH,
    )


def whole_kernel(
    planes, count, feat_ref, perm_ref, lift_in, lift_out, point, dec_in, dec_out, zf_ref, zi_ref,
    yf_ref, yi_ref, xf_ref, xi_ref, xh_ref, cells_ref, rates_ref, w_hbm, st_ref, res_ref,
    hid, wbuf, send_f, recv_f, send_b, recv_b, flat, spec, rows, mixed, turned, zs, sp, xs, plain,
    in_ref, lo_ref, kp_ref, di_ref, do_ref, cond, cells, rates, ends, edge_send, edge_recv,
    own_mixed, other_mixed,
    w_sem, sf_sem, rf_sem, sb_sem, rb_sem, es_sem, er_sem, om_sem, rm_sem,
):
    me = lax.axis_index("space")
    barrier = pltpu.get_barrier_semaphore()
    for shift in range(1, count):
        pl.semaphore_signal(
            barrier,
            inc=1,
            device_id={"space": lax.rem(me + shift, count)},
            device_id_type=pl.DeviceIdType.MESH,
        )
    fetch = pltpu.make_async_copy(w_hbm.at[0], wbuf, w_sem.at[0])
    fetch.start()
    xs[...] = jnp.zeros_like(xs)
    in_ref[...] = diag_of(lift_in[...], ROWS, 8, 0.5)
    lo_ref[...] = diag_of(lift_out[...], 2, lift_out.shape[1], 1.0, True)
    for layer in range(LAYERS):
        kp_ref[layer] = diag_of(point[layer], ROWS, C, 0.5)
    di_ref[...] = diag_of(dec_in[...], ROWS, C, 0.5)
    dec = dec_out.shape[1]
    do_ref[...] = spread(
        dec_out[...],
        2 * ROWS,
        ROWS * dec,
        lambda i: i // ROWS,
        lambda j: j % dec,
        lambda i, j: i % ROWS == j // dec,
        1.0,
        True,
    )
    wells_of(cells_ref, rates_ref, cells, rates, ends)
    pl.semaphore_wait(barrier, count - 1)

    def over(body):
        def run(plane, carry):
            body(plane)
            return carry

        lax.fori_loop(0, planes, run, 0)

    own = MY // count

    def send_forward(plane, soon):
        send_modes(me, count, plane, 0, send_f, recv_f, sf_sem, rf_sem)

        @pl.when(plane < soon)
        def _():
            send_rest(plane)

    def send_rest(plane):
        for jj in range(1, own):
            send_modes(me, count, plane, jj, send_f, recv_f, sf_sem, rf_sem)

    def send_late(soon):
        lax.fori_loop(soon, planes, lambda plane, carry: (send_rest(plane), carry)[1], 0)

    def lift(plane):
        lift_plane(plane, feat_ref, perm_ref, in_ref, lo_ref, hid, plain, xs, zs)
        to_modes(plane, count, zf_ref, yf_ref, zs, flat, send_f)
        send_forward(plane, SOON[0])

    over(lift)
    send_late(SOON[0])
    for layer in range(LAYERS):
        fetch.wait()
        last = layer + 1 == LAYERS
        tile_pairs = C * MZ // LANES // 2
        swaps = [
            swap_tile(me, count, n, own_mixed, other_mixed, om_sem, rm_sem)
            for n in range(0 if last else own * tile_pairs)
        ]
        for jj in range(own):
            over(lambda plane: wait_modes(count, plane, jj, recv_f, rf_sem))
            mix_modes(planes, count, jj, recv_f, wbuf, xf_ref, flat, spec, rows, mixed, turned)
            for pair in range(tile_pairs):
                tile = mixed_tile(pair, turned)
                if last:
                    to_planes(xi_ref[...], tile, jj, pair, count, flat)
                else:
                    n = jj * tile_pairs + pair
                    own_mixed[n] = tile
                    swaps[n].start()
        for jj in range(own):
            over(lambda plane: wait_modes(count, plane, jj, send_f, sf_sem))
        if not last:
            fetch = pltpu.make_async_copy(w_hbm.at[layer + 1], wbuf, w_sem.at[layer + 1])
            fetch.start()

        def turn(index):
            return lax.rem(planes - index, planes) if last else index

        if last:
            parts = count - 1
            pack_planes(planes, count, 0, count, flat, send_b)
            over(lambda n: send_plane(me, count, turn(n), send_b, recv_b, sb_sem, rb_sem))
        else:
            near = count // 2
            parts = 2 * (near - 1)
            table = xh_ref.at[me // near]
            for other in range(2):
                for n, swap in enumerate(swaps):
                    if other:
                        swap.wait_recv()
                    tile = other_mixed[n] if other else own_mixed[n]
                    to_planes(table[...], tile, n // tile_pairs, n % tile_pairs, count, flat)
                pack_planes(planes, count, other * near, near, flat, send_b)
                over(lambda n: send_half(me, count, n, other, send_b, recv_b, sb_sem, rb_sem))
            for swap in swaps:
                swap.wait_send()
        kp = kp_ref.at[layer]

        def rest(index):
            plane = turn(index)
            wait_plane(parts, plane, recv_b, rb_sem)
            from_modes(plane, count, recv_b, yi_ref, zi_ref, flat, sp)
            if not last:
                middle_plane(plane, kp, hid, sp, zs)
                to_modes(plane, count, zf_ref, yf_ref, zs, flat, send_f)
                send_forward(plane, SOON[1])
            else:
                final_plane(plane, kp, di_ref, do_ref, perm_ref, hid, sp, st_ref)
                residual_plane(
                    plane, me, planes, perm_ref, cells, rates, ends, st_ref, res_ref, cond
                )

                @pl.when(index == 1)
                def _():
                    for side in range(2):
                        edge_send[side, 0] = st_ref[0, 0, side * (planes - 1)].astype(BF)
                        edge_send[side, 1] = cond[side * (planes - 1)].astype(BF)
                        edge_copy(me, count, side, edge_send, edge_recv, es_sem, er_sem).start()

                @pl.when(index >= 2)
                def _():
                    add_face(plane, st_ref, res_ref, cond)

        over(rest)
        if not last:
            send_late(SOON[1])
        over(lambda plane: wait_plane(parts, plane, send_b, sb_sem))
    add_face(0, st_ref, res_ref, cond)
    for side in range(2):
        edge_copy(me, count, side, edge_send, edge_recv, es_sem, er_sem).wait()
    for side in range(2):
        plane = side * (planes - 1)
        press, conduct = (edge_recv[side, n].astype(F32) for n in range(2))
        face = face_term(cond[plane], conduct, st_ref[0, 0, plane], press)
        inside = me < count - 1 if side else me > 0
        res_ref[0, plane] = res_ref[0, plane] + jnp.where(inside, face, 0.0)


def ones_where(shape, test, value=1.0):
    row = lax.broadcasted_iota(jnp.int32, shape, 0)
    col = lax.broadcasted_iota(jnp.int32, shape, 1)
    return jnp.where(test(row, col), value, 0.0)


def spread(matrix, rows, cols, row_of, col_of, keep, value, turned):
    depth, height = matrix.shape[::-1] if turned else matrix.shape
    take = ones_where((rows, height), lambda i, j: row_of(i) == j).astype(BF)
    put = ones_where((depth, cols), lambda i, j: col_of(j) == i).astype(BF)
    dims = (((1,), (0 if turned else 1,)), ((), ()))
    part = lax.dot_general(take, matrix, dims, preferred_element_type=F32)
    return (dot32(part.astype(BF), put) * ones_where((rows, cols), keep, value)).astype(BF)


def diag_of(matrix, copies, width, value, turned=False):
    height = matrix.shape[0 if turned else 1]
    return spread(
        matrix,
        copies * height,
        copies * width,
        lambda i: i % height,
        lambda j: j % width,
        lambda i, j: i // height == j // width,
        value,
        turned,
    )


def local_fast(
    features,
    log_perm,
    well_cells,
    well_rates,
    lift_in,
    lift_out,
    spec_weight,
    point_weight,
    dec_in,
    dec_out,
):
    planes = features.shape[2]
    count = lax.axis_size("space")
    own = MY // count
    modes = own * MZ
    slots = 2 * modes * C // LANES
    tables = tables_for(count)
    lift, dec = lift_in.shape[1], dec_in.shape[1]
    operands = (
        features,
        log_perm,
        lift_in,
        lift_out.T,
        point_weight,
        dec_in,
        dec_out.T,
    ) + tuple(tables[name] for name in ("zf", "zi", "yf", "yi", "xf", "xi", "xh"))
    operands = operands + (well_cells, well_rates)
    vmem = pl.BlockSpec(memory_space=pltpu.VMEM)
    exchange = pltpu.VMEM((planes, count, slots, LANES), BF)
    results = pl.pallas_call(
        lambda *refs: whole_kernel(planes, count, *refs),
        in_specs=[vmem] * len(operands) + [pl.BlockSpec(memory_space=pl.ANY)],
        out_specs=[vmem, vmem],
        out_shape=[
            jax.ShapeDtypeStruct((1, 2, planes, NY, NZ), F32),
            jax.ShapeDtypeStruct((1, planes, NY, NZ), F32),
        ],
        scratch_shapes=[
            pltpu.VMEM((planes, PAIRS * C, 2 * NZ), BF),
            pltpu.VMEM(spec_weight.shape[1:], BF),
            exchange,
            exchange,
            exchange,
            exchange,
            pltpu.VMEM((planes * count * (slots + SKEW), LANES), F32),
            pltpu.VMEM((C * (MZ + SKEW), LANES), F32),
            pltpu.VMEM((MZ // MODE_STEP, 2 * MX, MODE_STEP * C), F32),
            pltpu.VMEM((MZ, MX * 2 * C), F32),
            pltpu.VMEM((2 * MX * (C + SKEW), LANES), F32),
            pltpu.VMEM((2, C * PITCH, LANES), F32),
            pltpu.VMEM((2, PAIRS * (C + SKEW), LANES), F32),
            pltpu.VMEM((2, PAIRS * 8, NZ), F32),
            pltpu.VMEM((NY, NZ), F32),
            pltpu.VMEM((ROWS * lift, ROWS * 8), BF),
            pltpu.VMEM((2 * C, 2 * lift), BF),
            pltpu.VMEM((LAYERS, ROWS * C, ROWS * C), BF),
            pltpu.VMEM((ROWS * dec, ROWS * C), BF),
            pltpu.VMEM((2 * ROWS, ROWS * dec), BF),
            pltpu.VMEM((planes, NY, NZ), F32),
            pltpu.VMEM((1, 3 * WELLS), jnp.int32),
            pltpu.VMEM((1, 3 * WELLS), F32),
            pltpu.VMEM((NZ, 3 * WELLS), BF),
            pltpu.VMEM((2, 2, NY, NZ), BF),
            pltpu.VMEM((2, 2, NY, NZ), BF),
            pltpu.VMEM((modes * C // 256, 2 * MX, 256), BF),
            pltpu.VMEM((modes * C // 256, 2 * MX, 256), BF),
            pltpu.SemaphoreType.DMA((LAYERS,)),
        ]
        + [pltpu.SemaphoreType.DMA((planes, own))] * 2
        + [pltpu.SemaphoreType.DMA((planes,))] * 2
        + [pltpu.SemaphoreType.DMA((2,))] * 2
        + [pltpu.SemaphoreType.DMA((modes * C // 256,))] * 2,
        compiler_params=pltpu.CompilerParams(
            collective_id=0, has_side_effects=True, vmem_limit_bytes=60 * 1024 * 1024
        ),
        name="whole",
    )(*operands, spec_weight)
    return handed_on(results)


def handed_on(results):
    pieces = [
        (n, at) for n, each in enumerate(results) for at in np.ndindex(*each.shape[:-2])
    ]

    def body(*refs):
        source, target, held = refs[:2], refs[2:4], refs[4:6]
        in_sem, out_sem = refs[6:]
        loads = [
            pltpu.make_async_copy(source[n].at[at], held[n].at[at], in_sem.at[k])
            for k, (n, at) in enumerate(pieces)
        ]
        stores = [
            pltpu.make_async_copy(held[n].at[at], target[n].at[at], out_sem.at[k])
            for k, (n, at) in enumerate(pieces)
        ]
        for load in loads:
            load.start()
        for load, store in zip(loads, stores):
            load.wait()
            store.start()
        for store in stores:
            store.wait()

    whole = pl.BlockSpec(memory_space=pl.ANY)
    return pl.pallas_call(
        body,
        in_specs=[whole] * 2,
        out_specs=[whole] * 2,
        out_shape=[jax.ShapeDtypeStruct(each.shape, each.dtype) for each in results],
        scratch_shapes=[pltpu.VMEM(each.shape, each.dtype) for each in results]
        + [pltpu.SemaphoreType.DMA((len(pieces),))] * 2,
        compiler_params=pltpu.CompilerParams(vmem_limit_bytes=60 * 1024 * 1024),
        name="handed_on",
    )(*results)


def local(features, log_perm, well_cells, well_rates, lift_in, lift_out, spec_weight, *rest):
    batches, planes = features.shape[0], features.shape[2]
    count = lax.axis_size("space")
    fits = batches == 1 and planes == 8 and count % 8 == 0 and MY == 2 * count
    run = local_fast if fits else local_general
    return run(
        features, log_perm, well_cells, well_rates, lift_in, lift_out, spec_weight, *rest
    )


def solution(mesh):
    return jax.shard_map(
        local,
        mesh=mesh,
        in_specs=(
            P("sample", None, "space", None, None),
            P("sample", "space", None, None),
            P("sample", None),
            P("sample", None),
            P(),
            P(),
            P(None, "space", None, None),
            P(),
            P(),
            P(),
        ),
        out_specs=(P("sample", None, "space", None, None), P("sample", "space", None, None)),
        check_vma=False,
    )
```

```python
import math

import jax
import jax.numpy as jnp
import numpy as np
from jax import lax
from jax.experimental import pallas as pl
from jax.experimental.pallas import tpu as pltpu
from jax.sharding import PartitionSpec as P

NX = 128
NY = 128
NZ = 128
MX = 32
MY = 32
MZ = 32
C = 32
FIN = 4
LAYERS = 2
WELLS = 32


def padded_2(block, sides, width):
    for axis, dim in sides:
        count = lax.axis_size(axis)
        forward = [(i, i + 1) for i in range(count - 1)]
        backward = [(target, source) for source, target in forward]
        low = lax.ppermute(
            lax.slice_in_dim(block, block.shape[dim] - width, None, axis=dim), axis, forward
        )
        high = lax.ppermute(lax.slice_in_dim(block, 0, width, axis=dim), axis, backward)
        block = jnp.concatenate([low, block, high], axis=dim)
    return block


def freq_table(length, kept, one_sided):
    indices = jnp.arange(kept, dtype=jnp.int32)
    if one_sided:
        return indices
    return jnp.where(indices < kept // 2, indices, length - kept + indices)


def wave_parts(length, kept, one_sided):
    freqs = freq_table(length, kept, one_sided)
    places = jnp.arange(length, dtype=jnp.int32)
    phase_turns = freqs[:, None] * places[None, :] % length
    angles = phase_turns.astype(jnp.float32) * (2.0 * math.pi / length)
    norm_scale = 1.0 / math.sqrt(length)
    return (jnp.cos(angles) * norm_scale, jnp.sin(angles) * norm_scale)


def forward_table(length, kept):
    cosine_vals, sine_vals = wave_parts(length, kept, False)
    return jnp.stack(
        [jnp.stack([cosine_vals.T, -sine_vals.T], 1), jnp.stack([sine_vals.T, cosine_vals.T], 1)], 1
    ).astype(jnp.bfloat16)


def inverse_table(length, kept):
    cosine_vals, sine_vals = wave_parts(length, kept, False)
    return jnp.stack(
        [jnp.stack([cosine_vals, sine_vals], 1), jnp.stack([-sine_vals, cosine_vals], 1)], 1
    ).astype(jnp.bfloat16)


def z_tables():
    cosine_vals, sine_vals = wave_parts(NZ, MZ, True)
    weights_k = jnp.where(jnp.arange(MZ) == 0, 1.0, 2.0).astype(jnp.float32)[:, None]
    z_forward = jnp.concatenate([cosine_vals.T, -sine_vals.T], 1).astype(jnp.bfloat16)
    z_inverse = jnp.concatenate([weights_k * cosine_vals, -weights_k * sine_vals], 0).astype(
        jnp.bfloat16
    )
    return (z_forward, z_inverse)


def gelu_tanh(values):
    return jax.nn.gelu(values, approximate=True)


def face_term(cond_a, cond_b, press_a, press_b):
    return 2.0 * cond_a * cond_b / (cond_a + cond_b) * (press_a - press_b)


def mobility_of(saturation, log_values):
    return jnp.exp(log_values) * (
        saturation * saturation + 0.5 * (1.0 - saturation) * (1.0 - saturation)
    )


def darcy(pressure, conduct, well_cells, well_rates):
    batches, planes = pressure.shape[0], pressure.shape[1]
    space_index = lax.axis_index("space")
    pad_cond = jnp.pad(conduct, ((0, 0), (0, 0), (1, 1), (1, 1)))
    pad_press = jnp.pad(pressure, ((0, 0), (0, 0), (1, 1), (1, 1)))
    flux_sum = face_term(conduct, pad_cond[:, :, 2:, 1:-1], pressure, pad_press[:, :, 2:, 1:-1])
    flux_sum = flux_sum + face_term(
        conduct, pad_cond[:, :, :-2, 1:-1], pressure, pad_press[:, :, :-2, 1:-1]
    )
    flux_sum = flux_sum + face_term(
        conduct, pad_cond[:, :, 1:-1, 2:], pressure, pad_press[:, :, 1:-1, 2:]
    )
    flux_sum = flux_sum + face_term(
        conduct, pad_cond[:, :, 1:-1, :-2], pressure, pad_press[:, :, 1:-1, :-2]
    )
    fields = jnp.stack([pressure, conduct], 1)
    padded = padded_2(fields.astype(jnp.bfloat16), (("space", 2),), 1).astype(fields.dtype)
    press_low = padded[:, 0, 0]
    press_high = padded[:, 0, -1]
    cond_low = padded[:, 1, 0]
    cond_high = padded[:, 1, -1]
    press_below = jnp.concatenate([press_low[:, None], pressure[:, :-1]], 1)
    cond_below = jnp.concatenate([cond_low[:, None], conduct[:, :-1]], 1)
    press_above = jnp.concatenate([pressure[:, 1:], press_high[:, None]], 1)
    cond_above = jnp.concatenate([conduct[:, 1:], cond_high[:, None]], 1)
    lower_terms = face_term(conduct, cond_below, pressure, press_below)
    upper_terms = face_term(conduct, cond_above, pressure, press_above)
    flux_sum = flux_sum + lower_terms + upper_terms
    well_x = well_cells // (NY * NZ) - space_index * planes
    well_y = well_cells // NZ % NY
    well_z = well_cells % NZ
    onehot_x = (well_x[:, :, None] == jnp.arange(planes, dtype=jnp.int32)[None, None, :]).astype(
        jnp.float32
    ) * well_rates[:, :, None]
    onehot_y = (well_y[:, :, None] == jnp.arange(NY, dtype=jnp.int32)[None, None, :]).astype(
        jnp.float32
    )
    onehot_z = (well_z[:, :, None] == jnp.arange(NZ, dtype=jnp.int32)[None, None, :]).astype(
        jnp.float32
    )
    plane_rows = (onehot_x[:, :, :, None] * onehot_y[:, :, None, :]).reshape(
        batches, WELLS, planes * NY
    )
    source = jnp.einsum(
        "bwa,bwz->baz", plane_rows, onehot_z, precision=lax.Precision.HIGHEST
    ).reshape(batches, planes, NY, NZ)
    return flux_sum - source


def local_general(
    features,
    log_perm,
    well_cells,
    well_rates,
    lift_in,
    lift_out,
    spec_weight,
    point_weight,
    dec_in,
    dec_out,
):
    batches = features.shape[0]
    planes = features.shape[2]
    space_index = lax.axis_index("space")
    block = spec_weight.shape[1]
    cell_count = planes * NY * NZ
    z_forward, z_inverse = z_tables()
    y_forward = forward_table(NY, MY)
    y_inverse = inverse_table(NY, MY)
    x_forward = forward_table(NX, MX)
    x_inverse = inverse_table(NX, MX)
    perm_b = log_perm.astype(jnp.bfloat16).reshape(batches, 1, cell_count)
    lift_input = jnp.concatenate([features.reshape(batches, FIN, cell_count), perm_b], 1)
    lift_hidden = jnp.einsum("bfn,fh->bhn", lift_input, lift_in, preferred_element_type=jnp.float32)
    lifted = gelu_tanh(lift_hidden).astype(jnp.bfloat16)
    hidden_state = jnp.einsum(
        "bhn,hc->bcn", lifted, lift_out, preferred_element_type=jnp.float32
    ).astype(jnp.bfloat16)
    for layer_idx in range(LAYERS):
        zspec = jnp.dot(hidden_state.reshape(-1, NZ), z_forward, preferred_element_type=jnp.float32)
        zspec = zspec.astype(jnp.bfloat16).reshape(batches * C * planes, NY, 2, MZ)
        yz_spec = jnp.einsum(
            "aypk,ypqj->aqjk", zspec, y_forward, preferred_element_type=jnp.float32
        )
        yz_spec = yz_spec.astype(jnp.bfloat16).reshape(batches, C, planes, 2, MY * MZ)
        mode_weights = spec_weight[layer_idx].reshape(block, C, MX, 2, C)
        spectrum = jnp.einsum(
            "bcxpm,xpqi->bcqim",
            lax.all_to_all(yz_spec, "space", split_axis=4, concat_axis=2, tiled=True),
            x_forward,
            preferred_element_type=jnp.float32,
        ).astype(jnp.bfloat16)
        products = jnp.einsum(
            "bcqim,mcipo->bimqpo", spectrum, mode_weights, preferred_element_type=jnp.float32
        )
        real_part = products[:, :, :, 0, 0] - products[:, :, :, 1, 1]
        imag_part = products[:, :, :, 0, 1] + products[:, :, :, 1, 0]
        mixed_modes = jnp.stack([real_part, imag_part], 3).astype(jnp.bfloat16)
        back_field = jnp.einsum(
            "bimqo,iqpx->boxpm", mixed_modes, x_inverse, preferred_element_type=jnp.float32
        ).astype(jnp.bfloat16)
        returned = lax.all_to_all(back_field, "space", split_axis=2, concat_axis=4, tiled=True)
        returned = returned.reshape(batches * C * planes, 2, MY, MZ)
        y_back = jnp.einsum(
            "aqjk,jqpy->aypk", returned, y_inverse, preferred_element_type=jnp.float32
        ).astype(jnp.bfloat16)
        spectral = jnp.dot(
            y_back.reshape(-1, 2 * MZ), z_inverse, preferred_element_type=jnp.float32
        ).reshape(batches, C, cell_count)
        local_term = jnp.einsum(
            "bcn,co->bon", hidden_state, point_weight[layer_idx], preferred_element_type=jnp.float32
        )
        hidden_state = gelu_tanh(spectral + local_term).astype(jnp.bfloat16)
    decoded = gelu_tanh(
        jnp.einsum("bcn,cd->bdn", hidden_state, dec_in, preferred_element_type=jnp.float32)
    ).astype(jnp.bfloat16)
    decoded_out = jnp.einsum("bdn,de->ben", decoded, dec_out, preferred_element_type=jnp.float32)
    pressure = decoded_out[:, 0].reshape(batches, planes, NY, NZ)
    saturation = jax.nn.sigmoid(decoded_out[:, 1]).reshape(batches, planes, NY, NZ)
    states = jnp.stack([pressure, saturation], 1)
    conduct = mobility_of(saturation, log_perm)
    return (states, darcy(pressure, conduct, well_cells, well_rates))


BF = jnp.bfloat16
F32 = jnp.float32
PAIRS = NY // 2
SKEW = 4
PITCH = PAIRS + SKEW
MODE_STEP = 8
SOON = (5, 3)
EARLY = 3
ROWS = 8
LOOK = 4
LAG = 1
MID = 3
TB = 2
FB = 4
LANES = 128


def np_waves(length, kept, one_sided):
    index = np.arange(kept)
    freqs = index if one_sided else np.where(index < kept // 2, index, length - kept + index)
    angles = (freqs[:, None] * np.arange(length)[None, :] % length) * (2.0 * math.pi / length)
    norm = 1.0 / math.sqrt(length)
    return np.cos(angles) * norm, np.sin(angles) * norm


def np_forward(length, kept):
    cosine, sine = np_waves(length, kept, False)
    return np.stack([np.stack([cosine.T, -sine.T], 1), np.stack([sine.T, cosine.T], 1)], 1)


def np_inverse(length, kept):
    cosine, sine = np_waves(length, kept, False)
    return np.stack([np.stack([cosine, sine], 1), np.stack([-sine, cosine], 1)], 1)


def by_plane(table, axis, count):
    planes = NX // count
    order = np.arange(NX).reshape(count, planes).T.reshape(-1)
    return np.take(table, order, axis)


def tables_for(count):
    own = MY // count
    cosine, sine = np_waves(NZ, MZ, True)
    twice = np.where(np.arange(MZ) == 0, 1.0, 2.0)[:, None]
    z_forward = np.concatenate([cosine.T, -sine.T], 1)
    z_inverse = np.concatenate([twice * cosine, -twice * sine], 0)
    y_forward = np_forward(NY, MY).reshape(PAIRS, 2, 2, 2, count, own)
    y_inverse = np_inverse(NY, MY).reshape(count, own, 2, 2, PAIRS, 2)
    four = np.eye(4)
    z_forward = np.einsum("zpk,cd->czpdk", z_forward.reshape(NZ, 2, MZ), four)
    z_inverse = np.einsum("pkz,cd->pckdz", z_inverse.reshape(2, MZ, NZ), four)
    tables = {
        "zf": z_forward.reshape(4 * NZ, 8 * MZ),
        "zi": 0.5 * z_inverse.reshape(8 * MZ, 4 * NZ),
        "yf": y_forward.transpose(3, 5, 4, 1, 2, 0).reshape(2 * MY, 2 * NY),
        "yi": y_inverse.transpose(5, 3, 4, 2, 1, 0).reshape(2 * NY, 2 * MY),
        "xf": by_plane(np_forward(NX, MX).transpose(2, 3, 1, 0), 3, count).reshape(2 * MX, 2 * NX),
        "xi": by_plane(np_inverse(NX, MX).transpose(2, 3, 0, 1), 1, count).reshape(2 * NX, 2 * MX),
    }
    halves = tables["xi"].reshape(2, NX // count, 2, count // 2, 2 * MX)
    tables["xh"] = halves.transpose(2, 0, 1, 3, 4).reshape(2, NX, 2 * MX)
    return {name: jnp.asarray(table.astype(np.float32)).astype(BF) for name, table in tables.items()}


def dot32(a, b):
    return jnp.dot(a, b, preferred_element_type=F32)


def gelu_of_half(values):
    u = values.astype(BF)
    scale = math.sqrt(2.0 / math.pi)
    inner = u * (BF(2.0 * scale) + BF(8.0 * scale * 0.044715) * (u * u))
    return u + u * jnp.tanh(inner)


def mode_half(jj, count):
    span = 2 * C * MZ // LANES
    return pl.ds(jj * span, span)


def others(me, count):
    return [lax.rem(me + shift, count) for shift in range(1, count)]


def send_modes(me, count, plane, jj, send, recv, send_sem, recv_sem):
    part = mode_half(jj, count)
    for target in others(me, count):
        pltpu.make_async_remote_copy(
            src_ref=send.at[plane, target, part],
            dst_ref=recv.at[plane, me, part],
            send_sem=send_sem.at[plane, jj],
            recv_sem=recv_sem.at[plane, jj],
            device_id={"space": target},
            device_id_type=pl.DeviceIdType.MESH,
        ).start()
    recv[plane, me, part] = send[plane, me, part]


def wait_modes(count, plane, jj, buffer, sem):
    part = buffer.at[plane, pl.ds(0, count - 1), mode_half(jj, count)]
    pltpu.make_async_copy(part, part, sem.at[plane, jj]).wait()


def wait_plane(parts, plane, buffer, sem):
    part = buffer.at[plane, pl.ds(0, parts)]
    pltpu.make_async_copy(part, part, sem.at[plane, 0]).wait()


def slot_of(s, count):
    own = MY // count
    return (s % own * 2 + s // own) * (C * MZ // LANES)


def to_modes(plane, count, zf_ref, yf_ref, zs, flat, send):
    tiles = C * MZ // LANES
    slots = 2 * MY // count * tiles
    halves = {}
    for first in range(0, tiles, 2 * TB):
        some = [(group, y2) for group in range(first, first + 2 * TB) for y2 in range(2)]
        left = [
            jnp.concatenate(
                [zs[y2, pl.ds((group * 4 + r) * PITCH, PAIRS), :] for r in range(4)], 1
            ).astype(BF)
            for group, y2 in some
        ]
        waves = dot32(jnp.concatenate(left, 0), zf_ref[...]).astype(BF)
        for n, key in enumerate(some):
            halves[key] = waves[n * PAIRS : (n + 1) * PAIRS, :]
    for pair in range(tiles // 2):
        columns = []
        for group in (pair * 2, pair * 2 + 1):
            parts = [
                halves[group, y2][:, p * LANES : (p + 1) * LANES] for y2 in range(2) for p in range(2)
            ]
            columns.append(jnp.concatenate(parts, 0))
        modes = dot32(yf_ref[...], jnp.concatenate(columns, 1))
        for s in range(2 * MY // count):
            for half in range(2):
                slot = slot_of(s, count) + pair * 2 + half
                flat[pl.ds(slot, count, stride=slots + SKEW), :] = modes[
                    s * count : (s + 1) * count, half * LANES : (half + 1) * LANES
                ]
    for dst in range(count):
        send[plane, dst] = flat[pl.ds(dst * (slots + SKEW), slots), :].astype(BF)


def lay_out(zs, start, values):
    for y2 in range(2):
        for r in range(ROWS):
            zs[y2, pl.ds(start + r, C, stride=PITCH), :] = values[
                r * C : (r + 1) * C, y2 * NZ : (y2 + 1) * NZ
            ]


def hid_rows(index):
    return pl.ds(index * ROWS * C, ROWS * C)


def lift_plane(plane, feat_ref, perm_ref, in_ref, lo_ref, hid, plain, xs, zs):
    for f in range(FIN + 1):
        plain[...] = perm_ref[0, plane] if f == FIN else feat_ref[0, f, plane].astype(F32)
        for y2 in range(2):
            xs[y2, pl.ds(f, PAIRS, stride=8), :] = plain[pl.ds(y2, PAIRS, stride=2), :]
    width = lo_ref.shape[1]
    parts = in_ref.shape[0] // width
    total = PAIRS // ROWS * parts

    def first(n):
        u, r = n // parts, n % parts
        x = jnp.concatenate([xs[y2, pl.ds(u * ROWS * 8, ROWS * 8), :] for y2 in range(2)], 1)
        return dot32(in_ref[r * width : (r + 1) * width, :], x.astype(BF))

    ahead = {n: first(n) for n in range(LOOK)}
    raw = {}

    def finish(n):
        if n % parts == parts - 1:
            u = n // parts
            hidden = jnp.concatenate([raw.pop(u * parts + r) for r in range(parts)], 0)
            hid[plane, hid_rows(u), :] = hidden.astype(BF)
            lay_out(zs, u * ROWS, hidden)

    for n in range(total):
        if n + LOOK < total:
            ahead[n + LOOK] = first(n + LOOK)
        raw[n] = dot32(lo_ref[...], gelu_of_half(ahead.pop(n)))
        if n >= LAG:
            finish(n - LAG)
    for n in range(total - LAG, total):
        finish(n)


def from_modes(plane, count, recv, yi_ref, zi_ref, flat, sp):
    tiles = C * MZ // LANES
    slots = 2 * MY // count * tiles
    for src in range(count):
        flat[pl.ds(src * (slots + SKEW), slots), :] = recv[plane, src].astype(F32)

    def back_of(pair):
        rows = []
        for s in range(2 * MY // count):
            part = [
                flat[pl.ds(slot_of(s, count) + pair * 2 + half, count, stride=slots + SKEW), :]
                for half in range(2)
            ]
            rows.append(jnp.concatenate(part, 1))
        return dot32(yi_ref[...], jnp.concatenate(rows, 0).astype(BF)).astype(BF)

    for first in range(0, tiles // 2, FB):
        left, some = [], []
        for pair in range(first, first + FB):
            back = back_of(pair)
            for half in range(2):
                lanes = slice(half * LANES, (half + 1) * LANES)
                for y2 in range(2):
                    parts = [
                        back[(y2 * 2 + p) * PAIRS : (y2 * 2 + p + 1) * PAIRS, lanes] for p in range(2)
                    ]
                    left.append(jnp.concatenate(parts, 1))
                    some.append(((pair * 2 + half) * 4, y2))
        field = dot32(jnp.concatenate(left, 0), zi_ref[...])
        for n, (o, y2) in enumerate(some):
            for r in range(4):
                sp[y2, pl.ds(o + r, PAIRS, stride=C + SKEW), :] = field[
                    n * PAIRS : (n + 1) * PAIRS, r * NZ : (r + 1) * NZ
                ]


def field_rows(index, sp):
    halves = []
    for y2 in range(2):
        rows = [sp[y2, pl.ds((index * ROWS + r) * (C + SKEW), C), :] for r in range(ROWS)]
        halves.append(jnp.concatenate(rows, 0))
    return jnp.concatenate(halves, 1)


def middle_plane(plane, kp, hid, sp, zs):
    total = PAIRS // ROWS

    def local_term(index):
        return dot32(kp[...], hid[plane, hid_rows(index), :])

    ahead = {n: local_term(n) for n in range(MID)}
    for n in range(total):
        if n + MID < total:
            ahead[n + MID] = local_term(n + MID)
        hidden = gelu_of_half(ahead.pop(n) + field_rows(n, sp))
        hid[plane, hid_rows(n), :] = hidden
        lay_out(zs, n * ROWS, hidden.astype(F32))


def final_plane(plane, kp, di_ref, do_ref, perm_ref, hid, sp, st_ref):
    total = PAIRS // ROWS
    width = di_ref.shape[1]
    parts = di_ref.shape[0] // width

    def local_term(index):
        return dot32(kp[...], hid[plane, hid_rows(index), :])

    def mixed(n):
        return gelu_of_half(ahead.pop(n) + field_rows(n, sp))

    def decode(hidden, r):
        return dot32(di_ref[r * width : (r + 1) * width, :], hidden)

    def shrink(n, r):
        return dot32(do_ref[:, r * width : (r + 1) * width], gelu_of_half(raw.pop((n, r))))

    ahead = {n: local_term(n) for n in range(MID)}
    raw = {}
    hiddens = {0: mixed(0)}
    for r in range(parts):
        raw[0, r] = decode(hiddens[0], r)
    hiddens[1] = mixed(1)
    for n in range(total):
        if n + MID < total:
            ahead[n + MID] = local_term(n + MID)
        both = 0.0
        for r in range(parts):
            if n + 1 < total:
                raw[n + 1, r] = decode(hiddens[n + 1], r)
            both = both + shrink(n, r)
            if r == 0 and n + 2 < total:
                hiddens[n + 2] = mixed(n + 2)
        for y2 in range(2):
            lanes = slice(y2 * NZ, (y2 + 1) * NZ)
            where = pl.ds(n * ROWS * 2 + y2, ROWS, stride=2)
            st_ref[0, 0, plane, where, :] = both[:ROWS, lanes]
            st_ref[0, 1, plane, where, :] = both[ROWS:, lanes]

def residual_plane(plane, me, planes, perm_ref, cells, rates, ends, st_ref, res_ref, cond):
    sat = jax.nn.sigmoid(st_ref[0, 1, plane])
    st_ref[0, 1, plane] = sat
    conduct = mobility_of(sat, perm_ref[0, plane])
    cond[plane] = conduct
    pressure = st_ref[0, 0, plane]
    flux = 0.0
    for axis in range(2):
        length = pressure.shape[axis]
        inner = lax.broadcasted_iota(jnp.int32, pressure.shape, axis) < length - 1
        beyond = (pltpu.roll(field, length - 1, axis) for field in (conduct, pressure))
        cond_next, press_next = beyond
        face = jnp.where(inner, face_term(conduct, cond_next, pressure, press_next), 0.0)
        flux = flux + face - pltpu.roll(face, 1, axis)
    shape = (NY, cells.shape[1])
    here = cells[...] - (me * planes + plane) * (NY * NZ)
    starts = lax.broadcasted_iota(jnp.int32, shape, 0) * NZ
    offset = here - starts
    hit = (offset >= 0) & (offset < NZ)
    left = jnp.where(hit, rates[...], 0.0).astype(BF)
    dims = (((1,), (1,)), ((), ()))
    source = lax.dot_general(left, ends[...], dims, preferred_element_type=F32)
    res_ref[0, plane] = flux - source


def add_face(plane, st_ref, res_ref, cond):
    face = face_term(cond[plane], cond[plane + 1], st_ref[0, 0, plane], st_ref[0, 0, plane + 1])
    res_ref[0, plane] = res_ref[0, plane] + face
    res_ref[0, plane + 1] = res_ref[0, plane + 1] - face


def edge_copy(me, count, side, edge_send, edge_recv, es_sem, er_sem):
    return pltpu.make_async_remote_copy(
        src_ref=edge_send.at[side],
        dst_ref=edge_recv.at[1 - side],
        send_sem=es_sem.at[side],
        recv_sem=er_sem.at[1 - side],
        device_id={"space": lax.rem(me + (1 if side else count - 1), count)},
        device_id_type=pl.DeviceIdType.MESH,
    )


def wells_of(cells_ref, rates_ref, cells, rates, ends):
    rate = rates_ref[...]
    high = rate.astype(BF).astype(F32)
    middle = (rate - high).astype(BF).astype(F32)
    for n, part in enumerate((high, middle, rate - high - middle)):
        lanes = slice(n * WELLS, (n + 1) * WELLS)
        cells[:, lanes] = cells_ref[...]
        rates[:, lanes] = part
    column = lax.broadcasted_iota(jnp.int32, ends.shape, 0)
    ends[...] = jnp.where((cells[...] & (NZ - 1)) == column, 1.0, 0.0).astype(BF)


def mix_modes(planes, count, jj, recv, wbuf, xf_ref, flat, spec, rows, mixed, turned):
    own = MY // count
    tiles = C * MZ // LANES
    slots = 2 * own * tiles
    pitch = slots + SKEW
    every = count * planes
    lane = lax.broadcasted_iota(jnp.int32, (1, LANES), 1)
    low = lane < 64
    even = lane % 64 < 32

    def unpack(plane, carry):
        for src in range(count):
            start = (plane * count + src) * pitch + jj * 2 * tiles
            flat[pl.ds(start, 2 * tiles), :] = recv[plane, src, mode_half(jj, count)].astype(F32)
        return carry

    lax.fori_loop(0, planes, unpack, 0)

    def column(p, t):
        return flat[pl.ds((jj * 2 + p) * tiles + t, every, stride=pitch), :].astype(BF)

    for pair in range(tiles // 2):
        right = jnp.concatenate(
            [
                jnp.concatenate([column(p, pair * 2 + half) for half in range(2)], 1)
                for p in range(2)
            ],
            0,
        )
        total = dot32(xf_ref[...], right)
        for half in range(2):
            part = total[:, half * LANES : (half + 1) * LANES].T
            for r in range(4):
                first = (pair * 2 + half) * 4 + r
                spec[pl.ds(first * (MZ + SKEW), MZ), : 2 * MX] = part[r * MZ : (r + 1) * MZ, :]
    groups = MZ // MODE_STEP
    for group in range(groups):
        base = group * MODE_STEP
        picked = [
            spec[pl.ds(base + r, C, stride=MZ + SKEW), : 2 * MX] for r in range(MODE_STEP)
        ]
        rows[group] = jnp.concatenate(picked, 0).T
    wide = MODE_STEP * C
    own_mode = lax.broadcasted_iota(jnp.int32, (MODE_STEP, wide), 0) == (
        lax.broadcasted_iota(jnp.int32, (MODE_STEP, wide), 1) // C
    )
    per = wide // (2 * C)

    def step(group, carry):
        first = pl.multiple_of(group * MODE_STEP, MODE_STEP)
        wfirst = pl.multiple_of(jj * MZ + group * MODE_STEP, MODE_STEP)
        for piece in range(MX // per):
            left = []
            for i in range(per):
                for q in range(2):
                    row = rows[group, pl.ds(q * MX + piece * per + i, MODE_STEP, stride=0), :]
                    left.append(jnp.where(own_mode, row, 0.0))
            lo = piece * wide
            weights = wbuf[pl.ds(wfirst, MODE_STEP), :, lo : lo + wide].reshape(wide, wide)
            both = dot32(jnp.concatenate(left, 0).astype(BF), weights)

            def part(i, q, t):
                at = (i * 2 + q) * MODE_STEP
                return both[at : at + MODE_STEP, t * LANES : (t + 1) * LANES]

            for t in range(2):
                real, imag = (
                    jnp.where(low, part(2 * t, q, t), part(2 * t + 1, q, t)) for q in range(2)
                )
                turn = jnp.where(even, -pltpu.roll(imag, LANES - C, 1), pltpu.roll(imag, C, 1))
                mixed[pl.ds(first, MODE_STEP), lo + t * LANES : lo + (t + 1) * LANES] = real + turn
        return carry

    lax.fori_loop(0, groups, step, 0)
    for block in range(MX * 2 * C // LANES):
        part = mixed[:, block * LANES : (block + 1) * LANES].T
        for r in range(4):
            first = (block * 4 + r) * (C + SKEW)
            turned[pl.ds(first, C), :MZ] = part[r * C : (r + 1) * C, :]


def mixed_tile(pair, turned):
    lane = lax.broadcasted_iota(jnp.int32, (1, LANES), 1)
    low = lane < 64
    even = lane % 64 < 32
    right = []
    for half in range(2):
        o = (pair * 2 + half) * 4
        a = [turned[pl.ds(o + r, 2 * MX, stride=C + SKEW), :] for r in range(4)]
        b = jnp.where(low, a[0], pltpu.roll(a[2], 64, 1))
        c = jnp.where(low, a[1], pltpu.roll(a[3], 64, 1))
        right.append(jnp.where(even, b, pltpu.roll(c, 32, 1)))
    return jnp.concatenate(right, 1).astype(BF)


def to_planes(table, tile, jj, pair, count, flat):
    own = MY // count
    tiles = C * MZ // LANES
    pitch = 2 * own * tiles + SKEW
    back = dot32(table, tile)
    every = back.shape[0] // 2
    for p in range(2):
        for half in range(2):
            slot = (jj * 2 + p) * tiles + pair * 2 + half
            flat[pl.ds(slot, every, stride=pitch), :] = back[
                p * every : (p + 1) * every, half * LANES : (half + 1) * LANES
            ]


def pack_planes(planes, count, first, targets, some, flat, send):
    slots = 2 * MY // count * C * MZ // LANES

    def pack(plane, carry):
        for dst in range(targets):
            start = (plane * targets + dst) * (slots + SKEW)
            for jj in some:
                part = mode_half(jj, count)
                rows = flat[pl.ds(start + part.start, part.size), :]
                send[plane, first + dst, part] = rows.astype(BF)
        return carry

    lax.fori_loop(0, planes, pack, 0)


def send_half(me, count, plane, other, send, recv, send_sem, recv_sem):
    near = count // 2
    owner = lax.rem(me + other * near, count)
    for shift in range(1, near):
        place = lax.rem(me + shift, near)
        pltpu.make_async_remote_copy(
            src_ref=send.at[plane, other * near + place],
            dst_ref=recv.at[plane, owner],
            send_sem=send_sem.at[plane, 0],
            recv_sem=recv_sem.at[plane, 0],
            device_id={"space": me // near * near + place},
            device_id_type=pl.DeviceIdType.MESH,
        ).start()
    recv[plane, owner] = send[plane, other * near + lax.rem(me, near)]


def swap_tile(me, count, n, own, other, send_sem, recv_sem):
    return pltpu.make_async_remote_copy(
        src_ref=own.at[n],
        dst_ref=other.at[n],
        send_sem=send_sem.at[n],
        recv_sem=recv_sem.at[n],
        device_id={"space": lax.rem(me + count // 2, count)},
        device_id_type=pl.DeviceIdType.MESH,
    )


def whole_kernel(
    planes, count, feat_ref, perm_ref, lift_in, lift_out, point, dec_in, dec_out, zf_ref, zi_ref,
    yf_ref, yi_ref, xf_ref, xi_ref, xh_ref, cells_ref, rates_ref, w_hbm, st_ref, res_ref,
    hid, wbuf, send_f, recv_f, send_b, recv_b, flat, spec, rows, mixed, turned, zs, sp, xs, plain,
    in_ref, lo_ref, kp_ref, di_ref, do_ref, cond, cells, rates, ends, edge_send, edge_recv,
    own_mixed, other_mixed,
    w_sem, sf_sem, rf_sem, sb_sem, rb_sem, es_sem, er_sem, om_sem, rm_sem,
):
    me = lax.axis_index("space")
    barrier = pltpu.get_barrier_semaphore()
    for shift in range(1, count):
        pl.semaphore_signal(
            barrier,
            inc=1,
            device_id={"space": lax.rem(me + shift, count)},
            device_id_type=pl.DeviceIdType.MESH,
        )
    fetch = pltpu.make_async_copy(w_hbm.at[0], wbuf, w_sem.at[0])
    fetch.start()
    xs[...] = jnp.zeros_like(xs)
    in_ref[...] = diag_of(lift_in[...], ROWS, 8, 0.5)
    lo_ref[...] = diag_of(lift_out[...], 2, lift_out.shape[1], 1.0, True)
    for layer in range(LAYERS):
        kp_ref[layer] = diag_of(point[layer], ROWS, C, 0.5)
    di_ref[...] = diag_of(dec_in[...], ROWS, C, 0.5)
    dec = dec_out.shape[1]
    do_ref[...] = spread(
        dec_out[...],
        2 * ROWS,
        ROWS * dec,
        lambda i: i // ROWS,
        lambda j: j % dec,
        lambda i, j: i % ROWS == j // dec,
        1.0,
        True,
    )
    wells_of(cells_ref, rates_ref, cells, rates, ends)
    pl.semaphore_wait(barrier, count - 1)

    def over(body):
        def run(plane, carry):
            body(plane)
            return carry

        lax.fori_loop(0, planes, run, 0)

    own = MY // count

    def send_forward(plane, soon):
        send_modes(me, count, plane, 0, send_f, recv_f, sf_sem, rf_sem)

        @pl.when(plane < soon)
        def _():
            send_rest(plane)

    def send_rest(plane):
        for jj in range(1, own):
            send_modes(me, count, plane, jj, send_f, recv_f, sf_sem, rf_sem)

    def send_late(soon):
        lax.fori_loop(soon, planes, lambda plane, carry: (send_rest(plane), carry)[1], 0)

    def lift(plane):
        lift_plane(plane, feat_ref, perm_ref, in_ref, lo_ref, hid, plain, xs, zs)
        to_modes(plane, count, zf_ref, yf_ref, zs, flat, send_f)
        send_forward(plane, SOON[0])

    over(lift)
    send_late(SOON[0])
    for layer in range(LAYERS):
        fetch.wait()
        last = layer + 1 == LAYERS
        tile_pairs = C * MZ // LANES // 2

        def turn(index):
            return lax.rem(planes - index, planes) if last else index

        def send_back(jj):
            def one(n, carry):
                if jj > 0:

                    @pl.when(n >= EARLY)
                    def _():
                        for before in range(jj):
                            send_modes(me, count, turn(n), before, send_b, recv_b, sb_sem, rb_sem)

                if jj + 1 == own:
                    send_modes(me, count, turn(n), jj, send_b, recv_b, sb_sem, rb_sem)
                return carry

            if jj + 1 < own:
                for n in range(EARLY):
                    send_modes(me, count, (planes - n) % planes, jj, send_b, recv_b, sb_sem, rb_sem)
            else:
                lax.fori_loop(0, planes, one, 0)

        swaps = [
            swap_tile(me, count, n, own_mixed, other_mixed, om_sem, rm_sem)
            for n in range(0 if last else own * tile_pairs)
        ]
        for jj in range(own):
            over(lambda plane: wait_modes(count, plane, jj, recv_f, rf_sem))
            mix_modes(planes, count, jj, recv_f, wbuf, xf_ref, flat, spec, rows, mixed, turned)
            for pair in range(tile_pairs):
                tile = mixed_tile(pair, turned)
                if last:
                    to_planes(xi_ref[...], tile, jj, pair, count, flat)
                else:
                    n = jj * tile_pairs + pair
                    own_mixed[n] = tile
                    swaps[n].start()
            if last:
                pack_planes(planes, count, 0, count, (jj,), flat, send_b)
                send_back(jj)
        for jj in range(own):
            over(lambda plane: wait_modes(count, plane, jj, send_f, sf_sem))
        if not last:
            fetch = pltpu.make_async_copy(w_hbm.at[layer + 1], wbuf, w_sem.at[layer + 1])
            fetch.start()

        if not last:
            near = count // 2
            parts = 2 * (near - 1)
            table = xh_ref.at[me // near]
            for other in range(2):
                for n, swap in enumerate(swaps):
                    if other:
                        swap.wait_recv()
                    tile = other_mixed[n] if other else own_mixed[n]
                    to_planes(table[...], tile, n // tile_pairs, n % tile_pairs, count, flat)
                pack_planes(planes, count, other * near, near, range(own), flat, send_b)
                over(lambda n: send_half(me, count, n, other, send_b, recv_b, sb_sem, rb_sem))
            for swap in swaps:
                swap.wait_send()
        kp = kp_ref.at[layer]

        def settle(plane, buffer, sem):
            if not last:
                wait_plane(parts, plane, buffer, sem)
            for jj in range(own if last else 0):
                wait_modes(count, plane, jj, buffer, sem)


        def rest(index):
            plane = turn(index)
            settle(plane, recv_b, rb_sem)
            from_modes(plane, count, recv_b, yi_ref, zi_ref, flat, sp)
            if not last:
                middle_plane(plane, kp, hid, sp, zs)
                to_modes(plane, count, zf_ref, yf_ref, zs, flat, send_f)
                send_forward(plane, SOON[1])
            else:
                final_plane(plane, kp, di_ref, do_ref, perm_ref, hid, sp, st_ref)
                residual_plane(
                    plane, me, planes, perm_ref, cells, rates, ends, st_ref, res_ref, cond
                )

                @pl.when(index == 1)
                def _():
                    for side in range(2):
                        edge_send[side, 0] = st_ref[0, 0, side * (planes - 1)].astype(BF)
                        edge_send[side, 1] = cond[side * (planes - 1)].astype(BF)
                        edge_copy(me, count, side, edge_send, edge_recv, es_sem, er_sem).start()

                @pl.when(index >= 2)
                def _():
                    add_face(plane, st_ref, res_ref, cond)

        over(rest)
        if not last:
            send_late(SOON[1])
        over(lambda plane: settle(plane, send_b, sb_sem))
    add_face(0, st_ref, res_ref, cond)
    for side in range(2):
        edge_copy(me, count, side, edge_send, edge_recv, es_sem, er_sem).wait()
    for side in range(2):
        plane = side * (planes - 1)
        press, conduct = (edge_recv[side, n].astype(F32) for n in range(2))
        face = face_term(cond[plane], conduct, st_ref[0, 0, plane], press)
        inside = me < count - 1 if side else me > 0
        res_ref[0, plane] = res_ref[0, plane] + jnp.where(inside, face, 0.0)


def ones_where(shape, test, value=1.0):
    row = lax.broadcasted_iota(jnp.int32, shape, 0)
    col = lax.broadcasted_iota(jnp.int32, shape, 1)
    return jnp.where(test(row, col), value, 0.0)


def spread(matrix, rows, cols, row_of, col_of, keep, value, turned):
    depth, height = matrix.shape[::-1] if turned else matrix.shape
    take = ones_where((rows, height), lambda i, j: row_of(i) == j).astype(BF)
    put = ones_where((depth, cols), lambda i, j: col_of(j) == i).astype(BF)
    dims = (((1,), (0 if turned else 1,)), ((), ()))
    part = lax.dot_general(take, matrix, dims, preferred_element_type=F32)
    return (dot32(part.astype(BF), put) * ones_where((rows, cols), keep, value)).astype(BF)


def diag_of(matrix, copies, width, value, turned=False):
    height = matrix.shape[0 if turned else 1]
    return spread(
        matrix,
        copies * height,
        copies * width,
        lambda i: i % height,
        lambda j: j % width,
        lambda i, j: i // height == j // width,
        value,
        turned,
    )


def local_fast(
    features,
    log_perm,
    well_cells,
    well_rates,
    lift_in,
    lift_out,
    spec_weight,
    point_weight,
    dec_in,
    dec_out,
):
    planes = features.shape[2]
    count = lax.axis_size("space")
    own = MY // count
    modes = own * MZ
    slots = 2 * modes * C // LANES
    tables = tables_for(count)
    lift, dec = lift_in.shape[1], dec_in.shape[1]
    operands = (
        features,
        log_perm,
        lift_in,
        lift_out.T,
        point_weight,
        dec_in,
        dec_out.T,
    ) + tuple(tables[name] for name in ("zf", "zi", "yf", "yi", "xf", "xi", "xh"))
    operands = operands + (well_cells, well_rates)
    vmem = pl.BlockSpec(memory_space=pltpu.VMEM)
    exchange = pltpu.VMEM((planes, count, slots, LANES), BF)
    results = pl.pallas_call(
        lambda *refs: whole_kernel(planes, count, *refs),
        in_specs=[vmem] * len(operands) + [pl.BlockSpec(memory_space=pl.ANY)],
        out_specs=[vmem, vmem],
        out_shape=[
            jax.ShapeDtypeStruct((1, 2, planes, NY, NZ), F32),
            jax.ShapeDtypeStruct((1, planes, NY, NZ), F32),
        ],
        scratch_shapes=[
            pltpu.VMEM((planes, PAIRS * C, 2 * NZ), BF),
            pltpu.VMEM(spec_weight.shape[1:], BF),
            exchange,
            exchange,
            exchange,
            exchange,
            pltpu.VMEM((planes * count * (slots + SKEW), LANES), F32),
            pltpu.VMEM((C * (MZ + SKEW), LANES), F32),
            pltpu.VMEM((MZ // MODE_STEP, 2 * MX, MODE_STEP * C), F32),
            pltpu.VMEM((MZ, MX * 2 * C), F32),
            pltpu.VMEM((2 * MX * (C + SKEW), LANES), F32),
            pltpu.VMEM((2, C * PITCH, LANES), F32),
            pltpu.VMEM((2, PAIRS * (C + SKEW), LANES), F32),
            pltpu.VMEM((2, PAIRS * 8, NZ), F32),
            pltpu.VMEM((NY, NZ), F32),
            pltpu.VMEM((ROWS * lift, ROWS * 8), BF),
            pltpu.VMEM((2 * C, 2 * lift), BF),
            pltpu.VMEM((LAYERS, ROWS * C, ROWS * C), BF),
            pltpu.VMEM((ROWS * dec, ROWS * C), BF),
            pltpu.VMEM((2 * ROWS, ROWS * dec), BF),
            pltpu.VMEM((planes, NY, NZ), F32),
            pltpu.VMEM((1, 3 * WELLS), jnp.int32),
            pltpu.VMEM((1, 3 * WELLS), F32),
            pltpu.VMEM((NZ, 3 * WELLS), BF),
            pltpu.VMEM((2, 2, NY, NZ), BF),
            pltpu.VMEM((2, 2, NY, NZ), BF),
            pltpu.VMEM((modes * C // 256, 2 * MX, 256), BF),
            pltpu.VMEM((modes * C // 256, 2 * MX, 256), BF),
            pltpu.SemaphoreType.DMA((LAYERS,)),
        ]
        + [pltpu.SemaphoreType.DMA((planes, own))] * 4
        + [pltpu.SemaphoreType.DMA((2,))] * 2
        + [pltpu.SemaphoreType.DMA((modes * C // 256,))] * 2,
        compiler_params=pltpu.CompilerParams(
            collective_id=0, has_side_effects=True, vmem_limit_bytes=60 * 1024 * 1024
        ),
        name="whole",
    )(*operands, spec_weight)
    return handed_on(results)


def handed_on(results):
    pieces = [
        (n, at) for n, each in enumerate(results) for at in np.ndindex(*each.shape[:-2])
    ]

    def body(*refs):
        source, target, held = refs[:2], refs[2:4], refs[4:6]
        in_sem, out_sem = refs[6:]
        loads = [
            pltpu.make_async_copy(source[n].at[at], held[n].at[at], in_sem.at[k])
            for k, (n, at) in enumerate(pieces)
        ]
        stores = [
            pltpu.make_async_copy(held[n].at[at], target[n].at[at], out_sem.at[k])
            for k, (n, at) in enumerate(pieces)
        ]
        for load in loads:
            load.start()
        for load, store in zip(loads, stores):
            load.wait()
            store.start()
        for store in stores:
            store.wait()

    whole = pl.BlockSpec(memory_space=pl.ANY)
    return pl.pallas_call(
        body,
        in_specs=[whole] * 2,
        out_specs=[whole] * 2,
        out_shape=[jax.ShapeDtypeStruct(each.shape, each.dtype) for each in results],
        scratch_shapes=[pltpu.VMEM(each.shape, each.dtype) for each in results]
        + [pltpu.SemaphoreType.DMA((len(pieces),))] * 2,
        compiler_params=pltpu.CompilerParams(vmem_limit_bytes=60 * 1024 * 1024),
        name="handed_on",
    )(*results)


def local(features, log_perm, well_cells, well_rates, lift_in, lift_out, spec_weight, *rest):
    batches, planes = features.shape[0], features.shape[2]
    count = lax.axis_size("space")
    fits = batches == 1 and planes == 8 and count % 8 == 0 and MY == 2 * count
    run = local_fast if fits else local_general
    return run(
        features, log_perm, well_cells, well_rates, lift_in, lift_out, spec_weight, *rest
    )


def solution(mesh):
    return jax.shard_map(
        local,
        mesh=mesh,
        in_specs=(
            P("sample", None, "space", None, None),
            P("sample", "space", None, None),
            P("sample", None),
            P("sample", None),
            P(),
            P(),
            P(None, "space", None, None),
            P(),
            P(),
            P(),
        ),
        out_specs=(P("sample", None, "space", None, None), P("sample", "space", None, None)),
        check_vma=False,
    )
```

```python
import math

import jax
import jax.numpy as jnp
import numpy as np
from jax import lax
from jax.experimental import pallas as pl
from jax.experimental.pallas import tpu as pltpu
from jax.sharding import PartitionSpec as P

NX = 128
NY = 128
NZ = 128
MX = 32
MY = 32
MZ = 32
C = 32
FIN = 4
LAYERS = 2
WELLS = 32


def padded_2(block, sides, width):
    for axis, dim in sides:
        count = lax.axis_size(axis)
        forward = [(i, i + 1) for i in range(count - 1)]
        backward = [(target, source) for source, target in forward]
        low = lax.ppermute(
            lax.slice_in_dim(block, block.shape[dim] - width, None, axis=dim), axis, forward
        )
        high = lax.ppermute(lax.slice_in_dim(block, 0, width, axis=dim), axis, backward)
        block = jnp.concatenate([low, block, high], axis=dim)
    return block


def freq_table(length, kept, one_sided):
    indices = jnp.arange(kept, dtype=jnp.int32)
    if one_sided:
        return indices
    return jnp.where(indices < kept // 2, indices, length - kept + indices)


def wave_parts(length, kept, one_sided):
    freqs = freq_table(length, kept, one_sided)
    places = jnp.arange(length, dtype=jnp.int32)
    phase_turns = freqs[:, None] * places[None, :] % length
    angles = phase_turns.astype(jnp.float32) * (2.0 * math.pi / length)
    norm_scale = 1.0 / math.sqrt(length)
    return (jnp.cos(angles) * norm_scale, jnp.sin(angles) * norm_scale)


def forward_table(length, kept):
    cosine_vals, sine_vals = wave_parts(length, kept, False)
    return jnp.stack(
        [jnp.stack([cosine_vals.T, -sine_vals.T], 1), jnp.stack([sine_vals.T, cosine_vals.T], 1)], 1
    ).astype(jnp.bfloat16)


def inverse_table(length, kept):
    cosine_vals, sine_vals = wave_parts(length, kept, False)
    return jnp.stack(
        [jnp.stack([cosine_vals, sine_vals], 1), jnp.stack([-sine_vals, cosine_vals], 1)], 1
    ).astype(jnp.bfloat16)


def z_tables():
    cosine_vals, sine_vals = wave_parts(NZ, MZ, True)
    weights_k = jnp.where(jnp.arange(MZ) == 0, 1.0, 2.0).astype(jnp.float32)[:, None]
    z_forward = jnp.concatenate([cosine_vals.T, -sine_vals.T], 1).astype(jnp.bfloat16)
    z_inverse = jnp.concatenate([weights_k * cosine_vals, -weights_k * sine_vals], 0).astype(
        jnp.bfloat16
    )
    return (z_forward, z_inverse)


def gelu_tanh(values):
    return jax.nn.gelu(values, approximate=True)


def face_term(cond_a, cond_b, press_a, press_b):
    return 2.0 * cond_a * cond_b / (cond_a + cond_b) * (press_a - press_b)


def mobility_of(saturation, log_values):
    return jnp.exp(log_values) * (
        saturation * saturation + 0.5 * (1.0 - saturation) * (1.0 - saturation)
    )


def darcy(pressure, conduct, well_cells, well_rates):
    batches, planes = pressure.shape[0], pressure.shape[1]
    space_index = lax.axis_index("space")
    pad_cond = jnp.pad(conduct, ((0, 0), (0, 0), (1, 1), (1, 1)))
    pad_press = jnp.pad(pressure, ((0, 0), (0, 0), (1, 1), (1, 1)))
    flux_sum = face_term(conduct, pad_cond[:, :, 2:, 1:-1], pressure, pad_press[:, :, 2:, 1:-1])
    flux_sum = flux_sum + face_term(
        conduct, pad_cond[:, :, :-2, 1:-1], pressure, pad_press[:, :, :-2, 1:-1]
    )
    flux_sum = flux_sum + face_term(
        conduct, pad_cond[:, :, 1:-1, 2:], pressure, pad_press[:, :, 1:-1, 2:]
    )
    flux_sum = flux_sum + face_term(
        conduct, pad_cond[:, :, 1:-1, :-2], pressure, pad_press[:, :, 1:-1, :-2]
    )
    fields = jnp.stack([pressure, conduct], 1)
    padded = padded_2(fields.astype(jnp.bfloat16), (("space", 2),), 1).astype(fields.dtype)
    press_low = padded[:, 0, 0]
    press_high = padded[:, 0, -1]
    cond_low = padded[:, 1, 0]
    cond_high = padded[:, 1, -1]
    press_below = jnp.concatenate([press_low[:, None], pressure[:, :-1]], 1)
    cond_below = jnp.concatenate([cond_low[:, None], conduct[:, :-1]], 1)
    press_above = jnp.concatenate([pressure[:, 1:], press_high[:, None]], 1)
    cond_above = jnp.concatenate([conduct[:, 1:], cond_high[:, None]], 1)
    lower_terms = face_term(conduct, cond_below, pressure, press_below)
    upper_terms = face_term(conduct, cond_above, pressure, press_above)
    flux_sum = flux_sum + lower_terms + upper_terms
    well_x = well_cells // (NY * NZ) - space_index * planes
    well_y = well_cells // NZ % NY
    well_z = well_cells % NZ
    onehot_x = (well_x[:, :, None] == jnp.arange(planes, dtype=jnp.int32)[None, None, :]).astype(
        jnp.float32
    ) * well_rates[:, :, None]
    onehot_y = (well_y[:, :, None] == jnp.arange(NY, dtype=jnp.int32)[None, None, :]).astype(
        jnp.float32
    )
    onehot_z = (well_z[:, :, None] == jnp.arange(NZ, dtype=jnp.int32)[None, None, :]).astype(
        jnp.float32
    )
    plane_rows = (onehot_x[:, :, :, None] * onehot_y[:, :, None, :]).reshape(
        batches, WELLS, planes * NY
    )
    source = jnp.einsum(
        "bwa,bwz->baz", plane_rows, onehot_z, precision=lax.Precision.HIGHEST
    ).reshape(batches, planes, NY, NZ)
    return flux_sum - source


def local_general(
    features,
    log_perm,
    well_cells,
    well_rates,
    lift_in,
    lift_out,
    spec_weight,
    point_weight,
    dec_in,
    dec_out,
):
    batches = features.shape[0]
    planes = features.shape[2]
    space_index = lax.axis_index("space")
    block = spec_weight.shape[1]
    cell_count = planes * NY * NZ
    z_forward, z_inverse = z_tables()
    y_forward = forward_table(NY, MY)
    y_inverse = inverse_table(NY, MY)
    x_forward = forward_table(NX, MX)
    x_inverse = inverse_table(NX, MX)
    perm_b = log_perm.astype(jnp.bfloat16).reshape(batches, 1, cell_count)
    lift_input = jnp.concatenate([features.reshape(batches, FIN, cell_count), perm_b], 1)
    lift_hidden = jnp.einsum("bfn,fh->bhn", lift_input, lift_in, preferred_element_type=jnp.float32)
    lifted = gelu_tanh(lift_hidden).astype(jnp.bfloat16)
    hidden_state = jnp.einsum(
        "bhn,hc->bcn", lifted, lift_out, preferred_element_type=jnp.float32
    ).astype(jnp.bfloat16)
    for layer_idx in range(LAYERS):
        zspec = jnp.dot(hidden_state.reshape(-1, NZ), z_forward, preferred_element_type=jnp.float32)
        zspec = zspec.astype(jnp.bfloat16).reshape(batches * C * planes, NY, 2, MZ)
        yz_spec = jnp.einsum(
            "aypk,ypqj->aqjk", zspec, y_forward, preferred_element_type=jnp.float32
        )
        yz_spec = yz_spec.astype(jnp.bfloat16).reshape(batches, C, planes, 2, MY * MZ)
        mode_weights = spec_weight[layer_idx].reshape(block, C, MX, 2, C)
        spectrum = jnp.einsum(
            "bcxpm,xpqi->bcqim",
            lax.all_to_all(yz_spec, "space", split_axis=4, concat_axis=2, tiled=True),
            x_forward,
            preferred_element_type=jnp.float32,
        ).astype(jnp.bfloat16)
        products = jnp.einsum(
            "bcqim,mcipo->bimqpo", spectrum, mode_weights, preferred_element_type=jnp.float32
        )
        real_part = products[:, :, :, 0, 0] - products[:, :, :, 1, 1]
        imag_part = products[:, :, :, 0, 1] + products[:, :, :, 1, 0]
        mixed_modes = jnp.stack([real_part, imag_part], 3).astype(jnp.bfloat16)
        back_field = jnp.einsum(
            "bimqo,iqpx->boxpm", mixed_modes, x_inverse, preferred_element_type=jnp.float32
        ).astype(jnp.bfloat16)
        returned = lax.all_to_all(back_field, "space", split_axis=2, concat_axis=4, tiled=True)
        returned = returned.reshape(batches * C * planes, 2, MY, MZ)
        y_back = jnp.einsum(
            "aqjk,jqpy->aypk", returned, y_inverse, preferred_element_type=jnp.float32
        ).astype(jnp.bfloat16)
        spectral = jnp.dot(
            y_back.reshape(-1, 2 * MZ), z_inverse, preferred_element_type=jnp.float32
        ).reshape(batches, C, cell_count)
        local_term = jnp.einsum(
            "bcn,co->bon", hidden_state, point_weight[layer_idx], preferred_element_type=jnp.float32
        )
        hidden_state = gelu_tanh(spectral + local_term).astype(jnp.bfloat16)
    decoded = gelu_tanh(
        jnp.einsum("bcn,cd->bdn", hidden_state, dec_in, preferred_element_type=jnp.float32)
    ).astype(jnp.bfloat16)
    decoded_out = jnp.einsum("bdn,de->ben", decoded, dec_out, preferred_element_type=jnp.float32)
    pressure = decoded_out[:, 0].reshape(batches, planes, NY, NZ)
    saturation = jax.nn.sigmoid(decoded_out[:, 1]).reshape(batches, planes, NY, NZ)
    states = jnp.stack([pressure, saturation], 1)
    conduct = mobility_of(saturation, log_perm)
    return (states, darcy(pressure, conduct, well_cells, well_rates))


BF = jnp.bfloat16
F32 = jnp.float32
PAIRS = NY // 2
SKEW = 4
PITCH = PAIRS + SKEW
MODE_STEP = 8
SOON = (5, 3)
EARLY = 3
ROWS = 8
LOOK = 4
LAG = 1
MID = 3
TB = 2
FB = 4
LANES = 128


def np_waves(length, kept, one_sided):
    index = np.arange(kept)
    freqs = index if one_sided else np.where(index < kept // 2, index, length - kept + index)
    angles = (freqs[:, None] * np.arange(length)[None, :] % length) * (2.0 * math.pi / length)
    norm = 1.0 / math.sqrt(length)
    return np.cos(angles) * norm, np.sin(angles) * norm


def np_forward(length, kept):
    cosine, sine = np_waves(length, kept, False)
    return np.stack([np.stack([cosine.T, -sine.T], 1), np.stack([sine.T, cosine.T], 1)], 1)


def np_inverse(length, kept):
    cosine, sine = np_waves(length, kept, False)
    return np.stack([np.stack([cosine, sine], 1), np.stack([-sine, cosine], 1)], 1)


def by_plane(table, axis, count):
    planes = NX // count
    order = np.arange(NX).reshape(count, planes).T.reshape(-1)
    return np.take(table, order, axis)


def tables_for(count):
    own = MY // count
    cosine, sine = np_waves(NZ, MZ, True)
    twice = np.where(np.arange(MZ) == 0, 1.0, 2.0)[:, None]
    z_forward = np.concatenate([cosine.T, -sine.T], 1)
    z_inverse = np.concatenate([twice * cosine, -twice * sine], 0)
    y_forward = np_forward(NY, MY).reshape(PAIRS, 2, 2, 2, count, own)
    y_inverse = np_inverse(NY, MY).reshape(count, own, 2, 2, PAIRS, 2)
    four = np.eye(4)
    z_forward = np.einsum("zpk,cd->czpdk", z_forward.reshape(NZ, 2, MZ), four)
    z_inverse = np.einsum("pkz,cd->pckdz", z_inverse.reshape(2, MZ, NZ), four)
    tables = {
        "zf": z_forward.reshape(4 * NZ, 8 * MZ),
        "zi": 0.5 * z_inverse.reshape(8 * MZ, 4 * NZ),
        "yf": y_forward.transpose(3, 5, 4, 1, 2, 0).reshape(2 * MY, 2 * NY),
        "yi": y_inverse.transpose(5, 3, 4, 2, 1, 0).reshape(2 * NY, 2 * MY),
        "xf": by_plane(np_forward(NX, MX).transpose(2, 3, 1, 0), 3, count).reshape(2 * MX, 2 * NX),
        "xi": by_plane(np_inverse(NX, MX).transpose(2, 3, 0, 1), 1, count).reshape(2 * NX, 2 * MX),
    }
    halves = tables["xi"].reshape(2, NX // count, 2, count // 2, 2 * MX)
    tables["xh"] = halves.transpose(2, 0, 1, 3, 4).reshape(2, NX, 2 * MX)
    return {name: jnp.asarray(table.astype(np.float32)).astype(BF) for name, table in tables.items()}


def dot32(a, b):
    return jnp.dot(a, b, preferred_element_type=F32)


def gelu_of_half(values):
    u = values.astype(BF)
    scale = math.sqrt(2.0 / math.pi)
    inner = u * (BF(2.0 * scale) + BF(8.0 * scale * 0.044715) * (u * u))
    return u + u * jnp.tanh(inner)


def mode_half(jj, count):
    span = 2 * C * MZ // LANES
    return pl.ds(jj * span, span)


def others(me, count):
    return [lax.rem(me + shift, count) for shift in range(1, count)]


def send_modes(me, count, plane, jj, send, recv, send_sem, recv_sem):
    part = mode_half(jj, count)
    for target in others(me, count):
        pltpu.make_async_remote_copy(
            src_ref=send.at[plane, target, part],
            dst_ref=recv.at[plane, me, part],
            send_sem=send_sem.at[plane, jj],
            recv_sem=recv_sem.at[plane, jj],
            device_id={"space": target},
            device_id_type=pl.DeviceIdType.MESH,
        ).start()
    recv[plane, me, part] = send[plane, me, part]


def wait_modes(count, plane, jj, buffer, sem):
    part = buffer.at[plane, pl.ds(0, count - 1), mode_half(jj, count)]
    pltpu.make_async_copy(part, part, sem.at[plane, jj]).wait()


def wait_plane(parts, plane, buffer, sem):
    part = buffer.at[plane, pl.ds(0, parts)]
    pltpu.make_async_copy(part, part, sem.at[plane, 0]).wait()


def slot_of(s, count):
    own = MY // count
    return (s % own * 2 + s // own) * (C * MZ // LANES)


def to_modes(plane, count, zf_ref, yf_ref, zs, flat, send):
    tiles = C * MZ // LANES
    slots = 2 * MY // count * tiles
    halves = {}
    for first in range(0, tiles, 2 * TB):
        some = [(group, y2) for group in range(first, first + 2 * TB) for y2 in range(2)]
        left = [
            jnp.concatenate(
                [zs[y2, pl.ds((group * 4 + r) * PITCH, PAIRS), :] for r in range(4)], 1
            ).astype(BF)
            for group, y2 in some
        ]
        waves = dot32(jnp.concatenate(left, 0), zf_ref[...]).astype(BF)
        for n, key in enumerate(some):
            halves[key] = waves[n * PAIRS : (n + 1) * PAIRS, :]
    for pair in range(tiles // 2):
        columns = []
        for group in (pair * 2, pair * 2 + 1):
            parts = [
                halves[group, y2][:, p * LANES : (p + 1) * LANES] for y2 in range(2) for p in range(2)
            ]
            columns.append(jnp.concatenate(parts, 0))
        modes = dot32(yf_ref[...], jnp.concatenate(columns, 1))
        for s in range(2 * MY // count):
            for half in range(2):
                slot = slot_of(s, count) + pair * 2 + half
                flat[pl.ds(slot, count, stride=slots + SKEW), :] = modes[
                    s * count : (s + 1) * count, half * LANES : (half + 1) * LANES
                ]
    for dst in range(count):
        send[plane, dst] = flat[pl.ds(dst * (slots + SKEW), slots), :].astype(BF)


def lay_out(zs, start, values):
    for y2 in range(2):
        for r in range(ROWS):
            zs[y2, pl.ds(start + r, C, stride=PITCH), :] = values[
                r * C : (r + 1) * C, y2 * NZ : (y2 + 1) * NZ
            ]


def hid_rows(index):
    return pl.ds(index * ROWS * C, ROWS * C)


def lift_plane(plane, feat_ref, perm_ref, in_ref, lo_ref, hid, plain, xs, zs):
    for f in range(FIN + 1):
        plain[...] = perm_ref[0, plane] if f == FIN else feat_ref[0, f, plane].astype(F32)
        for y2 in range(2):
            xs[y2, pl.ds(f, PAIRS, stride=8), :] = plain[pl.ds(y2, PAIRS, stride=2), :]
    width = lo_ref.shape[1]
    parts = in_ref.shape[0] // width
    total = PAIRS // ROWS * parts

    def first(n):
        u, r = n // parts, n % parts
        x = jnp.concatenate([xs[y2, pl.ds(u * ROWS * 8, ROWS * 8), :] for y2 in range(2)], 1)
        return dot32(in_ref[r * width : (r + 1) * width, :], x.astype(BF))

    ahead = {n: first(n) for n in range(LOOK)}
    raw = {}

    def finish(n):
        if n % parts == parts - 1:
            u = n // parts
            hidden = jnp.concatenate([raw.pop(u * parts + r) for r in range(parts)], 0)
            hid[plane, hid_rows(u), :] = hidden.astype(BF)
            lay_out(zs, u * ROWS, hidden)

    for n in range(total):
        if n + LOOK < total:
            ahead[n + LOOK] = first(n + LOOK)
        raw[n] = dot32(lo_ref[...], gelu_of_half(ahead.pop(n)))
        if n >= LAG:
            finish(n - LAG)
    for n in range(total - LAG, total):
        finish(n)


def from_modes(plane, count, recv, yi_ref, zi_ref, flat, sp):
    tiles = C * MZ // LANES
    slots = 2 * MY // count * tiles
    for src in range(count):
        flat[pl.ds(src * (slots + SKEW), slots), :] = recv[plane, src].astype(F32)

    def back_of(pair):
        rows = []
        for s in range(2 * MY // count):
            part = [
                flat[pl.ds(slot_of(s, count) + pair * 2 + half, count, stride=slots + SKEW), :]
                for half in range(2)
            ]
            rows.append(jnp.concatenate(part, 1))
        return dot32(yi_ref[...], jnp.concatenate(rows, 0).astype(BF)).astype(BF)

    for first in range(0, tiles // 2, FB):
        left, some = [], []
        for pair in range(first, first + FB):
            back = back_of(pair)
            for half in range(2):
                lanes = slice(half * LANES, (half + 1) * LANES)
                for y2 in range(2):
                    parts = [
                        back[(y2 * 2 + p) * PAIRS : (y2 * 2 + p + 1) * PAIRS, lanes] for p in range(2)
                    ]
                    left.append(jnp.concatenate(parts, 1))
                    some.append(((pair * 2 + half) * 4, y2))
        field = dot32(jnp.concatenate(left, 0), zi_ref[...])
        for n, (o, y2) in enumerate(some):
            for r in range(4):
                sp[y2, pl.ds(o + r, PAIRS, stride=C + SKEW), :] = field[
                    n * PAIRS : (n + 1) * PAIRS, r * NZ : (r + 1) * NZ
                ]


def field_rows(index, sp):
    halves = []
    for y2 in range(2):
        rows = [sp[y2, pl.ds((index * ROWS + r) * (C + SKEW), C), :] for r in range(ROWS)]
        halves.append(jnp.concatenate(rows, 0))
    return jnp.concatenate(halves, 1)


def middle_plane(plane, kp, hid, sp, zs):
    total = PAIRS // ROWS

    def local_term(index):
        return dot32(kp[...], hid[plane, hid_rows(index), :])

    ahead = {n: local_term(n) for n in range(MID)}
    for n in range(total):
        if n + MID < total:
            ahead[n + MID] = local_term(n + MID)
        hidden = gelu_of_half(ahead.pop(n) + field_rows(n, sp))
        hid[plane, hid_rows(n), :] = hidden
        lay_out(zs, n * ROWS, hidden.astype(F32))


def final_plane(plane, kp, di_ref, do_ref, perm_ref, hid, sp, st_ref):
    total = PAIRS // ROWS
    width = di_ref.shape[1]
    parts = di_ref.shape[0] // width

    def local_term(index):
        return dot32(kp[...], hid[plane, hid_rows(index), :])

    def mixed(n):
        return gelu_of_half(ahead.pop(n) + field_rows(n, sp))

    def decode(hidden, r):
        return dot32(di_ref[r * width : (r + 1) * width, :], hidden)

    def shrink(n, r):
        return dot32(do_ref[:, r * width : (r + 1) * width], gelu_of_half(raw.pop((n, r))))

    ahead = {n: local_term(n) for n in range(MID)}
    raw = {}
    hiddens = {0: mixed(0)}
    for r in range(parts):
        raw[0, r] = decode(hiddens[0], r)
    hiddens[1] = mixed(1)
    for n in range(total):
        if n + MID < total:
            ahead[n + MID] = local_term(n + MID)
        both = 0.0
        for r in range(parts):
            if n + 1 < total:
                raw[n + 1, r] = decode(hiddens[n + 1], r)
            both = both + shrink(n, r)
            if r == 0 and n + 2 < total:
                hiddens[n + 2] = mixed(n + 2)
        for y2 in range(2):
            lanes = slice(y2 * NZ, (y2 + 1) * NZ)
            where = pl.ds(n * ROWS * 2 + y2, ROWS, stride=2)
            st_ref[0, 0, plane, where, :] = both[:ROWS, lanes]
            st_ref[0, 1, plane, where, :] = both[ROWS:, lanes]

def residual_plane(plane, me, planes, perm_ref, cells, rates, ends, st_ref, res_ref, cond):
    sat = jax.nn.sigmoid(st_ref[0, 1, plane])
    st_ref[0, 1, plane] = sat
    conduct = mobility_of(sat, perm_ref[0, plane])
    cond[plane] = conduct
    pressure = st_ref[0, 0, plane]
    flux = 0.0
    for axis in range(2):
        length = pressure.shape[axis]
        inner = lax.broadcasted_iota(jnp.int32, pressure.shape, axis) < length - 1
        beyond = (pltpu.roll(field, length - 1, axis) for field in (conduct, pressure))
        cond_next, press_next = beyond
        face = jnp.where(inner, face_term(conduct, cond_next, pressure, press_next), 0.0)
        flux = flux + face - pltpu.roll(face, 1, axis)
    shape = (NY, cells.shape[1])
    here = cells[...] - (me * planes + plane) * (NY * NZ)
    starts = lax.broadcasted_iota(jnp.int32, shape, 0) * NZ
    offset = here - starts
    hit = (offset >= 0) & (offset < NZ)
    left = jnp.where(hit, rates[...], 0.0).astype(BF)
    dims = (((1,), (1,)), ((), ()))
    source = lax.dot_general(left, ends[...], dims, preferred_element_type=F32)
    res_ref[0, plane] = flux - source


def add_face(plane, st_ref, res_ref, cond):
    face = face_term(cond[plane], cond[plane + 1], st_ref[0, 0, plane], st_ref[0, 0, plane + 1])
    res_ref[0, plane] = res_ref[0, plane] + face
    res_ref[0, plane + 1] = res_ref[0, plane + 1] - face


def edge_copy(me, count, side, edge_send, edge_recv, es_sem, er_sem):
    return pltpu.make_async_remote_copy(
        src_ref=edge_send.at[side],
        dst_ref=edge_recv.at[1 - side],
        send_sem=es_sem.at[side],
        recv_sem=er_sem.at[1 - side],
        device_id={"space": lax.rem(me + (1 if side else count - 1), count)},
        device_id_type=pl.DeviceIdType.MESH,
    )


def wells_of(cells_ref, rates_ref, cells, rates, ends):
    rate = rates_ref[...]
    high = rate.astype(BF).astype(F32)
    middle = (rate - high).astype(BF).astype(F32)
    for n, part in enumerate((high, middle, rate - high - middle)):
        lanes = slice(n * WELLS, (n + 1) * WELLS)
        cells[:, lanes] = cells_ref[...]
        rates[:, lanes] = part
    column = lax.broadcasted_iota(jnp.int32, ends.shape, 0)
    ends[...] = jnp.where((cells[...] & (NZ - 1)) == column, 1.0, 0.0).astype(BF)


def mix_modes(planes, count, jj, recv, wbuf, xf_ref, flat, spec, rows, mixed, turned):
    own = MY // count
    tiles = C * MZ // LANES
    slots = 2 * own * tiles
    pitch = slots + SKEW
    every = count * planes
    lane = lax.broadcasted_iota(jnp.int32, (1, LANES), 1)
    low = lane < 64
    even = lane % 64 < 32

    def unpack(plane, carry):
        for src in range(count):
            start = (plane * count + src) * pitch + jj * 2 * tiles
            flat[pl.ds(start, 2 * tiles), :] = recv[plane, src, mode_half(jj, count)].astype(F32)
        return carry

    lax.fori_loop(0, planes, unpack, 0)

    def column(p, t):
        return flat[pl.ds((jj * 2 + p) * tiles + t, every, stride=pitch), :].astype(BF)

    for pair in range(tiles // 2):
        right = jnp.concatenate(
            [
                jnp.concatenate([column(p, pair * 2 + half) for half in range(2)], 1)
                for p in range(2)
            ],
            0,
        )
        total = dot32(xf_ref[...], right)
        for half in range(2):
            part = total[:, half * LANES : (half + 1) * LANES].T
            for r in range(4):
                first = (pair * 2 + half) * 4 + r
                spec[pl.ds(first * (MZ + SKEW), MZ), : 2 * MX] = part[r * MZ : (r + 1) * MZ, :]
    groups = MZ // MODE_STEP
    for group in range(groups):
        base = group * MODE_STEP
        picked = [
            spec[pl.ds(base + r, C, stride=MZ + SKEW), : 2 * MX] for r in range(MODE_STEP)
        ]
        rows[group, : 2 * MX, :] = jnp.concatenate(picked, 0).T
    wide = MODE_STEP * C
    own_mode = lax.broadcasted_iota(jnp.int32, (MODE_STEP, wide), 0) == (
        lax.broadcasted_iota(jnp.int32, (MODE_STEP, wide), 1) // C
    )
    per = wide // (2 * C)

    def step(group, carry):
        first = pl.multiple_of(group * MODE_STEP, MODE_STEP)
        wfirst = pl.multiple_of(jj * MZ + group * MODE_STEP, MODE_STEP)
        for piece in range(MX // per):
            left = []
            for i in range(per):
                for q in range(2):
                    row = rows[group, pl.ds(q * MX + piece * per + i, MODE_STEP, stride=0), :]
                    left.append(jnp.where(own_mode, row, 0.0))
            lo = piece * wide
            weights = wbuf[pl.ds(wfirst, MODE_STEP), :, lo : lo + wide].reshape(wide, wide)
            both = dot32(jnp.concatenate(left, 0).astype(BF), weights)

            def part(i, q, t):
                at = (i * 2 + q) * MODE_STEP
                return both[at : at + MODE_STEP, t * LANES : (t + 1) * LANES]

            for t in range(2):
                real, imag = (
                    jnp.where(low, part(2 * t, q, t), part(2 * t + 1, q, t)) for q in range(2)
                )
                turn = jnp.where(even, -pltpu.roll(imag, LANES - C, 1), pltpu.roll(imag, C, 1))
                mixed[pl.ds(first, MODE_STEP), lo + t * LANES : lo + (t + 1) * LANES] = real + turn
        return carry

    lax.fori_loop(0, groups, step, 0)
    for block in range(MX * 2 * C // LANES):
        part = mixed[:, block * LANES : (block + 1) * LANES].T
        for r in range(4):
            first = (block * 4 + r) * (C + SKEW)
            turned[pl.ds(first, C), :MZ] = part[r * C : (r + 1) * C, :]


def mixed_tile(pair, turned):
    lane = lax.broadcasted_iota(jnp.int32, (1, LANES), 1)
    low = lane < 64
    even = lane % 64 < 32
    right = []
    for half in range(2):
        o = (pair * 2 + half) * 4
        a = [turned[pl.ds(o + r, 2 * MX, stride=C + SKEW), :] for r in range(4)]
        b = jnp.where(low, a[0], pltpu.roll(a[2], 64, 1))
        c = jnp.where(low, a[1], pltpu.roll(a[3], 64, 1))
        right.append(jnp.where(even, b, pltpu.roll(c, 32, 1)))
    return jnp.concatenate(right, 1).astype(BF)


def to_planes(table, tile, jj, pair, count, flat):
    own = MY // count
    tiles = C * MZ // LANES
    pitch = 2 * own * tiles + SKEW
    back = dot32(table, tile)
    every = back.shape[0] // 2
    for p in range(2):
        for half in range(2):
            slot = (jj * 2 + p) * tiles + pair * 2 + half
            flat[pl.ds(slot, every, stride=pitch), :] = back[
                p * every : (p + 1) * every, half * LANES : (half + 1) * LANES
            ]


def pack_planes(planes, count, first, targets, some, flat, send):
    slots = 2 * MY // count * C * MZ // LANES

    def pack(plane, carry):
        for dst in range(targets):
            start = (plane * targets + dst) * (slots + SKEW)
            for jj in some:
                part = mode_half(jj, count)
                rows = flat[pl.ds(start + part.start, part.size), :]
                send[plane, first + dst, part] = rows.astype(BF)
        return carry

    lax.fori_loop(0, planes, pack, 0)


def send_half(me, count, plane, other, send, recv, send_sem, recv_sem):
    near = count // 2
    owner = lax.rem(me + other * near, count)
    for shift in range(1, near):
        place = lax.rem(me + shift, near)
        pltpu.make_async_remote_copy(
            src_ref=send.at[plane, other * near + place],
            dst_ref=recv.at[plane, owner],
            send_sem=send_sem.at[plane, 0],
            recv_sem=recv_sem.at[plane, 0],
            device_id={"space": me // near * near + place},
            device_id_type=pl.DeviceIdType.MESH,
        ).start()
    recv[plane, owner] = send[plane, other * near + lax.rem(me, near)]


def swap_tile(me, count, n, own, other, send_sem, recv_sem):
    return pltpu.make_async_remote_copy(
        src_ref=own.at[n],
        dst_ref=other.at[n],
        send_sem=send_sem.at[n],
        recv_sem=recv_sem.at[n],
        device_id={"space": lax.rem(me + count // 2, count)},
        device_id_type=pl.DeviceIdType.MESH,
    )


def whole_kernel(
    planes, count, feat_ref, perm_ref, lift_in, lift_out, point, dec_in, dec_out, zf_ref, zi_ref,
    yf_ref, yi_ref, xf_ref, xi_ref, xh_ref, cells_ref, rates_ref, w_hbm, st_ref, res_ref,
    hid, wbuf, send_f, recv_f, send_b, recv_b, flat, spec, rows, mixed, turned, zs, sp, xs, plain,
    in_ref, lo_ref, kp_ref, di_ref, do_ref, cond, cells, rates, ends, edge_send, edge_recv,
    own_mixed, other_mixed,
    w_sem, sf_sem, rf_sem, sb_sem, rb_sem, es_sem, er_sem, om_sem, rm_sem,
):
    me = lax.axis_index("space")
    barrier = pltpu.get_barrier_semaphore()
    for shift in range(1, count):
        pl.semaphore_signal(
            barrier,
            inc=1,
            device_id={"space": lax.rem(me + shift, count)},
            device_id_type=pl.DeviceIdType.MESH,
        )
    fetch = pltpu.make_async_copy(w_hbm.at[0], wbuf, w_sem.at[0])
    fetch.start()
    xs[...] = jnp.zeros_like(xs)
    in_ref[...] = diag_of(lift_in[...], ROWS, 8, 0.5)
    lo_ref[...] = diag_of(lift_out[...], 2, lift_out.shape[1], 1.0, True)
    for layer in range(LAYERS):
        kp_ref[layer] = diag_of(point[layer], ROWS, C, 0.5)
    di_ref[...] = diag_of(dec_in[...], ROWS, C, 0.5)
    dec = dec_out.shape[1]
    do_ref[...] = spread(
        dec_out[...],
        2 * ROWS,
        ROWS * dec,
        lambda i: i // ROWS,
        lambda j: j % dec,
        lambda i, j: i % ROWS == j // dec,
        1.0,
        True,
    )
    wells_of(cells_ref, rates_ref, cells, rates, ends)
    pl.semaphore_wait(barrier, count - 1)

    def over(body):
        def run(plane, carry):
            body(plane)
            return carry

        lax.fori_loop(0, planes, run, 0)

    own = MY // count

    def send_forward(plane, soon):
        send_modes(me, count, plane, 0, send_f, recv_f, sf_sem, rf_sem)

        @pl.when(plane < soon)
        def _():
            send_rest(plane)

    def send_rest(plane):
        for jj in range(1, own):
            send_modes(me, count, plane, jj, send_f, recv_f, sf_sem, rf_sem)

    def send_late(soon):
        lax.fori_loop(soon, planes, lambda plane, carry: (send_rest(plane), carry)[1], 0)

    def lift(plane):
        lift_plane(plane, feat_ref, perm_ref, in_ref, lo_ref, hid, plain, xs, zs)
        to_modes(plane, count, zf_ref, yf_ref, zs, flat, send_f)
        send_forward(plane, SOON[0])

    over(lift)
    send_late(SOON[0])
    for layer in range(LAYERS):
        fetch.wait()
        last = layer + 1 == LAYERS
        tile_pairs = C * MZ // LANES // 2

        def turn(index):
            return lax.rem(planes - index, planes) if last else index

        def send_back(jj):
            def one(n, carry):
                if jj > 0:

                    @pl.when(n >= EARLY)
                    def _():
                        for before in range(jj):
                            send_modes(me, count, turn(n), before, send_b, recv_b, sb_sem, rb_sem)

                if jj + 1 == own:
                    send_modes(me, count, turn(n), jj, send_b, recv_b, sb_sem, rb_sem)
                return carry

            if jj + 1 < own:
                for n in range(EARLY):
                    send_modes(me, count, (planes - n) % planes, jj, send_b, recv_b, sb_sem, rb_sem)
            else:
                lax.fori_loop(0, planes, one, 0)

        swaps = [
            swap_tile(me, count, n, own_mixed, other_mixed, om_sem, rm_sem)
            for n in range(0 if last else own * tile_pairs)
        ]
        for jj in range(own):
            over(lambda plane: wait_modes(count, plane, jj, recv_f, rf_sem))
            mix_modes(planes, count, jj, recv_f, wbuf, xf_ref, flat, spec, rows, mixed, turned)
            for pair in range(tile_pairs):
                tile = mixed_tile(pair, turned)
                if last:
                    to_planes(xi_ref[...], tile, jj, pair, count, flat)
                else:
                    n = jj * tile_pairs + pair
                    own_mixed[n] = tile
                    swaps[n].start()
            if last:
                pack_planes(planes, count, 0, count, (jj,), flat, send_b)
                send_back(jj)
        for jj in range(own):
            over(lambda plane: wait_modes(count, plane, jj, send_f, sf_sem))
        if not last:
            fetch = pltpu.make_async_copy(w_hbm.at[layer + 1], wbuf, w_sem.at[layer + 1])
            fetch.start()

        if not last:
            near = count // 2
            parts = 2 * (near - 1)
            table = xh_ref.at[me // near]
            for other in range(2):
                for n, swap in enumerate(swaps):
                    if other:
                        swap.wait_recv()
                    tile = other_mixed[n] if other else own_mixed[n]
                    to_planes(table[...], tile, n // tile_pairs, n % tile_pairs, count, flat)
                pack_planes(planes, count, other * near, near, range(own), flat, send_b)
                over(lambda n: send_half(me, count, n, other, send_b, recv_b, sb_sem, rb_sem))
            for swap in swaps:
                swap.wait_send()
        kp = kp_ref.at[layer]

        def settle(plane, buffer, sem):
            if not last:
                wait_plane(parts, plane, buffer, sem)
            for jj in range(own if last else 0):
                wait_modes(count, plane, jj, buffer, sem)


        def rest(index):
            plane = turn(index)
            settle(plane, recv_b, rb_sem)
            from_modes(plane, count, recv_b, yi_ref, zi_ref, flat, sp)
            if not last:
                middle_plane(plane, kp, hid, sp, zs)
                to_modes(plane, count, zf_ref, yf_ref, zs, flat, send_f)
                send_forward(plane, SOON[1])
            else:
                final_plane(plane, kp, di_ref, do_ref, perm_ref, hid, sp, st_ref)
                residual_plane(
                    plane, me, planes, perm_ref, cells, rates, ends, st_ref, res_ref, cond
                )

                @pl.when(index == 1)
                def _():
                    for side in range(2):
                        edge_send[side, 0] = st_ref[0, 0, side * (planes - 1)].astype(BF)
                        edge_send[side, 1] = cond[side * (planes - 1)].astype(BF)
                        edge_copy(me, count, side, edge_send, edge_recv, es_sem, er_sem).start()

                @pl.when(index >= 2)
                def _():
                    add_face(plane, st_ref, res_ref, cond)

        over(rest)
        if not last:
            send_late(SOON[1])
        over(lambda plane: settle(plane, send_b, sb_sem))
    add_face(0, st_ref, res_ref, cond)
    for side in range(2):
        edge_copy(me, count, side, edge_send, edge_recv, es_sem, er_sem).wait()
    for side in range(2):
        plane = side * (planes - 1)
        press, conduct = (edge_recv[side, n].astype(F32) for n in range(2))
        face = face_term(cond[plane], conduct, st_ref[0, 0, plane], press)
        inside = me < count - 1 if side else me > 0
        res_ref[0, plane] = res_ref[0, plane] + jnp.where(inside, face, 0.0)


def ones_where(shape, test, value=1.0):
    row = lax.broadcasted_iota(jnp.int32, shape, 0)
    col = lax.broadcasted_iota(jnp.int32, shape, 1)
    return jnp.where(test(row, col), value, 0.0)


def spread(matrix, rows, cols, row_of, col_of, keep, value, turned):
    depth, height = matrix.shape[::-1] if turned else matrix.shape
    take = ones_where((rows, height), lambda i, j: row_of(i) == j).astype(BF)
    put = ones_where((depth, cols), lambda i, j: col_of(j) == i).astype(BF)
    dims = (((1,), (0 if turned else 1,)), ((), ()))
    part = lax.dot_general(take, matrix, dims, preferred_element_type=F32)
    return (dot32(part.astype(BF), put) * ones_where((rows, cols), keep, value)).astype(BF)


def diag_of(matrix, copies, width, value, turned=False):
    height = matrix.shape[0 if turned else 1]
    return spread(
        matrix,
        copies * height,
        copies * width,
        lambda i: i % height,
        lambda j: j % width,
        lambda i, j: i // height == j // width,
        value,
        turned,
    )


def local_fast(
    features,
    log_perm,
    well_cells,
    well_rates,
    lift_in,
    lift_out,
    spec_weight,
    point_weight,
    dec_in,
    dec_out,
):
    planes = features.shape[2]
    count = lax.axis_size("space")
    own = MY // count
    modes = own * MZ
    slots = 2 * modes * C // LANES
    tables = tables_for(count)
    lift, dec = lift_in.shape[1], dec_in.shape[1]
    operands = (
        features,
        log_perm,
        lift_in,
        lift_out.T,
        point_weight,
        dec_in,
        dec_out.T,
    ) + tuple(tables[name] for name in ("zf", "zi", "yf", "yi", "xf", "xi", "xh"))
    operands = operands + (well_cells, well_rates)
    vmem = pl.BlockSpec(memory_space=pltpu.VMEM)
    exchange = pltpu.VMEM((planes, count, slots, LANES), BF)
    results = pl.pallas_call(
        lambda *refs: whole_kernel(planes, count, *refs),
        in_specs=[vmem] * len(operands) + [pl.BlockSpec(memory_space=pl.ANY)],
        out_specs=[vmem, vmem],
        out_shape=[
            jax.ShapeDtypeStruct((1, 2, planes, NY, NZ), F32),
            jax.ShapeDtypeStruct((1, planes, NY, NZ), F32),
        ],
        scratch_shapes=[
            pltpu.VMEM((planes, PAIRS * C, 2 * NZ), BF),
            pltpu.VMEM(spec_weight.shape[1:], BF),
            exchange,
            exchange,
            exchange,
            exchange,
            pltpu.VMEM((planes * count * (slots + SKEW), LANES), F32),
            pltpu.VMEM((C * (MZ + SKEW), LANES), F32),
            pltpu.VMEM((MZ // MODE_STEP, 2 * MX + MODE_STEP, MODE_STEP * C), F32),
            pltpu.VMEM((MZ, MX * 2 * C), F32),
            pltpu.VMEM((2 * MX * (C + SKEW), LANES), F32),
            pltpu.VMEM((2, C * PITCH, LANES), F32),
            pltpu.VMEM((2, PAIRS * (C + SKEW), LANES), F32),
            pltpu.VMEM((2, PAIRS * 8, NZ), F32),
            pltpu.VMEM((NY, NZ), F32),
            pltpu.VMEM((ROWS * lift, ROWS * 8), BF),
            pltpu.VMEM((2 * C, 2 * lift), BF),
            pltpu.VMEM((LAYERS, ROWS * C, ROWS * C), BF),
            pltpu.VMEM((ROWS * dec, ROWS * C), BF),
            pltpu.VMEM((2 * ROWS, ROWS * dec), BF),
            pltpu.VMEM((planes, NY, NZ), F32),
            pltpu.VMEM((1, 3 * WELLS), jnp.int32),
            pltpu.VMEM((1, 3 * WELLS), F32),
            pltpu.VMEM((NZ, 3 * WELLS), BF),
            pltpu.VMEM((2, 2, NY, NZ), BF),
            pltpu.VMEM((2, 2, NY, NZ), BF),
            pltpu.VMEM((modes * C // 256, 2 * MX, 256), BF),
            pltpu.VMEM((modes * C // 256, 2 * MX, 256), BF),
            pltpu.SemaphoreType.DMA((LAYERS,)),
        ]
        + [pltpu.SemaphoreType.DMA((planes, own))] * 4
        + [pltpu.SemaphoreType.DMA((2,))] * 2
        + [pltpu.SemaphoreType.DMA((modes * C // 256,))] * 2,
        compiler_params=pltpu.CompilerParams(
            collective_id=0, has_side_effects=True, vmem_limit_bytes=60 * 1024 * 1024
        ),
        name="whole",
    )(*operands, spec_weight)
    return handed_on(results)


def handed_on(results):
    pieces = [
        (n, at) for n, each in enumerate(results) for at in np.ndindex(*each.shape[:-2])
    ]

    def body(*refs):
        source, target, held = refs[:2], refs[2:4], refs[4:6]
        in_sem, out_sem = refs[6:]
        loads = [
            pltpu.make_async_copy(source[n].at[at], held[n].at[at], in_sem.at[k])
            for k, (n, at) in enumerate(pieces)
        ]
        stores = [
            pltpu.make_async_copy(held[n].at[at], target[n].at[at], out_sem.at[k])
            for k, (n, at) in enumerate(pieces)
        ]
        for load in loads:
            load.start()
        for load, store in zip(loads, stores):
            load.wait()
            store.start()
        for store in stores:
            store.wait()

    whole = pl.BlockSpec(memory_space=pl.ANY)
    return pl.pallas_call(
        body,
        in_specs=[whole] * 2,
        out_specs=[whole] * 2,
        out_shape=[jax.ShapeDtypeStruct(each.shape, each.dtype) for each in results],
        scratch_shapes=[pltpu.VMEM(each.shape, each.dtype) for each in results]
        + [pltpu.SemaphoreType.DMA((len(pieces),))] * 2,
        compiler_params=pltpu.CompilerParams(vmem_limit_bytes=60 * 1024 * 1024),
        name="handed_on",
    )(*results)


def local(features, log_perm, well_cells, well_rates, lift_in, lift_out, spec_weight, *rest):
    batches, planes = features.shape[0], features.shape[2]
    count = lax.axis_size("space")
    fits = batches == 1 and planes == 8 and count % 8 == 0 and MY == 2 * count
    run = local_fast if fits else local_general
    return run(
        features, log_perm, well_cells, well_rates, lift_in, lift_out, spec_weight, *rest
    )


def solution(mesh):
    return jax.shard_map(
        local,
        mesh=mesh,
        in_specs=(
            P("sample", None, "space", None, None),
            P("sample", "space", None, None),
            P("sample", None),
            P("sample", None),
            P(),
            P(),
            P(None, "space", None, None),
            P(),
            P(),
            P(),
        ),
        out_specs=(P("sample", None, "space", None, None), P("sample", "space", None, None)),
        check_vma=False,
    )
```
